128 devices in a mesh: req: 8 (over x, core), mlp: 16 (over z, y).
Axes of the slice: x: 4, y: 4, z: 4, core: 2. Of those that a mesh axis runs over, the one named last changes fastest.
Arguments:
- tokens: bfloat16 [8192, 4096], P(('req', 'mlp')), may hold values from -6 to 6
- layer_norm_gain: float32 [4096], replicated, may hold values from 0.1 to 1.9
- layer_norm_bias: float32 [4096], replicated, may hold values from -2 to 2
- query_key_weight: bfloat16 [4096, 16, 768], P(None, 'mlp')
- output_weight: bfloat16 [16, 256, 4096], P('mlp'), may hold values from -0.09375 to 0.09375
- up_weight: bfloat16 [4096, 8192], P(None, 'mlp'), may hold values from -0.09375 to 0.09375
- input_bias: float32 [8192], P('mlp'), may hold values from -3 to 3
- down_weight: bfloat16 [8192, 4096], P('mlp'), may hold values from -0.0625 to 0.0625
- output_bias: float32 [4096], replicated, may hold values from -2 to 2
- input_adapter_left: bfloat16 [4096, 2048], P(None, 'mlp'), may hold values from -0.09375 to 0.09375
- query_key_value_right: bfloat16 [1024, 16, 768], P(None, 'mlp'), may hold values from -1.5 to 1.5
- up_adapter_right: bfloat16 [1024, 8192], P(None, 'mlp'), may hold values from -1.5 to 1.5
- output_adapter_left: bfloat16 [16, 256, 1024], P('mlp'), may hold values from -0.09375 to 0.09375
- down_adapter_left: bfloat16 [8192, 1024], P('mlp'), may hold values from -0.0625 to 0.0625
- output_adapter_right: bfloat16 [2048, 4096], P('mlp'), may hold values from -1 to 1
- lengths: int32 [257], replicated, may hold values from 8 to 4096, as said below
- request_adapter: int32 [257], replicated, may hold values from 0 to 63
- slot_adapter: int32 [64], P('mlp'), may hold values from 0 to 63, each once
Outputs:
- mixed: bfloat16 [8192, 4096], P(('req', 'mlp'))
The draws below stay inside these ranges and needn't reach their ends.
Inputs may be any that keep to these rules, and one draw needn't show every extreme that they name: `lengths`: one request holds exactly 4096 tokens, every other one 8 to 24; together they hold 8192 tokens. `slot_adapter`: every adapter id stands in exactly one slot.
All inputs are finite; a program needn't handle non-finite values.
Results may differ from the reference program's by a relative error of at most 0.017.
Values may be sent and summed in bfloat16 or wider, within the bound.
A program may use at most 128 MiB of HBM per device.

```python
import math
import jax
import jax.numpy as jnp
import numpy as np
from jax import lax

MODEL_DIM = 4096
ATTENTION_HEADS = 16
HEAD_SIZE = 256
ROT = 64
FEEDFORWARD = 8192
ADAPTER_RANK = 16
TOK_DEV = 64
TOKENS = 8192
LONG = 4096
SHORTS = 256
REQS = 257
ADAPTER_COUNT = 64


def draw_query_key_weight(key, part):
    weights = jax.random.normal(key, (MODEL_DIM, ATTENTION_HEADS, 3 * HEAD_SIZE), jnp.float32) * MODEL_DIM ** (-0.5)
    return weights.astype(jnp.bfloat16)


def draw_lengths(key, part):
    key_first = jax.random.fold_in(key, 11)
    key_second = jax.random.fold_in(key, 12)
    key_third = jax.random.fold_in(key, 13)
    offset = jax.random.randint(key_first, (SHORTS // 2,), -8, 9)
    offset = offset.at[0].set(8)
    shorts = jnp.concatenate([16 + offset, 16 - offset]).astype(jnp.int32)
    shuffle = jax.random.permutation(key_second, SHORTS)
    shorts = shorts[shuffle]
    long_slot = jax.random.randint(key_third, (), 0, REQS)
    slot_index = jnp.arange(REQS, dtype=jnp.int32)
    before = shorts[jnp.clip(slot_index, 0, SHORTS - 1)]
    after_value = shorts[jnp.clip(slot_index - 1, 0, SHORTS - 1)]
    return jnp.where(slot_index < long_slot, before, jnp.where(slot_index == long_slot, LONG, after_value)).astype(jnp.int32)


def touch_ends(entries, own_key, low, top_value):
    longest = entries.shape.index(max(entries.shape))
    spots = []
    for shift in (0, 1):
        where = [jax.random.randint(jax.random.fold_in(own_key, axis), (), 0, length) for axis, length in enumerate(entries.shape)]
        where[longest] = (where[longest] + shift) % entries.shape[longest]
        spots.append(tuple(where))
    return entries.at[spots[0]].set(low).at[spots[1]].set(top_value)


def block_levels(stream_key, extent, cuts, low, top_value):
    def one(dim, blocks):
        draws = jax.random.uniform(jax.random.fold_in(jax.random.fold_in(stream_key, 6), dim), (blocks,), jnp.float32, low / len(cuts), top_value / len(cuts))
        return jnp.repeat(jnp.exp(draws), extent[dim] // blocks).reshape((-1,) + (1,) * (len(extent) - dim - 1))

    factor_of = one(*cuts[0])
    for cut in cuts[1:]:
        factor_of = factor_of * one(*cut)
    return factor_of


def rank_bounds(count, lean):
    weights = [(1 << 20) // math.isqrt(rank ** lean) + 1 for rank in range(1, count + 1)]
    scale = 1 + sum(weights) // (1 << 30)
    return np.cumsum(np.array([max(1, weight // scale) for weight in weights]))


def skewed_ids(key, dims, amount, slope):
    table = rank_bounds(amount, slope)
    lot = jax.random.randint(jax.random.fold_in(key, 1), dims, 0, int(table[amount - 1]))
    standing = jnp.searchsorted(jnp.asarray(table, jnp.int32), lot, side="right")
    return jax.random.permutation(jax.random.fold_in(key, 2), amount)[standing].astype(jnp.int32)


def scatter_about(rng, shape, width, reach, split=(), held_as=jnp.bfloat16):
    loudness = block_levels(rng, shape, split, -0.22, 0.18) if split else 1.0
    values = jax.random.normal(rng, shape, jnp.float32) * width * loudness
    return jnp.minimum(jnp.maximum(values, -reach), reach).astype(held_as)


def setup_inputs(seed: int = 0) -> dict:
    seeds = jax.random.split(jax.random.key(seed), 19)
    return {
        "tokens": scatter_about(seeds[0], (TOKENS, MODEL_DIM), 1.0, 6.0, ((0, 128),)),
        "layer_norm_gain": jnp.clip(1.0 + 0.18 * jax.random.normal(seeds[1], (MODEL_DIM,), jnp.float32), 0.1, 1.9),
        "layer_norm_bias": scatter_about(seeds[2], (MODEL_DIM,), 0.3, 2.0, (), jnp.float32),
        "query_key_weight": draw_query_key_weight(jax.random.fold_in(seeds[18], 71), 0),
        "output_weight": scatter_about(seeds[4], (ATTENTION_HEADS, HEAD_SIZE, MODEL_DIM), MODEL_DIM ** -0.5, 0.09375, ((0, 16),)),
        "up_weight": scatter_about(seeds[5], (MODEL_DIM, FEEDFORWARD), MODEL_DIM ** -0.5, 0.09375, ((1, 16),)),
        "input_bias": scatter_about(seeds[6], (FEEDFORWARD,), 0.5, 3.0, ((0, 16),), jnp.float32),
        "down_weight": scatter_about(seeds[7], (FEEDFORWARD, MODEL_DIM), FEEDFORWARD ** -0.5, 0.0625, ((0, 16),)),
        "output_bias": scatter_about(seeds[8], (MODEL_DIM,), 0.3, 2.0, (), jnp.float32),
        "input_adapter_left": scatter_about(seeds[9], (MODEL_DIM, ADAPTER_COUNT * 2 * ADAPTER_RANK), MODEL_DIM ** -0.5, 0.09375, ((1, 16),)),
        "query_key_value_right": scatter_about(seeds[10], (ADAPTER_COUNT * ADAPTER_RANK, ATTENTION_HEADS, 3 * HEAD_SIZE), ADAPTER_RANK ** -0.5, 1.5, ((1, 16),)),
        "up_adapter_right": scatter_about(seeds[11], (ADAPTER_COUNT * ADAPTER_RANK, FEEDFORWARD), ADAPTER_RANK ** -0.5, 1.5, ((1, 16),)),
        "output_adapter_left": scatter_about(seeds[12], (ATTENTION_HEADS, HEAD_SIZE, ADAPTER_COUNT * ADAPTER_RANK), MODEL_DIM ** -0.5, 0.09375, ((0, 16),)),
        "down_adapter_left": scatter_about(seeds[13], (FEEDFORWARD, ADAPTER_COUNT * ADAPTER_RANK), FEEDFORWARD ** -0.5, 0.0625, ((0, 16),)),
        "output_adapter_right": scatter_about(seeds[14], (ADAPTER_COUNT * 2 * ADAPTER_RANK, MODEL_DIM), (2 * ADAPTER_RANK) ** -0.5, 1.0, ((0, 16),)),
        "lengths": draw_lengths(jax.random.fold_in(seeds[18], 71), 0),
        "request_adapter": touch_ends(skewed_ids(seeds[16], (REQS,), ADAPTER_COUNT, 2), jax.random.fold_in(seeds[16], 3), 0, ADAPTER_COUNT - 1).astype(jnp.int32),
        "slot_adapter": jax.random.permutation(seeds[17], ADAPTER_COUNT).astype(jnp.int32),
    }


EPSILON = 1e-05
NEGATIVE_FILL = -1e+30

def rank_product(left_side, right_side):
    return jnp.dot(left_side, right_side, preferred_element_type=jnp.float32)

def normalize(inputs, layer_norm_gain, layer_norm_bias):
    values = inputs.astype(jnp.float32)
    center = values - lax.optimization_barrier(jnp.mean(values, axis=1, keepdims=True))
    spread = lax.optimization_barrier(jnp.mean(center * center, axis=1, keepdims=True))
    scaled = center * lax.rsqrt(spread + EPSILON)
    return (scaled * layer_norm_gain + layer_norm_bias).astype(jnp.bfloat16)

def token_info(lengths, request_adapter, first_row, row_count):
    endings = jnp.cumsum(lengths).astype(jnp.int32)
    anchors = (endings - lengths).astype(jnp.int32)
    token_index = (first_row + lax.iota(jnp.int32, row_count)).astype(jnp.int32)
    inside = anchors[None, :] <= token_index[:, None]
    request = (lax.optimization_barrier(jnp.sum(inside.astype(jnp.int32), axis=1)) - 1).astype(jnp.int32)
    request_start = lax.optimization_barrier(jnp.max(jnp.where(inside, anchors[None, :], jnp.zeros((), jnp.int32)), axis=1)).astype(jnp.int32)
    adapter_id = jnp.take(request_adapter, jnp.maximum(request, 0)).astype(jnp.int32)
    return (token_index, request, (token_index - request_start).astype(jnp.int32), adapter_id)

def rotate(matrix, position):
    row_count = matrix.shape[0]
    head_count = matrix.shape[1]
    half_rot = ROT // 2
    frequency = jnp.exp(jnp.arange(half_rot, dtype=jnp.float32) * (-2.0 * math.log(10000.0) / ROT))
    angles = position.astype(jnp.float32)[:, None] * frequency[None, :]
    cosine = jnp.cos(angles)[:, None, :]
    sine_value = jnp.sin(angles)[:, None, :]
    paired_part = matrix[:, :, :ROT].reshape(row_count, head_count, half_rot, 2)
    even_part = paired_part[:, :, :, 0]
    odd_part = paired_part[:, :, :, 1]
    turned = jnp.stack([even_part * cosine - odd_part * sine_value, odd_part * cosine + even_part * sine_value], axis=-1)
    return jnp.concatenate([turned.reshape(row_count, head_count, ROT), matrix[:, :, ROT:]], axis=2)

def slot_selector(products, chosen, adapter_id, column_count):
    row_count = products.shape[0]
    selector = (adapter_id[:, None] == chosen[None, :]).astype(jnp.float32)
    reshaped = products.reshape(row_count, chosen.shape[0], column_count)
    return lax.optimization_barrier(jnp.sum(selector[:, :, None] * reshaped, axis=1))

def widen_rows(values, chosen, adapter_id):
    selector = adapter_id[:, None] == chosen[None, :]
    spread = jnp.where(selector[:, :, None], values[:, None, :], jnp.zeros((), values.dtype))
    return spread.reshape(values.shape[0], chosen.shape[0] * values.shape[1])

def reference(tokens, layer_norm_gain, layer_norm_bias, query_key_weight, output_weight, up_weight, input_bias, down_weight, output_bias, input_adapter_left, query_key_value_right, up_adapter_right, output_adapter_left, down_adapter_left, output_adapter_right, lengths, request_adapter, slot_adapter):
    normed_rows = normalize(tokens, layer_norm_gain, layer_norm_bias)
    token_index, request, position, adapter_id = token_info(lengths, request_adapter, 0, TOKENS)
    every_id = jnp.arange(ADAPTER_COUNT, dtype=jnp.int32)
    rank_input = slot_selector(rank_product(normed_rows, input_adapter_left), slot_adapter, adapter_id, 2 * ADAPTER_RANK).astype(jnp.bfloat16)
    query_key_columns = ATTENTION_HEADS * 3 * HEAD_SIZE
    projected_rows = rank_product(normed_rows, query_key_weight.reshape(MODEL_DIM, query_key_columns)) + rank_product(widen_rows(rank_input[:, :ADAPTER_RANK], every_id, adapter_id), query_key_value_right.reshape(ADAPTER_COUNT * ADAPTER_RANK, query_key_columns))
    projected_rows = projected_rows.reshape(TOKENS, ATTENTION_HEADS, 3 * HEAD_SIZE)
    hidden_units = jax.nn.gelu(rank_product(normed_rows, up_weight) + rank_product(widen_rows(rank_input[:, ADAPTER_RANK:], every_id, adapter_id), up_adapter_right) + input_bias, approximate=True).astype(jnp.bfloat16)
    queries = rotate(projected_rows[:, :, :HEAD_SIZE], position).astype(jnp.bfloat16)
    key_rows = rotate(projected_rows[:, :, HEAD_SIZE:2 * HEAD_SIZE], position).astype(jnp.bfloat16)
    value_rows = projected_rows[:, :, 2 * HEAD_SIZE:].astype(jnp.bfloat16)
    keys_wide = key_rows.astype(jnp.float32)
    values_wide = value_rows.astype(jnp.float32)
    window = min(TOKENS, LONG + TOK_DEV)
    score_scale = HEAD_SIZE ** (-0.5)

    def one_block(number):
        first_row = (number * TOK_DEV).astype(jnp.int32)
        window_start = jnp.clip(first_row + TOK_DEV - window, 0, TOKENS - window).astype(jnp.int32)
        block_queries = lax.dynamic_slice_in_dim(queries, first_row, TOK_DEV, 0).astype(jnp.float32)
        block_request = lax.dynamic_slice_in_dim(request, first_row, TOK_DEV, 0)
        block_index = lax.dynamic_slice_in_dim(token_index, first_row, TOK_DEV, 0)
        near_keys = lax.dynamic_slice_in_dim(keys_wide, window_start, window, 0)
        near_values = lax.dynamic_slice_in_dim(values_wide, window_start, window, 0)
        near_request = lax.dynamic_slice_in_dim(request, window_start, window, 0)
        near_index = lax.dynamic_slice_in_dim(token_index, window_start, window, 0)
        scores = jnp.einsum('qhd,khd->qhk', block_queries, near_keys, precision=lax.Precision.HIGHEST) * score_scale
        allowed = jnp.logical_and(near_request[None, :] == block_request[:, None], near_index[None, :] <= block_index[:, None])[:, None, :]
        masked = jnp.where(allowed, scores, NEGATIVE_FILL)
        highest = lax.optimization_barrier(jnp.max(masked, axis=2, keepdims=True))
        weights = jnp.where(allowed, jnp.exp(masked - highest), 0.0)
        totals = lax.optimization_barrier(jnp.sum(weights, axis=2))
        summed = jnp.einsum('qhk,khd->qhd', weights.astype(jnp.bfloat16).astype(jnp.float32), near_values, precision=lax.Precision.HIGHEST)
        return (summed / totals[:, :, None]).astype(jnp.bfloat16)
    attention_output = lax.map(one_block, jnp.arange(TOKENS // TOK_DEV, dtype=jnp.int32)).reshape(TOKENS, MODEL_DIM)
    output_rank_rows = rank_product(attention_output, output_adapter_left.reshape(MODEL_DIM, ADAPTER_COUNT * ADAPTER_RANK))
    down_rank_rows = rank_product(hidden_units, down_adapter_left)
    rank_output = jnp.concatenate([slot_selector(output_rank_rows, every_id, adapter_id, ADAPTER_RANK), slot_selector(down_rank_rows, every_id, adapter_id, ADAPTER_RANK)], axis=1).astype(jnp.bfloat16)
    adapter_delta = rank_product(widen_rows(rank_output, every_id, adapter_id), output_adapter_right)
    total = rank_product(attention_output, output_weight.reshape(MODEL_DIM, MODEL_DIM)) + rank_product(hidden_units, down_weight) + adapter_delta + tokens.astype(jnp.float32) + output_bias
    return total.astype(jnp.bfloat16)
```

```python
import functools
import math

import jax
import jax.numpy as jnp
from jax import lax
from jax.experimental import pallas as pl
from jax.experimental.pallas import tpu as pltpu
from jax.sharding import PartitionSpec as P

HEAD = 256
ROT = 64
RANK = 16
EPSILON = 1e-05
NEGATIVE_FILL = -1e30
MESH = pl.DeviceIdType.MESH
F32 = jnp.float32
BF16 = jnp.bfloat16
VMEM_LIMIT = 60 * 1024 * 1024
SIDE = 4
GROUP = 16
UNIT = 16
QKV = 3 * HEAD


def dot(a, b):
    return jnp.dot(a, b, preferred_element_type=F32)


class Plane:
    def __init__(self):
        self.me = lax.axis_index("mlp")
        self.z = self.me // SIDE
        self.y = self.me % SIDE

    def at(self, dz, dy):
        return ((self.z + dz + SIDE) % SIDE) * SIDE + (self.y + dy + SIDE) % SIDE

    def off(self, half, d1, d2):
        return self.at(d1, d2) if half == 0 else self.at(d2, d1)

    def source(self, half, d1, d2):
        return self.off(half, -d1, -d2)


def barrier_all(me, count):
    sem = pltpu.get_barrier_semaphore()
    for k in range(1, count):
        pl.semaphore_signal(sem, inc=1, device_id={"mlp": (me + k) % count}, device_id_type=MESH)
    return sem


def exchange_sum(me, packed, landed, full, sems):
    def scatter(k, carry):
        to = (me + k) % GROUP
        pltpu.make_async_remote_copy(
            packed.at[to], landed.at[me], sems.at[0], sems.at[1], device_id={"mlp": to}, device_id_type=MESH
        ).start()
        return carry

    lax.fori_loop(1, GROUP, scatter, 0)
    landed[me] = packed[me]
    many = landed.at[pl.ds(0, GROUP - 1)]
    pltpu.make_async_copy(many, many, sems.at[1]).wait()
    full[me] = jnp.sum(landed[...].astype(F32), axis=0).astype(BF16)

    def gather(k, carry):
        to = (me + k) % GROUP
        pltpu.make_async_remote_copy(
            full.at[me], full.at[me], sems.at[2], sems.at[3], device_id={"mlp": to}, device_id_type=MESH
        ).start()
        return carry

    lax.fori_loop(1, GROUP, gather, 0)
    pltpu.make_async_copy(many, many, sems.at[0]).wait()
    return many


def exchange_wait(many, sems):
    pltpu.make_async_copy(many, many, sems.at[3]).wait()
    pltpu.make_async_copy(many, many, sems.at[2]).wait()


GATHER_GROUPS = (
    tuple((h, d1, 0) for h in (0, 1) for d1 in (0, 1, -1, 2)),
    tuple((h, d1, d2) for h in (0, 1) for d1 in (0, 1) for d2 in (1, -1)),
    tuple((h, d1, d2) for h in (0, 1) for d1 in (-1, 2) for d2 in (1, -1)),
    tuple((h, d1, 2) for h in (0, 1) for d1 in (0, 1, -1, 2)),
)


def input_kernel(
    tokens, gain, bias, in_bias, adapter, slots, cosine, sine, w_qkv, w_up, w_left, w_qkv_right, w_up_right,
    out_qkv, out_hidden,
    xs, weights, right_qkv, right_up, rows_in, acc, picked, packed, landed, full,
    load_sems, send_sem, recv_sems, ex_sems,
):
    plane = Plane()
    me = plane.me
    hid = w_up.shape[1]
    loads = [
        pltpu.make_async_copy(w_qkv, weights.at[:, pl.ds(0, QKV)], load_sems.at[0]),
        pltpu.make_async_copy(w_up, weights.at[:, pl.ds(QKV, hid)], load_sems.at[1]),
        pltpu.make_async_copy(w_left, weights.at[:, pl.ds(QKV + hid, 128)], load_sems.at[2]),
        pltpu.make_async_copy(w_qkv_right, right_qkv, load_sems.at[3]),
        pltpu.make_async_copy(w_up_right, right_up, load_sems.at[4]),
    ]
    for load in loads:
        load.start()
    sem = barrier_all(me, GROUP)
    for part in range(0, 64, 16):
        values = tokens[part : part + 16, :].astype(F32)
        center = values - jnp.mean(values, axis=1, keepdims=True)
        spread = jnp.mean(center * center, axis=1, keepdims=True)
        scaled = center * lax.rsqrt(spread + EPSILON)
        xs[me, part : part + 16, :] = (scaled * gain[...] + bias[...]).astype(BF16)
    pl.semaphore_wait(sem, GROUP - 1)

    def send(slot, half, units, axis, step):
        first, count = units
        rows = pl.ds(half * 32 + first * UNIT, count * UNIT)
        to = plane.off(half, step, 0) if axis == 1 else plane.off(half, 0, step)
        pltpu.make_async_remote_copy(
            xs.at[slot, rows, :], xs.at[slot, rows, :], send_sem, recv_sems.at[slot, half * 2 + first],
            device_id={"mlp": to}, device_id_type=MESH,
        ).start()

    def landed_piece(half, d1, d2, units):
        first, count = units
        slot = plane.source(half, d1, d2)
        rows = pl.ds(half * 32 + first * UNIT, count * UNIT)
        view = xs.at[slot, rows, :]
        pltpu.make_async_copy(view, view, recv_sems.at[slot, half * 2 + first]).wait()
        return slot

    whole = (0, 2)
    for half in (0, 1):
        for step in (1, -1):
            send(me, half, whole, 1, step)
    for half in (0, 1):
        for step in (1, -1):
            send(me, half, whole, 2, step)
    for half in (0, 1):
        for d1 in (1, -1):
            slot = landed_piece(half, d1, 0, whole)
            send(slot, half, (0, 1) if d1 == 1 else (1, 1), 1, d1)
            for step in (1, -1):
                send(slot, half, whole, 2, step)

    def relay(half, d1, d2, pieces):
        for units in pieces:
            slot = landed_piece(half, d1, d2, units)
        send(slot, half, (0, 1) if d2 == 1 else (1, 1), 2, d2)

    def multiply(number):
        places = []
        for i, (half, d1, d2) in enumerate(GATHER_GROUPS[number]):
            slot = plane.source(half, d1, d2)
            rows_in[i * 32 : (i + 1) * 32, :] = xs[slot, pl.ds(half * 32, 32), :]
            places.append((slot, half))

        left = dot(rows_in[...], weights[:, QKV + hid :])
        for i, (slot, half) in enumerate(places):
            for u in (0, 1):
                unit = half * 2 + u
                at = i * 32 + u * UNIT
                picked[slot, unit] = left[at : at + UNIT, :].astype(BF16)

    def multiply_wide(number):
        def column(n, carry):
            columns = pl.ds(pl.multiple_of(n * 256, 256), 256)
            result = dot(rows_in[...], weights[:, columns])
            for i, (half, d1, d2) in enumerate(GATHER_GROUPS[number]):
                slot = plane.source(half, d1, d2)
                for u in (0, 1):
                    at = i * 32 + u * UNIT
                    acc[slot, half * 2 + u, :, columns] = result[at : at + UNIT, :]
            return carry

        lax.fori_loop(0, (QKV + hid) // 256, column, 0)

    for load in loads[:3]:
        load.wait()
    for half in (0, 1):
        for d2 in (1, -1):
            relay(half, 0, d2, (whole,))
    for half in (0, 1):
        for unit in ((0, 1), (1, 1)):
            slot = landed_piece(half, 2, 0, unit)
            for step in (1, -1):
                send(slot, half, unit, 2, step)
    multiply(0)
    multiply_wide(0)
    for half in (0, 1):
        for d1 in (1, -1):
            for d2 in (1, -1):
                relay(half, d1, d2, (whole,))
    multiply(1)
    multiply_wide(1)
    for half in (0, 1):
        for d2 in (1, -1):
            relay(half, 2, d2, ((0, 1), (1, 1)))
    multiply(2)
    multiply_wide(2)
    for half in (0, 1):
        for d1 in (0, 1, -1, 2):
            for unit in ((0, 1), (1, 1)):
                landed_piece(half, d1, 2, unit)
    multiply(3)

    lane = lax.broadcasted_iota(jnp.int32, (1, 128), 1)
    chosen = jnp.where(lane < 32, slots[0], jnp.where(lane < 64, slots[1], jnp.where(lane < 96, slots[2], slots[3])))
    row_id = lax.broadcasted_iota(jnp.int32, (128, 128), 0)
    col_id = lax.broadcasted_iota(jnp.int32, (128, 128), 1)
    together = jnp.zeros((256, 128), F32)
    for unit in range(4):
        mine = adapter[:, unit].reshape(256, 1) == chosen
        kept = jnp.where(mine, picked[:, unit].reshape(256, 128).astype(F32), 0.0).astype(BF16)
        fold = jnp.logical_and(col_id // 32 == unit, row_id % 32 == col_id % 32).astype(F32).astype(BF16)
        together = together + dot(kept, fold)
    packed[...] = together.astype(BF16).reshape(GROUP, UNIT, 128)
    many = exchange_sum(me, packed, landed, full, ex_sems)
    multiply_wide(3)
    exchange_wait(many, ex_sems)
    sent = xs.at[pl.ds(0, GROUP - 1)]
    pltpu.make_async_copy(sent, sent, send_sem).wait()
    for load in loads[3:]:
        load.wait()

    lane = lax.broadcasted_iota(jnp.int32, (1, 1024), 1)
    row_id = lax.broadcasted_iota(jnp.int32, (128, 1024), 0)
    col_id = lax.broadcasted_iota(jnp.int32, (128, 1024), 1)
    even = lax.broadcasted_iota(jnp.int32, (1, 128), 1) % 2 == 0

    def finish(unit, carry):
        ranks = full[...].reshape(256, 128)
        mine = adapter[:, unit].reshape(256, 1) == lane // RANK

        def widened(first):
            spread = (row_id == unit * 32 + first + col_id % RANK).astype(F32).astype(BF16)
            return jnp.where(mine, dot(ranks, spread), 0.0).astype(BF16)

        wide = widened(0)
        turn = cosine[:, unit].reshape(256, 128)
        sway = sine[:, unit].reshape(256, 128)
        for part in range(3):
            columns = slice(part * HEAD, (part + 1) * HEAD)
            value = acc[:, unit, :, columns].reshape(256, HEAD) + dot(wide, right_qkv[:, columns])
            if part < 2:
                head = value[:, :128]
                swapped = jnp.where(even, pltpu.roll(head, 127, 1), pltpu.roll(head, 1, 1))
                value = jnp.concatenate([head * turn + swapped * sway, value[:, 128:]], axis=1)
            out_qkv[:, unit, :, columns] = value.astype(BF16).reshape(GROUP, UNIT, HEAD)
        wide = widened(RANK)
        for part in range(hid // 256):
            columns = slice(part * 256, (part + 1) * 256)
            value = acc[:, unit, :, QKV + part * 256 : QKV + (part + 1) * 256].reshape(256, 256)
            value = value + dot(wide, right_up[:, columns]) + in_bias[:, columns]
            value = jax.nn.gelu(value, approximate=True)
            out_hidden[:, unit, :, columns] = value.astype(BF16).reshape(GROUP, UNIT, 256)
        return carry

    lax.fori_loop(0, 4, finish, 0)


def attend_kernel(first_chunk, queries, keys_values, starts, out, top, total, summed, *, chunk):
    block = queries.shape[0]
    number = pl.program_id(0)
    req = lax.axis_index("req")
    rows = keys_values.shape[1]
    first_row = req * rows + number * block
    per = rows // chunk
    top[...] = jnp.full_like(top, NEGATIVE_FILL)
    total[...] = jnp.zeros_like(total)
    summed[...] = jnp.zeros_like(summed)
    scaled = queries[...] * jnp.asarray(HEAD ** (-0.5), BF16)
    row_id = first_row + lax.broadcasted_iota(jnp.int32, (block, 1), 0)
    begin = starts[...]
    lane = lax.broadcasted_iota(jnp.int32, (1, chunk), 1)

    def step(c, carry):
        slot = req - c // per
        at = pl.ds(pl.multiple_of((c % per) * chunk, chunk), chunk)
        keys = keys_values[slot, at, :HEAD]
        values = keys_values[slot, at, HEAD:]
        scores = lax.dot_general(scaled, keys, (((1,), (1,)), ((), ())), preferred_element_type=F32)
        key_id = c * chunk + lane
        allowed = jnp.logical_and(key_id >= begin, key_id <= row_id)
        masked = jnp.where(allowed, scores, NEGATIVE_FILL)
        new_top = jnp.maximum(top[...], jnp.max(masked, axis=1, keepdims=True))
        weights = jnp.where(allowed, jnp.exp(masked - new_top), 0.0)
        decay = jnp.exp(top[...] - new_top)
        total[...] = total[...] * decay + jnp.sum(weights, axis=1, keepdims=True)
        summed[...] = summed[...] * decay + dot(weights.astype(BF16), values)
        top[...] = new_top
        return carry

    lax.fori_loop(first_chunk[number], (first_row + block - 1) // chunk + 1, step, 0)
    out[...] = (summed[...] / total[...]).astype(BF16)


REDUCE_GROUPS = (
    tuple((h, d1, 2) for h in (0, 1) for d1 in (2, 1, -1, 0)),
    tuple((h, d1, d2) for h in (0, 1) for d1 in (2, 1) for d2 in (1, -1)),
    tuple((h, d1, d2) for h in (0, 1) for d1 in (-1, 0) for d2 in (1, -1)),
    tuple((h, d1, 0) for h in (0, 1) for d1 in (2, 1, -1, 0)),
)
FAR = {2: 0, 1: 1, -1: 2, 0: 3}


def output_kernel(
    attended, hidden, adapter, tokens, out_bias, w_left_attn, w_left_hid, w_attn, w_down, w_right,
    out,
    inputs, left, weights, part, from2, from1, rows_in, packed, landed, full,
    load_sems, send_sem, sems2, sems1, ex_sems,
):
    plane = Plane()
    me = plane.me
    hid = w_left_hid.shape[0]
    depth = HEAD + hid
    loads = [
        pltpu.make_async_copy(attended, inputs.at[:, :, :, pl.ds(0, HEAD)], load_sems.at[0]),
        pltpu.make_async_copy(hidden, inputs.at[:, :, :, pl.ds(HEAD, hid)], load_sems.at[1]),
        pltpu.make_async_copy(w_left_attn, left.at[pl.ds(0, HEAD)], load_sems.at[2]),
        pltpu.make_async_copy(w_left_hid, left.at[pl.ds(HEAD, hid)], load_sems.at[3]),
        pltpu.make_async_copy(w_attn, weights.at[pl.ds(0, HEAD)], load_sems.at[4]),
        pltpu.make_async_copy(w_down, weights.at[pl.ds(HEAD, hid)], load_sems.at[5]),
        pltpu.make_async_copy(w_right, weights.at[pl.ds(depth, 128)], load_sems.at[6]),
    ]
    for load in loads:
        load.start()
    sem = barrier_all(me, GROUP)
    for load in loads[:4]:
        load.wait()

    lane = lax.broadcasted_iota(jnp.int32, (1, 1024), 1)
    fold_row = lax.broadcasted_iota(jnp.int32, (1024, 128), 0)
    fold_col = lax.broadcasted_iota(jnp.int32, (1024, 128), 1)

    def lower(unit, together):
        mine = adapter[:, unit].reshape(256, 1) == lane // RANK
        for first, begin, end in ((0, 0, HEAD), (RANK, HEAD, depth)):
            product = dot(inputs[:, unit, :, begin:end].reshape(256, end - begin), left[begin:end, :])
            kept = jnp.where(mine, product, 0.0).astype(BF16)
            fold = (fold_col == unit * 32 + first + fold_row % RANK).astype(F32).astype(BF16)
            together = together + dot(kept, fold)
        return together

    together = lax.fori_loop(0, 4, lower, jnp.zeros((256, 128), F32))
    packed[...] = together.astype(BF16).reshape(GROUP, UNIT, 128)
    pl.semaphore_wait(sem, GROUP - 1)
    many = exchange_sum(me, packed, landed, full, ex_sems)
    for load in loads[4:]:
        load.wait()
    exchange_wait(many, ex_sems)
    lane = lax.broadcasted_iota(jnp.int32, (1, 128), 1)
    row_id = lax.broadcasted_iota(jnp.int32, (128, 128), 0)
    col_id = lax.broadcasted_iota(jnp.int32, (128, 128), 1)
    for unit in range(4):
        mine = adapter[:, unit].reshape(256, 1) == me * 4 + lane // 32
        spread = (row_id == unit * 32 + col_id % 32).astype(F32).astype(BF16)
        wide = jnp.where(mine, dot(full[...].reshape(256, 128), spread), 0.0).astype(BF16)
        inputs[:, unit, :, depth:] = wide.reshape(GROUP, UNIT, 128)

    def multiply(number):
        for i, (half, d1, d2) in enumerate(REDUCE_GROUPS[number]):
            slot = plane.source(half, d1, d2)
            for u in (0, 1):
                at = i * 32 + u * UNIT
                rows_in[at : at + UNIT, :] = inputs[slot, half * 2 + u]

        def column(n, carry):
            columns = pl.ds(pl.multiple_of(n * 256, 256), 256)
            result = dot(rows_in[...], weights[:, columns]).astype(BF16)
            for i, (half, d1, d2) in enumerate(REDUCE_GROUPS[number]):
                slot = plane.source(half, d1, d2)
                part[slot, pl.ds(half * 32, 32), columns] = result[i * 32 : (i + 1) * 32, :]
            return carry

        lax.fori_loop(0, out.shape[1] // 256, column, 0)

    def rows_of(half, u):
        return pl.ds(half * 32 + u * UNIT, UNIT)

    def landing(half, axis, side, d1, place):
        index = half * 2 + side
        if axis == 2:
            return from2.at[index, FAR[d1], place], sems2.at[index, FAR[d1] * 3 + place]
        return from1.at[index, place], sems1.at[index, place]

    def send(half, d1, d2, u, axis):
        d = d2 if axis == 2 else d1
        back = d if d != 2 else (1 if u == 0 else -1)
        side = 0 if back == 1 else 1
        place = 2 if d == 2 else u
        slot = plane.source(half, d1, d2)
        to = plane.off(half, 0, -back) if axis == 2 else plane.off(half, -back, 0)
        target, arrived = landing(half, axis, side, d1, place)
        pltpu.make_async_remote_copy(
            part.at[slot, rows_of(half, u), :], target, send_sem, arrived, device_id={"mlp": to}, device_id_type=MESH
        ).start()

    def arrive(half, axis, side, d1, place):
        ref, arrived = landing(half, axis, side, d1, place)
        pltpu.make_async_copy(ref, ref, arrived).wait()
        return ref

    def add(half, d1, d2, u, children):
        refs = [arrive(half, axis, side, d1, place) for axis, side, place in children]
        slot = plane.source(half, d1, d2)
        here = part.at[slot, rows_of(half, u), :]
        value = here[...].astype(F32)
        for ref in refs:
            value = value + ref[...].astype(F32)
        here[...] = value.astype(BF16)

    multiply(0)
    for d1 in (2, 1, -1, 0):
        for half in (0, 1):
            for u in (0, 1):
                send(half, d1, 2, u, 2)
    for number in (1, 2):
        multiply(number)
        for half, d1, d2 in REDUCE_GROUPS[number]:
            send(half, d1, d2, 1 if d2 == 1 else 0, 2)
    for number in (1, 2):
        for half, d1, d2 in REDUCE_GROUPS[number]:
            u = 0 if d2 == 1 else 1
            add(half, d1, d2, u, ((2, 0 if d2 == 1 else 1, 2),))
            send(half, d1, d2, u, 2)
    multiply(3)
    both = lambda u: ((2, 0, u), (2, 1, u))
    for half in (0, 1):
        for u in (0, 1):
            add(half, 2, 0, u, both(u))
            send(half, 2, 0, u, 1)
    for d1 in (1, -1):
        for half in (0, 1):
            u = 1 if d1 == 1 else 0
            add(half, d1, 0, u, both(u))
            send(half, d1, 0, u, 1)
    for d1 in (1, -1):
        for half in (0, 1):
            u = 0 if d1 == 1 else 1
            add(half, d1, 0, u, both(u) + ((1, 0 if d1 == 1 else 1, 2),))
            send(half, d1, 0, u, 1)
    for half in (0, 1):
        for u in (0, 1):
            refs = [arrive(half, axis, side, 0, place) for axis, side, place in both(u) + ((1, 0, u), (1, 1, u))]
            rows = rows_of(half, u)
            value = part[me, rows, :].astype(F32)
            for ref in refs:
                value = value + ref[...].astype(F32)
            out[rows, :] = (value + tokens[rows, :].astype(F32) + out_bias[...]).astype(BF16)
    sent = part.at[pl.ds(0, GROUP - 1)]
    pltpu.make_async_copy(sent, sent, send_sem).wait()


def per_device(
    tokens, layer_norm_gain, layer_norm_bias, query_key_weight, output_weight, up_weight, input_bias, down_weight,
    output_bias, input_adapter_left, query_key_value_right, up_adapter_right, output_adapter_left, down_adapter_left,
    output_adapter_right, lengths, request_adapter, slot_adapter,
):
    rows, width = tokens.shape
    group_rows = rows * GROUP
    req = lax.axis_index("req")
    hid = up_weight.shape[1]

    ends = jnp.cumsum(lengths)
    begins = ends - lengths
    index = req * group_rows + lax.iota(jnp.int32, group_rows)
    inside = jnp.logical_and(begins[None, :] <= index[:, None], index[:, None] < ends[None, :])
    start = jnp.sum(jnp.where(inside, begins[None, :], 0), axis=1)
    adapter = jnp.sum(jnp.where(inside, request_adapter[None, :], 0), axis=1)
    lane = lax.iota(jnp.int32, 128)
    frequency = jnp.exp((lane // 2).astype(F32) * (-2.0 * math.log(10000.0) / ROT))
    angle = (index - start).astype(F32)[:, None] * frequency[None, :]
    turned = (lane < ROT)[None, :]
    cosine = jnp.where(turned, jnp.cos(angle), 1.0)
    sine = jnp.where(turned, jnp.where(lane % 2 == 0, -1.0, 1.0)[None, :] * jnp.sin(angle), 0.0)

    vmem = pl.BlockSpec(memory_space=pltpu.VMEM)
    smem = pl.BlockSpec(memory_space=pltpu.SMEM)
    anywhere = pl.BlockSpec(memory_space=pl.ANY)
    dma = pltpu.SemaphoreType.DMA
    by_unit = (GROUP, 4, UNIT)
    adapter_units = adapter.reshape(by_unit + (1,))
    qkv, hidden = pl.pallas_call(
        input_kernel,
        out_shape=(
            jax.ShapeDtypeStruct(by_unit + (QKV,), BF16),
            jax.ShapeDtypeStruct(by_unit + (hid,), BF16),
        ),
        in_specs=[vmem] * 5 + [smem] + [vmem] * 2 + [anywhere] * 5,
        out_specs=(vmem, vmem),
        scratch_shapes=[
            pltpu.VMEM((GROUP, rows, width), BF16),
            pltpu.VMEM((width, QKV + hid + 128), BF16),
            pltpu.VMEM(query_key_value_right.shape[:1] + (QKV,), BF16),
            pltpu.VMEM(up_adapter_right.shape, BF16),
            pltpu.VMEM((256, width), BF16),
            pltpu.VMEM(by_unit + (QKV + hid,), F32),
            pltpu.VMEM(by_unit + (128,), BF16),
            pltpu.VMEM((GROUP, UNIT, 128), BF16),
            pltpu.VMEM((GROUP, UNIT, 128), BF16),
            pltpu.VMEM((GROUP, UNIT, 128), BF16),
            dma((5,)),
            dma,
            dma((GROUP, 4)),
            dma((4,)),
        ],
        compiler_params=pltpu.CompilerParams(
            collective_id=0, has_side_effects=True, vmem_limit_bytes=VMEM_LIMIT
        ),
        name="input_stage",
    )(
        tokens, layer_norm_gain[None, :], layer_norm_bias[None, :], input_bias[None, :], adapter_units, slot_adapter,
        cosine.reshape(by_unit + (128,)), sine.reshape(by_unit + (128,)),
        query_key_weight.reshape(width, QKV), up_weight, input_adapter_left,
        query_key_value_right.reshape(-1, QKV), up_adapter_right,
    )
    qkv = qkv.reshape(group_rows, QKV)

    gathered = lax.all_gather(qkv[:, HEAD:], "req", axis=0)
    slots = jnp.maximum(req - lax.iota(jnp.int32, 5), 0)
    window = jnp.stack([lax.dynamic_index_in_dim(gathered, slots[i], 0, keepdims=False) for i in range(5)])

    block, chunk = 256, 512
    blocks = group_rows // block
    first_chunk = start.reshape(blocks, block)[:, 0] // chunk
    attended = pl.pallas_call(
        functools.partial(attend_kernel, chunk=chunk),
        out_shape=jax.ShapeDtypeStruct((group_rows, HEAD), BF16),
        grid_spec=pltpu.PrefetchScalarGridSpec(
            num_scalar_prefetch=1,
            grid=(blocks,),
            in_specs=[
                pl.BlockSpec((block, HEAD), lambda i, s: (i, 0)),
                pl.BlockSpec((5, group_rows, 2 * HEAD), lambda i, s: (0, 0, 0), pipeline_mode=pl.Buffered(1)),
                pl.BlockSpec((block, 1), lambda i, s: (i, 0)),
            ],
            out_specs=pl.BlockSpec((block, HEAD), lambda i, s: (i, 0)),
            scratch_shapes=[
                pltpu.VMEM((block, 1), F32),
                pltpu.VMEM((block, 1), F32),
                pltpu.VMEM((block, HEAD), F32),
            ],
        ),
        compiler_params=pltpu.CompilerParams(vmem_limit_bytes=VMEM_LIMIT),
        name="attend_stage",
    )(first_chunk, qkv[:, :HEAD], window, start[:, None])

    depth = HEAD + hid + 128
    return pl.pallas_call(
        output_kernel,
        out_shape=jax.ShapeDtypeStruct((rows, width), BF16),
        in_specs=[anywhere] * 2 + [vmem] * 3 + [anywhere] * 5,
        out_specs=vmem,
        scratch_shapes=[
            pltpu.VMEM(by_unit + (depth,), BF16),
            pltpu.VMEM((HEAD + hid, 1024), BF16),
            pltpu.VMEM((depth, width), BF16),
            pltpu.VMEM((GROUP, rows, width), BF16),
            pltpu.VMEM((4, 4, 3, UNIT, width), BF16),
            pltpu.VMEM((4, 3, UNIT, width), BF16),
            pltpu.VMEM((256, depth), BF16),
            pltpu.VMEM((GROUP, UNIT, 128), BF16),
            pltpu.VMEM((GROUP, UNIT, 128), BF16),
            pltpu.VMEM((GROUP, UNIT, 128), BF16),
            dma((7,)),
            dma,
            dma((4, 12)),
            dma((4, 3)),
            dma((4,)),
        ],
        compiler_params=pltpu.CompilerParams(
            collective_id=1, has_side_effects=True, vmem_limit_bytes=VMEM_LIMIT
        ),
        name="output_stage",
    )(
        attended.reshape(by_unit + (HEAD,)), hidden, adapter_units, tokens, output_bias[None, :],
        output_adapter_left.reshape(HEAD, -1), down_adapter_left, output_weight.reshape(HEAD, width), down_weight,
        output_adapter_right,
    )


def solution(mesh):
    in_specs = (
        P(("req", "mlp"), None), P(), P(), P(None, "mlp", None), P("mlp", None, None), P(None, "mlp"), P("mlp"),
        P("mlp", None), P(), P(None, "mlp"), P(None, "mlp", None), P(None, "mlp"), P("mlp", None, None),
        P("mlp", None), P("mlp", None), P(), P(), P("mlp"),
    )
    return jax.shard_map(
        per_device, mesh=mesh, in_specs=in_specs, out_specs=P(("req", "mlp"), None), check_vma=False
    )
```

```python
import math

import jax
import jax.numpy as jnp
from jax import lax
from jax.experimental import pallas as pl
from jax.experimental.pallas import tpu as pltpu
from jax.sharding import PartitionSpec as P

HEAD = 256
ROT = 64
RANK = 16
EPSILON = 1e-05
NEGATIVE_FILL = -1e30
MESH = pl.DeviceIdType.MESH
F32 = jnp.float32
BF16 = jnp.bfloat16
VMEM_LIMIT = 60 * 1024 * 1024
SIDE = 4
GROUP = 16
UNIT = 16
QKV = 3 * HEAD
CUT = 6


def dot(a, b):
    return jnp.dot(a, b, preferred_element_type=F32)


class Plane:
    def __init__(self):
        self.me = lax.axis_index("mlp")
        self.z = self.me // SIDE
        self.y = self.me % SIDE

    def at(self, dz, dy):
        return ((self.z + dz + SIDE) % SIDE) * SIDE + (self.y + dy + SIDE) % SIDE

    def off(self, half, d1, d2):
        return self.at(d1, d2) if half == 0 else self.at(d2, d1)

    def source(self, half, d1, d2):
        return self.off(half, -d1, -d2)


def barrier_all(me, count):
    sem = pltpu.get_barrier_semaphore()
    for k in range(1, count):
        pl.semaphore_signal(sem, inc=1, device_id={"mlp": (me + k) % count}, device_id_type=MESH)
    return sem


def exchange_sum(me, packed, landed, full, sems, meanwhile):
    def scatter(k, carry):
        to = (me + k) % GROUP
        pltpu.make_async_remote_copy(
            packed.at[to], landed.at[me], sems.at[0], sems.at[1], device_id={"mlp": to}, device_id_type=MESH
        ).start()
        return carry

    lax.fori_loop(1, GROUP, scatter, 0)
    landed[me] = packed[me]
    meanwhile()
    many = landed.at[pl.ds(0, GROUP - 1)]
    pltpu.make_async_copy(many, many, sems.at[1]).wait()
    full[me] = jnp.sum(landed[...].astype(F32), axis=0).astype(BF16)

    def gather(k, carry):
        to = (me + k) % GROUP
        pltpu.make_async_remote_copy(
            full.at[me], full.at[me], sems.at[2], sems.at[3], device_id={"mlp": to}, device_id_type=MESH
        ).start()
        return carry

    lax.fori_loop(1, GROUP, gather, 0)
    pltpu.make_async_copy(many, many, sems.at[0]).wait()
    return many


def exchange_wait(many, sems):
    pltpu.make_async_copy(many, many, sems.at[3]).wait()
    pltpu.make_async_copy(many, many, sems.at[2]).wait()


GATHER_GROUPS = (
    tuple((h, d1, 0) for h in (0, 1) for d1 in (0, 1, -1, 2)),
    tuple((h, d1, d2) for h in (0, 1) for d1 in (0, 1) for d2 in (1, -1)),
    tuple((h, d1, d2) for h in (0, 1) for d1 in (-1, 2) for d2 in (1, -1)),
    tuple((h, d1, 2) for h in (0, 1) for d1 in (0, 1, -1, 2)),
)


def front_kernel(
    tokens, gain, bias, in_bias, lengths, request_adapter, slots, frequency, w_qkv, w_up, w_left, w_qkv_right, w_up_right,
    out_attended, out_hidden, adapter,
    xs, weights, right_qkv, right_up, rows_in, acc, picked, packed, landed, full,
    starts, cosine, sine, queries, window, passing, top, total, summed,
    load_sems, send_sem, recv_sems, ex_sems, near_send, near_recv,
):
    plane = Plane()
    me = plane.me
    req = lax.axis_index("req")
    chip, core = req // 2, req % 2
    ahead = ((chip + 1) % SIDE) * 2 + core
    behind = ((chip + 3) % SIDE) * 2 + core
    other = chip * 2 + 1 - core
    hid = w_up.shape[1]
    count = GROUP * 64
    loads = [
        pltpu.make_async_copy(w_qkv, weights.at[:, pl.ds(0, QKV)], load_sems.at[0]),
        pltpu.make_async_copy(w_up, weights.at[:, pl.ds(QKV, hid)], load_sems.at[1]),
        pltpu.make_async_copy(w_left, weights.at[:, pl.ds(QKV + hid, 128)], load_sems.at[2]),
        pltpu.make_async_copy(w_qkv_right, right_qkv, load_sems.at[3]),
        pltpu.make_async_copy(w_up_right, right_up, load_sems.at[4]),
    ]
    for load in loads:
        load.start()
    sem = barrier_all(me, GROUP)
    for device in (ahead, behind, other):
        pl.semaphore_signal(sem, inc=1, device_id={"req": device}, device_id_type=MESH)
    for part in range(0, 64, 16):
        values = tokens[part : part + 16, :].astype(F32)
        center = values - jnp.mean(values, axis=1, keepdims=True)
        spread = jnp.mean(center * center, axis=1, keepdims=True)
        scaled = center * lax.rsqrt(spread + EPSILON)
        xs[me, part : part + 16, :] = (scaled * gain[...] + bias[...]).astype(BF16)
    pl.semaphore_wait(sem, GROUP + 2)

    def send(slot, half, units, axis, step):
        first, many = units
        rows = pl.ds(half * 32 + first * UNIT, many * UNIT)
        to = plane.off(half, step, 0) if axis == 1 else plane.off(half, 0, step)
        pltpu.make_async_remote_copy(
            xs.at[slot, rows, :], xs.at[slot, rows, :], send_sem, recv_sems.at[slot, half * 2 + first],
            device_id={"mlp": to}, device_id_type=MESH,
        ).start()

    def landed_piece(half, d1, d2, units):
        first, many = units
        slot = plane.source(half, d1, d2)
        rows = pl.ds(half * 32 + first * UNIT, many * UNIT)
        view = xs.at[slot, rows, :]
        pltpu.make_async_copy(view, view, recv_sems.at[slot, half * 2 + first]).wait()
        return slot

    whole = (0, 2)
    for half in (0, 1):
        for step in (1, -1):
            send(me, half, whole, 1, step)
    for half in (0, 1):
        for step in (1, -1):
            send(me, half, whole, 2, step)

    long = lengths[...].astype(F32)
    requests = long.shape[1]
    before = lax.broadcasted_iota(jnp.int32, (requests, requests), 0) < lax.broadcasted_iota(
        jnp.int32, (requests, requests), 1
    )
    begins = dot(jnp.broadcast_to(long, (8, requests)).astype(BF16), before.astype(F32).astype(BF16))[:1, :]
    ends = begins + long
    ids = request_adapter[...].astype(F32)

    def locate(block, carry):
        rows = lax.broadcasted_iota(jnp.int32, (64, 1), 0)
        index = (req * count + block * 64 + rows).astype(F32)
        inside = jnp.logical_and(begins <= index, index < ends)
        start = jnp.sum(jnp.where(inside, begins, 0.0), axis=1, keepdims=True)
        mine = jnp.sum(jnp.where(inside, ids, 0.0), axis=1, keepdims=True)
        starts[block] = start.reshape(4, UNIT, 1)
        adapter[block] = mine.reshape(4, UNIT, 1)
        return carry

    lax.fori_loop(0, GROUP, locate, 0)

    for half in (0, 1):
        for d1 in (1, -1):
            slot = landed_piece(half, d1, 0, whole)
            send(slot, half, (0, 1) if d1 == 1 else (1, 1), 1, d1)
            for step in (1, -1):
                send(slot, half, whole, 2, step)

    def relay(half, d1, d2, pieces):
        for units in pieces:
            slot = landed_piece(half, d1, d2, units)
        send(slot, half, (0, 1) if d2 == 1 else (1, 1), 2, d2)

    lane = lax.broadcasted_iota(jnp.int32, (1, 128), 1)
    even = lane % 2 == 0

    def angles(block, carry):
        rows = lax.broadcasted_iota(jnp.int32, (64, 1), 0)
        index = (req * count + block * 64 + rows).astype(F32)
        angle = (index - starts[block].reshape(64, 1)) * frequency[...]
        turned = lane < ROT
        cosine[block] = jnp.where(turned, jnp.cos(angle), 1.0).reshape(4, UNIT, 128)
        sine[block] = jnp.where(turned, jnp.where(even, -1.0, 1.0) * jnp.sin(angle), 0.0).reshape(4, UNIT, 128)
        return carry

    def multiply(number):
        for i, (half, d1, d2) in enumerate(GATHER_GROUPS[number]):
            rows_in[i * 32 : (i + 1) * 32, :] = xs[plane.source(half, d1, d2), pl.ds(half * 32, 32), :]
        left = dot(rows_in[...], weights[:, QKV + hid :])
        for i, (half, d1, d2) in enumerate(GATHER_GROUPS[number]):
            slot = plane.source(half, d1, d2)
            for u in (0, 1):
                at = i * 32 + u * UNIT
                picked[slot, half * 2 + u] = left[at : at + UNIT, :].astype(BF16)

    def multiply_wide(number, begin, end):
        def column(n, carry):
            columns = pl.ds(pl.multiple_of(n * 256, 256), 256)
            result = dot(rows_in[...], weights[:, columns])
            for i, (half, d1, d2) in enumerate(GATHER_GROUPS[number]):
                slot = plane.source(half, d1, d2)
                for u in (0, 1):
                    at = i * 32 + u * UNIT
                    acc[slot, half * 2 + u, :, columns] = result[at : at + UNIT, :]
            return carry

        lax.fori_loop(begin, end, column, 0)

    tiles = (QKV + hid) // 256
    lax.fori_loop(0, GROUP // 2, angles, 0)
    for half in (0, 1):
        for d2 in (1, -1):
            relay(half, 0, d2, (whole,))
    for half in (0, 1):
        for unit in ((0, 1), (1, 1)):
            slot = landed_piece(half, 2, 0, unit)
            for step in (1, -1):
                send(slot, half, unit, 2, step)
    for load in loads[:3]:
        load.wait()
    multiply(0)
    multiply_wide(0, 0, tiles)
    for half in (0, 1):
        for d1 in (1, -1):
            for d2 in (1, -1):
                relay(half, d1, d2, (whole,))
    multiply(1)
    multiply_wide(1, 0, tiles)
    lax.fori_loop(GROUP // 2, GROUP, angles, 0)
    for half in (0, 1):
        for d2 in (1, -1):
            relay(half, 2, d2, ((0, 1), (1, 1)))
    multiply(2)
    multiply_wide(2, 0, tiles)
    for half in (0, 1):
        for d1 in (0, 1, -1, 2):
            for unit in ((0, 1), (1, 1)):
                landed_piece(half, d1, 2, unit)
    multiply(3)

    chosen = jnp.where(lane < 32, slots[0], jnp.where(lane < 64, slots[1], jnp.where(lane < 96, slots[2], slots[3])))
    chosen = chosen.astype(F32)
    row_id = lax.broadcasted_iota(jnp.int32, (128, 128), 0)
    col_id = lax.broadcasted_iota(jnp.int32, (128, 128), 1)
    together = jnp.zeros((256, 128), F32)
    for unit in range(4):
        mine = adapter[:, unit].reshape(256, 1) == chosen
        kept = jnp.where(mine, picked[:, unit].reshape(256, 128).astype(F32), 0.0).astype(BF16)
        fold = jnp.logical_and(col_id // 32 == unit, row_id % 32 == col_id % 32).astype(F32).astype(BF16)
        together = together + dot(kept, fold)
    packed[...] = together.astype(BF16).reshape(GROUP, UNIT, 128)
    many = exchange_sum(me, packed, landed, full, ex_sems, lambda: multiply_wide(3, 0, 2))
    multiply_wide(3, 2, tiles)
    exchange_wait(many, ex_sems)
    for load in loads[3:]:
        load.wait()

    wide_lane = lax.broadcasted_iota(jnp.int32, (1, 1024), 1)
    owner = (wide_lane // RANK).astype(F32)
    row_id = lax.broadcasted_iota(jnp.int32, (128, 1024), 0)
    col_id = lax.broadcasted_iota(jnp.int32, (128, 1024), 1)

    def widened(unit, first):
        spread = (row_id == unit * 32 + first + col_id % RANK).astype(F32).astype(BF16)
        mine = adapter[:, unit].reshape(256, 1) == owner
        return jnp.where(mine, dot(full[...].reshape(256, 128), spread), 0.0).astype(BF16)

    def finish_heads(unit, carry):
        wide = widened(unit, 0)
        turn = cosine[:, unit].reshape(256, 128)
        sway = sine[:, unit].reshape(256, 128)
        for part in range(3):
            columns = slice(part * HEAD, (part + 1) * HEAD)
            value = acc[:, unit, :, columns].reshape(256, HEAD) + dot(wide, right_qkv[:, columns])
            if part < 2:
                head = value[:, :128]
                swapped = jnp.where(even, pltpu.roll(head, 127, 1), pltpu.roll(head, 1, 1))
                value = jnp.concatenate([head * turn + swapped * sway, value[:, 128:]], axis=1)
            value = value.astype(BF16)
            if part == 0:
                queries[:, unit] = (value * jnp.asarray(HEAD ** (-0.5), BF16)).reshape(GROUP, UNIT, HEAD)
            else:
                window[0, :, unit, :, (part - 1) * HEAD : part * HEAD] = value.reshape(GROUP, UNIT, HEAD)
        return carry

    def finish_hidden(unit, carry):
        wide = widened(unit, RANK)
        for part in range(hid // 256):
            columns = slice(part * 256, (part + 1) * 256)
            value = acc[:, unit, :, QKV + part * 256 : QKV + (part + 1) * 256].reshape(256, 256)
            value = value + dot(wide, right_up[:, columns]) + in_bias[:, columns]
            value = jax.nn.gelu(value, approximate=True)
            out_hidden[:, unit, :, columns] = value.astype(BF16).reshape(GROUP, UNIT, 256)
        return carry

    lax.fori_loop(0, 4, finish_heads, 0)

    low, high = pl.ds(0, CUT), pl.ds(CUT, GROUP - CUT)
    started = []

    def pass_on(src, dst, number, device):
        copy = pltpu.make_async_remote_copy(
            src, dst, near_send.at[number], near_recv.at[number], device_id={"req": device}, device_id_type=MESH
        )
        copy.start()
        started.append(copy)

    def take(ref, number):
        pltpu.make_async_copy(ref, ref, near_recv.at[number]).wait()

    pass_on(window.at[0, low], window.at[2, low], 0, ahead)
    pass_on(window.at[0, high], passing, 2, behind)
    pass_on(window.at[0, high], window.at[2, high], 1, ahead)
    pass_on(window.at[0], window.at[1 + 4 * core], 3, other)

    def attend(slot, m0, m1, b, causal):
        keys = window[slot, m0:m1, :, :, :HEAD].reshape((m1 - m0) * 64, HEAD)
        values = window[slot, m0:m1, :, :, HEAD:].reshape((m1 - m0) * 64, HEAD)
        four = pl.ds(b * 4, 4)
        scores = lax.dot_general(
            queries[four].reshape(256, HEAD), keys, (((1,), (1,)), ((), ())), preferred_element_type=F32
        )
        key_id = lax.broadcasted_iota(jnp.int32, (1, (m1 - m0) * 64), 1) + (req - slot) * count + m0 * 64
        allowed = key_id.astype(F32) >= starts[four].reshape(256, 1)
        if causal:
            row = lax.broadcasted_iota(jnp.int32, (256, 1), 0) + req * count + b * 256
            allowed = jnp.logical_and(allowed, key_id <= row)
        scores = jnp.where(allowed, scores, NEGATIVE_FILL)
        peak = jnp.max(scores, axis=1, keepdims=True)
        if causal:
            kept = jnp.exp(scores - peak)
            top[b] = peak
            total[b] = jnp.sum(kept, axis=1, keepdims=True)
            summed[b] = dot(kept.astype(BF16), values)
        else:
            old = top[b]
            peak = jnp.maximum(old, peak)
            kept = jnp.exp(scores - peak)
            decay = jnp.exp(old - peak)
            top[b] = peak
            total[b] = total[b] * decay + jnp.sum(kept, axis=1, keepdims=True)
            summed[b] = summed[b] * decay + dot(kept.astype(BF16), values)

    def attend_all(slot, m0, m1):
        def body(b, carry):
            attend(slot, m0, m1, b, False)
            return carry

        lax.fori_loop(0, 4, body, 0)

    for b in range(4):
        attend(0, 0, (b + 1) * 4, b, True)
    take(window.at[2, low], 0)
    pass_on(window.at[2, low], window.at[4, low], 6, ahead)
    pass_on(window.at[2, low], window.at[3 - 2 * core, low], 4, other)
    take(window.at[5 - 4 * core], 3)

    @pl.when(core == 1)
    def _():
        attend_all(1, 0, GROUP)

    take(passing, 2)
    pass_on(passing, window.at[4, high], 7, behind)
    lax.fori_loop(0, 4, finish_hidden, 0)
    attend_all(2, 0, CUT)
    take(window.at[2, high], 1)
    pass_on(window.at[2, high], window.at[3 - 2 * core, high], 5, other)
    attend_all(2, CUT, GROUP)
    take(window.at[1 + 2 * core, low], 4)
    attend_all(1 + 2 * core, 0, CUT)
    take(window.at[1 + 2 * core, high], 5)
    attend_all(1 + 2 * core, CUT, GROUP)
    take(window.at[4, high], 7)
    pass_on(window.at[4, high], window.at[5 - 2 * core, high], 9, other)
    attend_all(4, CUT, GROUP)
    take(window.at[4, low], 6)
    pass_on(window.at[4, low], window.at[5 - 2 * core, low], 8, other)
    attend_all(4, 0, CUT)
    take(window.at[3 + 2 * core, high], 9)

    @pl.when(core == 0)
    def _():
        attend_all(3, CUT, GROUP)

    take(window.at[3 + 2 * core, low], 8)

    @pl.when(core == 0)
    def _():
        attend_all(3, 0, CUT)

    for b in range(4):
        out_attended[b * 4 : (b + 1) * 4] = (summed[b] / total[b]).astype(BF16).reshape(4, 4, UNIT, HEAD)
    for copy in started:
        copy.wait_send()
    sent = xs.at[pl.ds(0, GROUP - 1)]
    pltpu.make_async_copy(sent, sent, send_sem).wait()


REDUCE_GROUPS = (
    tuple((h, d1, 2) for h in (0, 1) for d1 in (2, 1, -1, 0)),
    tuple((h, d1, d2) for h in (0, 1) for d1 in (2, 1) for d2 in (1, -1)),
    tuple((h, d1, d2) for h in (0, 1) for d1 in (-1, 0) for d2 in (1, -1)),
    tuple((h, d1, 0) for h in (0, 1) for d1 in (2, 1, -1, 0)),
)
FAR = {2: 0, 1: 1, -1: 2, 0: 3}


def output_kernel(
    attended, hidden, adapter, tokens, out_bias, w_left_attn, w_left_hid, w_attn, w_down, w_right,
    out,
    inputs, left, weights, part, from2, from1, rows_in, packed, landed, full,
    load_sems, send_sem, sems2, sems1, ex_sems,
):
    plane = Plane()
    me = plane.me
    hid = w_left_hid.shape[0]
    depth = HEAD + hid
    loads = [
        pltpu.make_async_copy(attended, inputs.at[:, :, :, pl.ds(0, HEAD)], load_sems.at[0]),
        pltpu.make_async_copy(hidden, inputs.at[:, :, :, pl.ds(HEAD, hid)], load_sems.at[1]),
        pltpu.make_async_copy(w_left_attn, left.at[pl.ds(0, HEAD)], load_sems.at[2]),
        pltpu.make_async_copy(w_left_hid, left.at[pl.ds(HEAD, hid)], load_sems.at[3]),
        pltpu.make_async_copy(w_attn, weights.at[pl.ds(0, HEAD)], load_sems.at[4]),
        pltpu.make_async_copy(w_down, weights.at[pl.ds(HEAD, hid)], load_sems.at[5]),
        pltpu.make_async_copy(w_right, weights.at[pl.ds(depth, 128)], load_sems.at[6]),
    ]
    for load in loads:
        load.start()
    sem = barrier_all(me, GROUP)
    for load in loads[:4]:
        load.wait()

    lane = lax.broadcasted_iota(jnp.int32, (1, 1024), 1)
    fold_row = lax.broadcasted_iota(jnp.int32, (1024, 128), 0)
    fold_col = lax.broadcasted_iota(jnp.int32, (1024, 128), 1)

    def lower(unit, together):
        mine = adapter[:, unit].reshape(256, 1) == (lane // RANK).astype(F32)
        for first, begin, end in ((0, 0, HEAD), (RANK, HEAD, depth)):
            product = dot(inputs[:, unit, :, begin:end].reshape(256, end - begin), left[begin:end, :])
            kept = jnp.where(mine, product, 0.0).astype(BF16)
            fold = (fold_col == unit * 32 + first + fold_row % RANK).astype(F32).astype(BF16)
            together = together + dot(kept, fold)
        return together

    together = lax.fori_loop(0, 4, lower, jnp.zeros((256, 128), F32))
    packed[...] = together.astype(BF16).reshape(GROUP, UNIT, 128)
    pl.semaphore_wait(sem, GROUP - 1)
    many = exchange_sum(me, packed, landed, full, ex_sems, lambda: None)
    for load in loads[4:]:
        load.wait()
    exchange_wait(many, ex_sems)
    lane = lax.broadcasted_iota(jnp.int32, (1, 128), 1)
    row_id = lax.broadcasted_iota(jnp.int32, (128, 128), 0)
    col_id = lax.broadcasted_iota(jnp.int32, (128, 128), 1)
    for unit in range(4):
        mine = adapter[:, unit].reshape(256, 1) == (me * 4 + lane // 32).astype(F32)
        spread = (row_id == unit * 32 + col_id % 32).astype(F32).astype(BF16)
        wide = jnp.where(mine, dot(full[...].reshape(256, 128), spread), 0.0).astype(BF16)
        inputs[:, unit, :, depth:] = wide.reshape(GROUP, UNIT, 128)

    def multiply(number):
        for i, (half, d1, d2) in enumerate(REDUCE_GROUPS[number]):
            slot = plane.source(half, d1, d2)
            for u in (0, 1):
                at = i * 32 + u * UNIT
                rows_in[at : at + UNIT, :] = inputs[slot, half * 2 + u]

        def column(n, carry):
            columns = pl.ds(pl.multiple_of(n * 256, 256), 256)
            result = dot(rows_in[...], weights[:, columns]).astype(BF16)
            for i, (half, d1, d2) in enumerate(REDUCE_GROUPS[number]):
                slot = plane.source(half, d1, d2)
                part[slot, pl.ds(half * 32, 32), columns] = result[i * 32 : (i + 1) * 32, :]
            return carry

        lax.fori_loop(0, out.shape[1] // 256, column, 0)

    def rows_of(half, u):
        return pl.ds(half * 32 + u * UNIT, UNIT)

    def landing(half, axis, side, d1, place):
        index = half * 2 + side
        if axis == 2:
            return from2.at[index, FAR[d1], place], sems2.at[index, FAR[d1] * 3 + place]
        return from1.at[index, place], sems1.at[index, place]

    def send(half, d1, d2, u, axis):
        d = d2 if axis == 2 else d1
        back = d if d != 2 else (1 if u == 0 else -1)
        side = 0 if back == 1 else 1
        place = 2 if d == 2 else u
        slot = plane.source(half, d1, d2)
        to = plane.off(half, 0, -back) if axis == 2 else plane.off(half, -back, 0)
        target, arrived = landing(half, axis, side, d1, place)
        pltpu.make_async_remote_copy(
            part.at[slot, rows_of(half, u), :], target, send_sem, arrived, device_id={"mlp": to}, device_id_type=MESH
        ).start()

    def arrive(half, axis, side, d1, place):
        ref, arrived = landing(half, axis, side, d1, place)
        pltpu.make_async_copy(ref, ref, arrived).wait()
        return ref

    def add(half, d1, d2, u, children):
        refs = [arrive(half, axis, side, d1, place) for axis, side, place in children]
        slot = plane.source(half, d1, d2)
        here = part.at[slot, rows_of(half, u), :]
        value = here[...].astype(F32)
        for ref in refs:
            value = value + ref[...].astype(F32)
        here[...] = value.astype(BF16)

    multiply(0)
    for d1 in (2, 1, -1, 0):
        for half in (0, 1):
            for u in (0, 1):
                send(half, d1, 2, u, 2)
    for number in (1, 2):
        multiply(number)
        for half, d1, d2 in REDUCE_GROUPS[number]:
            send(half, d1, d2, 1 if d2 == 1 else 0, 2)
    for number in (1, 2):
        for half, d1, d2 in REDUCE_GROUPS[number]:
            u = 0 if d2 == 1 else 1
            add(half, d1, d2, u, ((2, 0 if d2 == 1 else 1, 2),))
            send(half, d1, d2, u, 2)
    multiply(3)
    both = lambda u: ((2, 0, u), (2, 1, u))
    for half in (0, 1):
        for u in (0, 1):
            add(half, 2, 0, u, both(u))
            send(half, 2, 0, u, 1)
    for d1 in (1, -1):
        for half in (0, 1):
            u = 1 if d1 == 1 else 0
            add(half, d1, 0, u, both(u))
            send(half, d1, 0, u, 1)
    for d1 in (1, -1):
        for half in (0, 1):
            u = 0 if d1 == 1 else 1
            add(half, d1, 0, u, both(u) + ((1, 0 if d1 == 1 else 1, 2),))
            send(half, d1, 0, u, 1)
    for half in (0, 1):
        for u in (0, 1):
            refs = [arrive(half, axis, side, 0, place) for axis, side, place in both(u) + ((1, 0, u), (1, 1, u))]
            rows = rows_of(half, u)
            value = part[me, rows, :].astype(F32)
            for ref in refs:
                value = value + ref[...].astype(F32)
            out[rows, :] = (value + tokens[rows, :].astype(F32) + out_bias[...]).astype(BF16)
    sent = part.at[pl.ds(0, GROUP - 1)]
    pltpu.make_async_copy(sent, sent, send_sem).wait()


def per_device(
    tokens, layer_norm_gain, layer_norm_bias, query_key_weight, output_weight, up_weight, input_bias, down_weight,
    output_bias, input_adapter_left, query_key_value_right, up_adapter_right, output_adapter_left, down_adapter_left,
    output_adapter_right, lengths, request_adapter, slot_adapter,
):
    rows, width = tokens.shape
    hid = up_weight.shape[1]
    lane = lax.iota(jnp.int32, 128)
    frequency = jnp.exp((lane // 2).astype(F32) * (-2.0 * math.log(10000.0) / ROT))
    vmem = pl.BlockSpec(memory_space=pltpu.VMEM)
    smem = pl.BlockSpec(memory_space=pltpu.SMEM)
    anywhere = pl.BlockSpec(memory_space=pl.ANY)
    dma = pltpu.SemaphoreType.DMA
    by_unit = (GROUP, 4, UNIT)
    attended, hidden, adapter = pl.pallas_call(
        front_kernel,
        out_shape=(
            jax.ShapeDtypeStruct(by_unit + (HEAD,), BF16),
            jax.ShapeDtypeStruct(by_unit + (hid,), BF16),
            jax.ShapeDtypeStruct(by_unit + (1,), F32),
        ),
        in_specs=[vmem] * 6 + [smem] + [vmem] + [anywhere] * 5,
        out_specs=(vmem, vmem, vmem),
        scratch_shapes=[
            pltpu.VMEM((GROUP, rows, width), BF16),
            pltpu.VMEM((width, QKV + hid + 128), BF16),
            pltpu.VMEM(query_key_value_right.shape[:1] + (QKV,), BF16),
            pltpu.VMEM(up_adapter_right.shape, BF16),
            pltpu.VMEM((256, width), BF16),
            pltpu.VMEM(by_unit + (QKV + hid,), F32),
            pltpu.VMEM(by_unit + (128,), BF16),
            pltpu.VMEM((GROUP, UNIT, 128), BF16),
            pltpu.VMEM((GROUP, UNIT, 128), BF16),
            pltpu.VMEM((GROUP, UNIT, 128), BF16),
            pltpu.VMEM(by_unit + (1,), F32),
            pltpu.VMEM(by_unit + (128,), F32),
            pltpu.VMEM(by_unit + (128,), F32),
            pltpu.VMEM(by_unit + (HEAD,), BF16),
            pltpu.VMEM((6,) + by_unit + (2 * HEAD,), BF16),
            pltpu.VMEM((GROUP - CUT, 4, UNIT, 2 * HEAD), BF16),
            pltpu.VMEM((4, 256, 1), F32),
            pltpu.VMEM((4, 256, 1), F32),
            pltpu.VMEM((4, 256, HEAD), F32),
            dma((5,)),
            dma,
            dma((GROUP, 4)),
            dma((4,)),
            dma((10,)),
            dma((10,)),
        ],
        compiler_params=pltpu.CompilerParams(
            collective_id=0, has_side_effects=True, vmem_limit_bytes=VMEM_LIMIT
        ),
        name="front_stage",
    )(
        tokens, layer_norm_gain[None, :], layer_norm_bias[None, :], input_bias[None, :], lengths[None, :],
        request_adapter[None, :], slot_adapter, frequency[None, :],
        query_key_weight.reshape(width, QKV), up_weight, input_adapter_left,
        query_key_value_right.reshape(-1, QKV), up_adapter_right,
    )

    depth = HEAD + hid + 128
    return pl.pallas_call(
        output_kernel,
        out_shape=jax.ShapeDtypeStruct((rows, width), BF16),
        in_specs=[anywhere] * 2 + [vmem] * 3 + [anywhere] * 5,
        out_specs=vmem,
        scratch_shapes=[
            pltpu.VMEM(by_unit + (depth,), BF16),
            pltpu.VMEM((HEAD + hid, 1024), BF16),
            pltpu.VMEM((depth, width), BF16),
            pltpu.VMEM((GROUP, rows, width), BF16),
            pltpu.VMEM((4, 4, 3, UNIT, width), BF16),
            pltpu.VMEM((4, 3, UNIT, width), BF16),
            pltpu.VMEM((256, depth), BF16),
            pltpu.VMEM((GROUP, UNIT, 128), BF16),
            pltpu.VMEM((GROUP, UNIT, 128), BF16),
            pltpu.VMEM((GROUP, UNIT, 128), BF16),
            dma((7,)),
            dma,
            dma((4, 12)),
            dma((4, 3)),
            dma((4,)),
        ],
        compiler_params=pltpu.CompilerParams(
            collective_id=1, has_side_effects=True, vmem_limit_bytes=VMEM_LIMIT
        ),
        name="output_stage",
    )(
        attended, hidden, adapter, tokens, output_bias[None, :],
        output_adapter_left.reshape(HEAD, -1), down_adapter_left, output_weight.reshape(HEAD, width), down_weight,
        output_adapter_right,
    )


def solution(mesh):
    in_specs = (
        P(("req", "mlp"), None), P(), P(), P(None, "mlp", None), P("mlp", None, None), P(None, "mlp"), P("mlp"),
        P("mlp", None), P(), P(None, "mlp"), P(None, "mlp", None), P(None, "mlp"), P("mlp", None, None),
        P("mlp", None), P("mlp", None), P(), P(), P("mlp"),
    )
    return jax.shard_map(
        per_device, mesh=mesh, in_specs=in_specs, out_specs=P(("req", "mlp"), None), check_vma=False
    )
```

```python
import math

import jax
import jax.numpy as jnp
from jax import lax
from jax.experimental import pallas as pl
from jax.experimental.pallas import tpu as pltpu
from jax.sharding import PartitionSpec as P

HEAD = 256
ROT = 64
RANK = 16
EPSILON = 1e-05
NEGATIVE_FILL = -1e30
MESH = pl.DeviceIdType.MESH
F32 = jnp.float32
BF16 = jnp.bfloat16
VMEM_LIMIT = 60 * 1024 * 1024
SIDE = 4
GROUP = 16
UNIT = 16
QKV = 3 * HEAD
CUT = 6
PLACES = (0, 3, 1, 2)


def dot(a, b):
    return jnp.dot(a, b, preferred_element_type=F32)


class Plane:
    def __init__(self):
        self.me = lax.axis_index("mlp")
        self.z = self.me // SIDE
        self.y = self.me % SIDE

    def at(self, dz, dy):
        return ((self.z + dz + SIDE) % SIDE) * SIDE + (self.y + dy + SIDE) % SIDE

    def off(self, half, d1, d2):
        return self.at(d1, d2) if half == 0 else self.at(d2, d1)

    def source(self, half, d1, d2):
        return self.off(half, -d1, -d2)


def barrier_all(me, count):
    sem = pltpu.get_barrier_semaphore()
    for k in range(1, count):
        pl.semaphore_signal(sem, inc=1, device_id={"mlp": (me + k) % count}, device_id_type=MESH)
    return sem


def exchange_start(me, packed, landed, sems):
    def scatter(k, carry):
        to = (me + k) % GROUP
        pltpu.make_async_remote_copy(
            packed.at[to], landed.at[me], sems.at[0], sems.at[1], device_id={"mlp": to}, device_id_type=MESH
        ).start()
        return carry

    lax.fori_loop(1, GROUP, scatter, 0)
    landed[me] = packed[me]


def exchange_middle(me, landed, full, sems):
    many = landed.at[pl.ds(0, GROUP - 1)]
    pltpu.make_async_copy(many, many, sems.at[1]).wait()
    full[me] = jnp.sum(landed[...].astype(F32), axis=0).astype(BF16)

    def gather(k, carry):
        to = (me + k) % GROUP
        pltpu.make_async_remote_copy(
            full.at[me], full.at[me], sems.at[2], sems.at[3], device_id={"mlp": to}, device_id_type=MESH
        ).start()
        return carry

    lax.fori_loop(1, GROUP, gather, 0)


def exchange_end(landed, sems):
    many = landed.at[pl.ds(0, GROUP - 1)]
    for number in (3, 0, 2):
        pltpu.make_async_copy(many, many, sems.at[number]).wait()


EARLY = tuple((h, d1, 0) for h in (0, 1) for d1 in (0, 1, -1, 2)) + tuple(
    (h, d1, d2) for h in (0, 1) for d1 in (0, 1) for d2 in (1, -1)
)
LATE = tuple((h, d1, d2) for h in (0, 1) for d1 in (-1, 2) for d2 in (1, -1)) + tuple(
    (h, d1, 2) for h in (0, 1) for d1 in (0, 1, -1, 2)
)


def front_kernel(
    tokens, gain, bias, in_bias, table, slots, w_qkv, w_up, w_left, w_qkv_right, w_up_right,
    out_attended, out_hidden, adapter,
    xs, weights, right_qkv, right_up, rows_in, acc, picked, packed, landed, full,
    starts, cosine, sine, queries, window, passing, top, total, summed,
    load_sems, send_sem, recv_sems, ex_sems, near_send, near_recv,
):
    plane = Plane()
    me = plane.me
    req = lax.axis_index("req")
    chip, core = req // 2, req % 2
    ahead = ((chip + 1) % SIDE) * 2 + core
    behind = ((chip + 3) % SIDE) * 2 + core
    other = chip * 2 + 1 - core
    hid = w_up.shape[1]
    count = GROUP * 64
    loads = [
        pltpu.make_async_copy(w_qkv, weights.at[:, pl.ds(0, QKV)], load_sems.at[0]),
        pltpu.make_async_copy(w_up, weights.at[:, pl.ds(QKV, hid)], load_sems.at[1]),
        pltpu.make_async_copy(w_left, weights.at[:, pl.ds(QKV + hid, 128)], load_sems.at[2]),
        pltpu.make_async_copy(w_qkv_right, right_qkv, load_sems.at[3]),
        pltpu.make_async_copy(w_up_right, right_up, load_sems.at[4]),
    ]
    for load in loads:
        load.start()
    sem = barrier_all(me, GROUP)
    for device in (ahead, behind, other):
        pl.semaphore_signal(sem, inc=1, device_id={"req": device}, device_id_type=MESH)
    for part in range(0, 64, 16):
        values = tokens[part : part + 16, :].astype(F32)
        center = values - jnp.mean(values, axis=1, keepdims=True)
        spread = jnp.mean(center * center, axis=1, keepdims=True)
        scaled = center * lax.rsqrt(spread + EPSILON)
        xs[me, part : part + 16, :] = (scaled * gain[...] + bias[...]).astype(BF16)
    pl.semaphore_wait(sem, GROUP + 2)

    def unit_of(half, chunk):
        return chunk if half == 0 else 1 - chunk

    def far_way(half, chunk):
        return 1 if unit_of(half, chunk) == 0 else -1

    def rows_of(half, chunk):
        return pl.ds(half * 32 + unit_of(half, chunk) * UNIT, UNIT)

    def send(slot, half, chunk, axis, step):
        view = xs.at[slot, rows_of(half, chunk), :]
        to = plane.off(half, step, 0) if axis == 1 else plane.off(half, 0, step)
        pltpu.make_async_remote_copy(
            view, view, send_sem, recv_sems.at[slot, half * 2 + unit_of(half, chunk)],
            device_id={"mlp": to}, device_id_type=MESH,
        ).start()

    def arrive(half, chunk, d1, d2):
        slot = plane.source(half, d1, d2)
        view = xs.at[slot, rows_of(half, chunk), :]
        pltpu.make_async_copy(view, view, recv_sems.at[slot, half * 2 + unit_of(half, chunk)]).wait()
        return slot

    def own_sends(chunk, ways):
        for axis in (1, 2):
            for half in (0, 1):
                along_z = (half == 0) == (axis == 1)
                for step in (1, -1):
                    if (along_z, step) in ways:
                        send(me, half, chunk, axis, step)

    def first_hop(chunk):
        for d1 in (1, -1):
            for half in (0, 1):
                slot = arrive(half, chunk, d1, 0)
                for step in (1, -1):
                    send(slot, half, chunk, 2, step)
                if d1 == far_way(half, chunk):
                    send(slot, half, chunk, 1, d1)

    def relay(chunk, d1):
        for half in (0, 1):
            way = far_way(half, chunk)
            send(arrive(half, chunk, d1, way), half, chunk, 2, way)

    def far(chunk):
        for half in (0, 1):
            slot = arrive(half, chunk, 2, 0)
            for step in (1, -1):
                send(slot, half, chunk, 2, step)

    def rest_early(chunk):
        for d1 in (0, 1):
            for half in (0, 1):
                arrive(half, chunk, d1, -far_way(half, chunk))

    def rest_late(chunk):
        for d1 in (-1, 2):
            for half in (0, 1):
                arrive(half, chunk, d1, -far_way(half, chunk))
        for d1 in (0, 1, -1, 2):
            for half in (0, 1):
                arrive(half, chunk, d1, 2)

    light, heavy = ((True, 1), (False, -1)), ((True, -1), (False, 1))
    own_sends(0, light + heavy)

    long = table[0:1, :].astype(F32)
    requests = long.shape[1]
    before = lax.broadcasted_iota(jnp.int32, (requests, requests), 0) < lax.broadcasted_iota(
        jnp.int32, (requests, requests), 1
    )
    begins = dot(jnp.broadcast_to(long, (8, requests)).astype(BF16), before.astype(F32).astype(BF16))[:1, :]
    ends = begins + long
    ids = table[1:2, :].astype(F32)

    def locate(block, carry):
        rows = lax.broadcasted_iota(jnp.int32, (64, 1), 0)
        index = (req * count + block * 64 + rows).astype(F32)
        inside = jnp.logical_and(begins <= index, index < ends)
        start = jnp.sum(jnp.where(inside, begins, 0.0), axis=1, keepdims=True)
        mine = jnp.sum(jnp.where(inside, ids, 0.0), axis=1, keepdims=True)
        starts[block] = start.reshape(4, UNIT, 1)
        adapter[block] = mine.reshape(4, UNIT, 1)
        return carry

    lax.fori_loop(0, GROUP, locate, 0)

    first_hop(0)
    relay(0, 0)
    far(0)
    own_sends(1, light)
    relay(0, 1)
    relay(0, -1)
    own_sends(1, heavy)

    lane = lax.broadcasted_iota(jnp.int32, (1, 128), 1)
    even = lane % 2 == 0
    frequency = jnp.exp((lane // 2).astype(F32) * (-2.0 * math.log(10000.0) / ROT))

    def angles(block, carry):
        rows = lax.broadcasted_iota(jnp.int32, (64, 1), 0)
        index = (req * count + block * 64 + rows).astype(F32)
        angle = (index - starts[block].reshape(64, 1)) * frequency
        turned = lane < ROT
        cosine[block] = jnp.where(turned, jnp.cos(angle), 1.0).reshape(4, UNIT, 128)
        sine[block] = jnp.where(turned, jnp.where(even, -1.0, 1.0) * jnp.sin(angle), 0.0).reshape(4, UNIT, 128)
        return carry

    def multiply(chunk, pieces):
        for i, (half, d1, d2) in enumerate(pieces):
            slot = plane.source(half, d1, d2)
            rows_in[i * UNIT : (i + 1) * UNIT, :] = xs[slot, rows_of(half, chunk), :]
        left = dot(rows_in[...], weights[:, QKV + hid :])
        for i, (half, d1, d2) in enumerate(pieces):
            unit = half * 2 + unit_of(half, chunk)
            picked[plane.source(half, d1, d2), unit] = left[i * UNIT : (i + 1) * UNIT, :].astype(BF16)

    def multiply_wide(chunk, pieces, begin, end):
        def column(n, carry):
            columns = pl.ds(pl.multiple_of(n * 256, 256), 256)
            result = dot(rows_in[...], weights[:, columns])
            for i, (half, d1, d2) in enumerate(pieces):
                unit = half * 2 + unit_of(half, chunk)
                acc[plane.source(half, d1, d2), unit, :, columns] = result[i * UNIT : (i + 1) * UNIT, :]
            return carry

        lax.fori_loop(begin, end, column, 0)

    chosen = jnp.where(lane < 32, slots[0], jnp.where(lane < 64, slots[1], jnp.where(lane < 96, slots[2], slots[3])))
    chosen = chosen.astype(F32)

    def pack(chunk):
        row_id = lax.broadcasted_iota(jnp.int32, (128, 128), 0)
        col_id = lax.broadcasted_iota(jnp.int32, (128, 128), 1)
        together = jnp.zeros((256, 128), F32)
        for unit in PLACES[chunk * 2 : chunk * 2 + 2]:
            mine = adapter[:, unit].reshape(256, 1) == chosen
            kept = jnp.where(mine, picked[:, unit].reshape(256, 128).astype(F32), 0.0).astype(BF16)
            fold = jnp.logical_and(col_id // 32 == unit, row_id % 32 == col_id % 32).astype(F32).astype(BF16)
            together = together + dot(kept, fold)
        packed[chunk] = together.astype(BF16).reshape(GROUP, UNIT, 128)
        exchange_start(me, packed.at[chunk], landed.at[chunk], ex_sems.at[chunk])

    def middle(chunk):
        exchange_middle(me, landed.at[chunk], full.at[chunk], ex_sems.at[chunk])

    wide_lane = lax.broadcasted_iota(jnp.int32, (1, 1024), 1)
    owner = (wide_lane // RANK).astype(F32)
    row_id = lax.broadcasted_iota(jnp.int32, (128, 1024), 0)
    col_id = lax.broadcasted_iota(jnp.int32, (128, 1024), 1)

    def widened(chunk, unit, first):
        spread = (row_id == unit * 32 + first + col_id % RANK).astype(F32).astype(BF16)
        mine = adapter[:, unit].reshape(256, 1) == owner
        return jnp.where(mine, dot(full[chunk].reshape(256, 128), spread), 0.0).astype(BF16)

    def finish_heads(place):
        unit = PLACES[place]
        wide = widened(place // 2, unit, 0)
        turn = cosine[:, unit].reshape(256, 128)
        sway = sine[:, unit].reshape(256, 128)
        for part in range(3):
            columns = slice(part * HEAD, (part + 1) * HEAD)
            value = acc[:, unit, :, columns].reshape(256, HEAD) + dot(wide, right_qkv[:, columns])
            if part < 2:
                head = value[:, :128]
                swapped = jnp.where(even, pltpu.roll(head, 127, 1), pltpu.roll(head, 1, 1))
                value = jnp.concatenate([head * turn + swapped * sway, value[:, 128:]], axis=1)
            value = value.astype(BF16)
            if part == 0:
                queries[:, unit] = (value * jnp.asarray(HEAD ** (-0.5), BF16)).reshape(GROUP, UNIT, HEAD)
            else:
                window[0, place, :, :, (part - 1) * HEAD : part * HEAD] = value.reshape(GROUP, UNIT, HEAD)

    def finish_hidden(place):
        unit = PLACES[place]
        wide = widened(place // 2, unit, RANK)
        for part in range(hid // 256):
            columns = slice(part * 256, (part + 1) * 256)
            value = acc[:, unit, :, QKV + part * 256 : QKV + (part + 1) * 256].reshape(256, 256)
            value = value + dot(wide, right_up[:, columns]) + in_bias[:, columns]
            value = jax.nn.gelu(value, approximate=True)
            out_hidden[:, unit, :, columns] = value.astype(BF16).reshape(GROUP, UNIT, 256)

    low, high = pl.ds(0, CUT), pl.ds(CUT, GROUP - CUT)
    started = []

    def pass_on(src, dst, number, device):
        copy = pltpu.make_async_remote_copy(
            src, dst, near_send.at[number], near_recv.at[number], device_id={"req": device}, device_id_type=MESH
        )
        copy.start()
        started.append(copy)

    def take(ref, number):
        pltpu.make_async_copy(ref, ref, near_recv.at[number]).wait()

    def part_of(slot, chunk, blocks=None):
        if blocks is None:
            return window.at[slot, pl.ds(2 * chunk, 2)]
        return window.at[slot, pl.ds(2 * chunk, 2), blocks]

    def near_sends(chunk):
        at = 10 * chunk
        pass_on(part_of(0, chunk, low), part_of(2, chunk, low), at, ahead)
        pass_on(part_of(0, chunk, high), passing.at[chunk], at + 2, behind)
        pass_on(part_of(0, chunk, high), part_of(2, chunk, high), at + 1, ahead)
        pass_on(part_of(0, chunk), part_of(1 + 4 * core, chunk), at + 3, other)

    def near_low(chunk):
        at = 10 * chunk
        take(part_of(2, chunk, low), at)
        pass_on(part_of(2, chunk, low), part_of(4, chunk, low), at + 6, ahead)
        pass_on(part_of(2, chunk, low), part_of(3 - 2 * core, chunk, low), at + 4, other)

    def near_passing(chunk):
        at = 10 * chunk
        take(passing.at[chunk], at + 2)
        pass_on(passing.at[chunk], part_of(4, chunk, high), at + 7, behind)

    def near_high(chunk):
        at = 10 * chunk
        take(part_of(2, chunk, high), at + 1)
        pass_on(part_of(2, chunk, high), part_of(3 - 2 * core, chunk, high), at + 5, other)

    def next_high(chunk):
        at = 10 * chunk
        take(part_of(4, chunk, high), at + 7)
        pass_on(part_of(4, chunk, high), part_of(5 - 2 * core, chunk, high), at + 9, other)

    def next_low(chunk):
        at = 10 * chunk
        take(part_of(4, chunk, low), at + 6)
        pass_on(part_of(4, chunk, low), part_of(5 - 2 * core, chunk, low), at + 8, other)

    def attend(slot, p0, p1, blocks, b, causal):
        many = (p1 - p0) * blocks * UNIT
        keys = window[slot, p0:p1, :blocks, :, :HEAD].reshape(many, HEAD)
        values = window[slot, p0:p1, :blocks, :, HEAD:].reshape(many, HEAD)
        four = pl.ds(b * 4, 4)
        scores = lax.dot_general(
            queries[four].reshape(256, HEAD), keys, (((1,), (1,)), ((), ())), preferred_element_type=F32
        )
        index = lax.broadcasted_iota(jnp.int32, (1, many), 1)
        place = index // (blocks * UNIT) + p0
        unit = jnp.where(place == 0, 0, jnp.where(place == 1, 3, place - 1))
        key_id = ((index // UNIT) % blocks) * 64 + unit * UNIT + index % UNIT + (req - slot) * count
        allowed = key_id.astype(F32) >= starts[four].reshape(256, 1)
        if causal:
            row = lax.broadcasted_iota(jnp.int32, (256, 1), 0) + req * count + b * 256
            allowed = jnp.logical_and(allowed, key_id <= row)
        scores = jnp.where(allowed, scores, NEGATIVE_FILL)
        peak = jnp.max(scores, axis=1, keepdims=True)
        if causal:
            kept = jnp.exp(scores - peak)
            top[b] = peak
            total[b] = jnp.sum(kept, axis=1, keepdims=True)
            summed[b] = dot(kept.astype(BF16), values)
        else:
            old = top[b]
            peak = jnp.maximum(old, peak)
            kept = jnp.exp(scores - peak)
            decay = jnp.exp(old - peak)
            top[b] = peak
            total[b] = total[b] * decay + jnp.sum(kept, axis=1, keepdims=True)
            summed[b] = summed[b] * decay + dot(kept.astype(BF16), values)

    def attend_all(slot, chunk):
        def body(b, carry):
            attend(slot, 2 * chunk, 2 * chunk + 2, GROUP, b, False)
            return carry

        lax.fori_loop(0, 4, body, 0)

    def attend_on(which, slot, chunk):
        @pl.when(core == which)
        def _():
            attend_all(slot, chunk)

    tiles = (QKV + hid) // 256
    lax.fori_loop(0, GROUP // 2, angles, 0)
    for load in loads[:3]:
        load.wait()
    rest_early(0)
    multiply(0, EARLY)
    multiply_wide(0, EARLY, 0, tiles)
    relay(0, 2)
    first_hop(1)
    lax.fori_loop(GROUP // 2, GROUP, angles, 0)
    rest_late(0)
    multiply(0, LATE)
    pack(0)
    relay(1, 0)
    multiply_wide(0, LATE, 0, 2)
    far(1)
    middle(0)
    multiply_wide(0, LATE, 2, tiles)
    for load in loads[3:]:
        load.wait()
    relay(1, 1)
    exchange_end(landed.at[0], ex_sems.at[0])
    finish_heads(0)
    finish_heads(1)
    near_sends(0)
    relay(1, -1)
    rest_early(1)
    multiply(1, EARLY)
    multiply_wide(1, EARLY, 0, tiles)
    relay(1, 2)
    near_low(0)
    near_passing(0)
    rest_late(1)
    multiply(1, LATE)
    pack(1)
    multiply_wide(1, LATE, 0, 2)
    middle(1)
    near_high(0)
    multiply_wide(1, LATE, 2, tiles)
    exchange_end(landed.at[1], ex_sems.at[1])
    finish_heads(2)
    finish_heads(3)
    near_sends(1)
    next_high(0)
    for b in range(4):
        attend(0, 0, 4, (b + 1) * 4, b, True)
    next_low(0)
    take(part_of(5 - 4 * core, 0), 3)
    attend_on(1, 1, 0)
    attend_all(2, 0)
    near_low(1)
    take(part_of(1 + 2 * core, 0, low), 4)
    take(part_of(1 + 2 * core, 0, high), 5)
    attend_all(1 + 2 * core, 0)
    near_passing(1)
    attend_all(4, 0)
    take(part_of(3 + 2 * core, 0, low), 8)
    take(part_of(3 + 2 * core, 0, high), 9)
    attend_on(0, 3, 0)
    for place in range(4):
        finish_hidden(place)
    take(part_of(5 - 4 * core, 1), 13)
    attend_on(1, 1, 1)
    near_high(1)
    attend_all(2, 1)
    take(part_of(1 + 2 * core, 1, low), 14)
    take(part_of(1 + 2 * core, 1, high), 15)
    attend_all(1 + 2 * core, 1)
    next_high(1)
    next_low(1)
    attend_all(4, 1)
    take(part_of(3 + 2 * core, 1, high), 19)
    take(part_of(3 + 2 * core, 1, low), 18)
    attend_on(0, 3, 1)

    for b in range(4):
        out_attended[b * 4 : (b + 1) * 4] = (summed[b] / total[b]).astype(BF16).reshape(4, 4, UNIT, HEAD)
    for copy in started:
        copy.wait_send()
    sent = xs.at[pl.ds(0, GROUP - 1)]
    pltpu.make_async_copy(sent, sent, send_sem).wait()


REDUCE_GROUPS = (
    tuple((h, d1, 2) for h in (0, 1) for d1 in (2, 1, -1, 0)),
    tuple((h, d1, d2) for h in (0, 1) for d1 in (2, 1) for d2 in (1, -1)),
    tuple((h, d1, d2) for h in (0, 1) for d1 in (-1, 0) for d2 in (1, -1)),
    tuple((h, d1, 0) for h in (0, 1) for d1 in (2, 1, -1, 0)),
)
FAR = {2: 0, 1: 1, -1: 2, 0: 3}


def output_kernel(
    attended, hidden, adapter, tokens, out_bias, w_left_attn, w_left_hid, w_attn, w_down, w_right,
    out,
    inputs, left, weights, part, from2, from1, rows_in, packed, landed, full,
    load_sems, send_sem, sems2, sems1, ex_sems,
):
    plane = Plane()
    me = plane.me
    hid = w_left_hid.shape[0]
    depth = HEAD + hid
    loads = [
        pltpu.make_async_copy(attended, inputs.at[:, :, :, pl.ds(0, HEAD)], load_sems.at[0]),
        pltpu.make_async_copy(hidden, inputs.at[:, :, :, pl.ds(HEAD, hid)], load_sems.at[1]),
        pltpu.make_async_copy(w_left_attn, left.at[pl.ds(0, HEAD)], load_sems.at[2]),
        pltpu.make_async_copy(w_left_hid, left.at[pl.ds(HEAD, hid)], load_sems.at[3]),
        pltpu.make_async_copy(w_attn, weights.at[pl.ds(0, HEAD)], load_sems.at[4]),
        pltpu.make_async_copy(w_down, weights.at[pl.ds(HEAD, hid)], load_sems.at[5]),
        pltpu.make_async_copy(w_right, weights.at[pl.ds(depth, 128)], load_sems.at[6]),
    ]
    for load in loads:
        load.start()
    sem = barrier_all(me, GROUP)
    for load in loads[:4]:
        load.wait()

    lane = lax.broadcasted_iota(jnp.int32, (1, 1024), 1)
    fold_row = lax.broadcasted_iota(jnp.int32, (1024, 128), 0)
    fold_col = lax.broadcasted_iota(jnp.int32, (1024, 128), 1)

    def lower(unit, together):
        mine = adapter[:, unit].reshape(256, 1) == (lane // RANK).astype(F32)
        for first, begin, end in ((0, 0, HEAD), (RANK, HEAD, depth)):
            product = dot(inputs[:, unit, :, begin:end].reshape(256, end - begin), left[begin:end, :])
            kept = jnp.where(mine, product, 0.0).astype(BF16)
            fold = (fold_col == unit * 32 + first + fold_row % RANK).astype(F32).astype(BF16)
            together = together + dot(kept, fold)
        return together

    together = lax.fori_loop(0, 4, lower, jnp.zeros((256, 128), F32))
    packed[...] = together.astype(BF16).reshape(GROUP, UNIT, 128)
    pl.semaphore_wait(sem, GROUP - 1)
    exchange_start(me, packed, landed, ex_sems)
    exchange_middle(me, landed, full, ex_sems)
    for load in loads[4:]:
        load.wait()
    exchange_end(landed, ex_sems)
    lane = lax.broadcasted_iota(jnp.int32, (1, 128), 1)
    row_id = lax.broadcasted_iota(jnp.int32, (128, 128), 0)
    col_id = lax.broadcasted_iota(jnp.int32, (128, 128), 1)
    for unit in range(4):
        mine = adapter[:, unit].reshape(256, 1) == (me * 4 + lane // 32).astype(F32)
        spread = (row_id == unit * 32 + col_id % 32).astype(F32).astype(BF16)
        wide = jnp.where(mine, dot(full[...].reshape(256, 128), spread), 0.0).astype(BF16)
        inputs[:, unit, :, depth:] = wide.reshape(GROUP, UNIT, 128)

    def multiply(number):
        for i, (half, d1, d2) in enumerate(REDUCE_GROUPS[number]):
            slot = plane.source(half, d1, d2)
            for u in (0, 1):
                at = i * 32 + u * UNIT
                rows_in[at : at + UNIT, :] = inputs[slot, half * 2 + u]

        def column(n, carry):
            columns = pl.ds(pl.multiple_of(n * 256, 256), 256)
            result = dot(rows_in[...], weights[:, columns]).astype(BF16)
            for i, (half, d1, d2) in enumerate(REDUCE_GROUPS[number]):
                slot = plane.source(half, d1, d2)
                part[slot, pl.ds(half * 32, 32), columns] = result[i * 32 : (i + 1) * 32, :]
            return carry

        lax.fori_loop(0, out.shape[1] // 256, column, 0)

    def rows_of(half, u):
        return pl.ds(half * 32 + u * UNIT, UNIT)

    def landing(half, axis, side, d1, place):
        index = half * 2 + side
        if axis == 2:
            return from2.at[index, FAR[d1], place], sems2.at[index, FAR[d1] * 3 + place]
        return from1.at[index, place], sems1.at[index, place]

    def send(half, d1, d2, u, axis):
        d = d2 if axis == 2 else d1
        back = d if d != 2 else (1 if u == 0 else -1)
        side = 0 if back == 1 else 1
        place = 2 if d == 2 else u
        slot = plane.source(half, d1, d2)
        to = plane.off(half, 0, -back) if axis == 2 else plane.off(half, -back, 0)
        target, arrived = landing(half, axis, side, d1, place)
        pltpu.make_async_remote_copy(
            part.at[slot, rows_of(half, u), :], target, send_sem, arrived, device_id={"mlp": to}, device_id_type=MESH
        ).start()

    def arrive(half, axis, side, d1, place):
        ref, arrived = landing(half, axis, side, d1, place)
        pltpu.make_async_copy(ref, ref, arrived).wait()
        return ref

    def add(half, d1, d2, u, children):
        refs = [arrive(half, axis, side, d1, place) for axis, side, place in children]
        slot = plane.source(half, d1, d2)
        here = part.at[slot, rows_of(half, u), :]
        value = here[...].astype(F32)
        for ref in refs:
            value = value + ref[...].astype(F32)
        here[...] = value.astype(BF16)

    multiply(0)
    for d1 in (2, 1, -1, 0):
        for half in (0, 1):
            for u in (0, 1):
                send(half, d1, 2, u, 2)
    for number in (1, 2):
        multiply(number)
        for half, d1, d2 in REDUCE_GROUPS[number]:
            send(half, d1, d2, 1 if d2 == 1 else 0, 2)
    for number in (1, 2):
        for half, d1, d2 in REDUCE_GROUPS[number]:
            u = 0 if d2 == 1 else 1
            add(half, d1, d2, u, ((2, 0 if d2 == 1 else 1, 2),))
            send(half, d1, d2, u, 2)
    multiply(3)
    both = lambda u: ((2, 0, u), (2, 1, u))
    for half in (0, 1):
        for u in (0, 1):
            add(half, 2, 0, u, both(u))
            send(half, 2, 0, u, 1)
    for d1 in (1, -1):
        for half in (0, 1):
            u = 1 if d1 == 1 else 0
            add(half, d1, 0, u, both(u))
            send(half, d1, 0, u, 1)
    for d1 in (1, -1):
        for half in (0, 1):
            u = 0 if d1 == 1 else 1
            add(half, d1, 0, u, both(u) + ((1, 0 if d1 == 1 else 1, 2),))
            send(half, d1, 0, u, 1)
    for half in (0, 1):
        for u in (0, 1):
            refs = [arrive(half, axis, side, 0, place) for axis, side, place in both(u) + ((1, 0, u), (1, 1, u))]
            rows = rows_of(half, u)
            value = part[me, rows, :].astype(F32)
            for ref in refs:
                value = value + ref[...].astype(F32)
            out[rows, :] = (value + tokens[rows, :].astype(F32) + out_bias[...]).astype(BF16)
    sent = part.at[pl.ds(0, GROUP - 1)]
    pltpu.make_async_copy(sent, sent, send_sem).wait()


def per_device(
    tokens, layer_norm_gain, layer_norm_bias, query_key_weight, output_weight, up_weight, input_bias, down_weight,
    output_bias, input_adapter_left, query_key_value_right, up_adapter_right, output_adapter_left, down_adapter_left,
    output_adapter_right, lengths, request_adapter, slot_adapter,
):
    rows, width = tokens.shape
    hid = up_weight.shape[1]
    vmem = pl.BlockSpec(memory_space=pltpu.VMEM)
    smem = pl.BlockSpec(memory_space=pltpu.SMEM)
    anywhere = pl.BlockSpec(memory_space=pl.ANY)
    dma = pltpu.SemaphoreType.DMA
    by_unit = (GROUP, 4, UNIT)
    attended, hidden, adapter = pl.pallas_call(
        front_kernel,
        out_shape=(
            jax.ShapeDtypeStruct(by_unit + (HEAD,), BF16),
            jax.ShapeDtypeStruct(by_unit + (hid,), BF16),
            jax.ShapeDtypeStruct(by_unit + (1,), F32),
        ),
        in_specs=[vmem] * 5 + [smem] + [anywhere] * 5,
        out_specs=(vmem, vmem, vmem),
        scratch_shapes=[
            pltpu.VMEM((GROUP, rows, width), BF16),
            pltpu.VMEM((width, QKV + hid + 128), BF16),
            pltpu.VMEM(query_key_value_right.shape[:1] + (QKV,), BF16),
            pltpu.VMEM(up_adapter_right.shape, BF16),
            pltpu.VMEM((256, width), BF16),
            pltpu.VMEM(by_unit + (QKV + hid,), F32),
            pltpu.VMEM(by_unit + (128,), BF16),
            pltpu.VMEM((2, GROUP, UNIT, 128), BF16),
            pltpu.VMEM((2, GROUP, UNIT, 128), BF16),
            pltpu.VMEM((2, GROUP, UNIT, 128), BF16),
            pltpu.VMEM(by_unit + (1,), F32),
            pltpu.VMEM(by_unit + (128,), F32),
            pltpu.VMEM(by_unit + (128,), F32),
            pltpu.VMEM(by_unit + (HEAD,), BF16),
            pltpu.VMEM((6, 4, GROUP, UNIT, 2 * HEAD), BF16),
            pltpu.VMEM((2, 2, GROUP - CUT, UNIT, 2 * HEAD), BF16),
            pltpu.VMEM((4, 256, 1), F32),
            pltpu.VMEM((4, 256, 1), F32),
            pltpu.VMEM((4, 256, HEAD), F32),
            dma((5,)),
            dma,
            dma((GROUP, 4)),
            dma((2, 4)),
            dma((20,)),
            dma((20,)),
        ],
        compiler_params=pltpu.CompilerParams(
            collective_id=0, has_side_effects=True, vmem_limit_bytes=VMEM_LIMIT
        ),
        name="front_stage",
    )(
        tokens, layer_norm_gain[None, :], layer_norm_bias[None, :], input_bias[None, :],
        jnp.stack([lengths, request_adapter]), slot_adapter,
        query_key_weight.reshape(width, QKV), up_weight, input_adapter_left,
        query_key_value_right.reshape(-1, QKV), up_adapter_right,
    )

    depth = HEAD + hid + 128
    return pl.pallas_call(
        output_kernel,
        out_shape=jax.ShapeDtypeStruct((rows, width), BF16),
        in_specs=[anywhere] * 2 + [vmem] * 3 + [anywhere] * 5,
        out_specs=vmem,
        scratch_shapes=[
            pltpu.VMEM(by_unit + (depth,), BF16),
            pltpu.VMEM((HEAD + hid, 1024), BF16),
            pltpu.VMEM((depth, width), BF16),
            pltpu.VMEM((GROUP, rows, width), BF16),
            pltpu.VMEM((4, 4, 3, UNIT, width), BF16),
            pltpu.VMEM((4, 3, UNIT, width), BF16),
            pltpu.VMEM((256, depth), BF16),
            pltpu.VMEM((GROUP, UNIT, 128), BF16),
            pltpu.VMEM((GROUP, UNIT, 128), BF16),
            pltpu.VMEM((GROUP, UNIT, 128), BF16),
            dma((7,)),
            dma,
            dma((4, 12)),
            dma((4, 3)),
            dma((4,)),
        ],
        compiler_params=pltpu.CompilerParams(
            collective_id=1, has_side_effects=True, vmem_limit_bytes=VMEM_LIMIT
        ),
        name="output_stage",
    )(
        attended, hidden, adapter, tokens, output_bias[None, :],
        output_adapter_left.reshape(HEAD, -1), down_adapter_left, output_weight.reshape(HEAD, width), down_weight,
        output_adapter_right,
    )


def solution(mesh):
    in_specs = (
        P(("req", "mlp"), None), P(), P(), P(None, "mlp", None), P("mlp", None, None), P(None, "mlp"), P("mlp"),
        P("mlp", None), P(), P(None, "mlp"), P(None, "mlp", None), P(None, "mlp"), P("mlp", None, None),
        P("mlp", None), P("mlp", None), P(), P(), P("mlp"),
    )
    return jax.shard_map(
        per_device, mesh=mesh, in_specs=in_specs, out_specs=P(("req", "mlp"), None), check_vma=False
    )
```

```python
import math

import jax
import jax.numpy as jnp
from jax import lax
from jax.experimental import pallas as pl
from jax.experimental.pallas import tpu as pltpu
from jax.sharding import PartitionSpec as P

HEAD = 256
ROT = 64
RANK = 16
EPSILON = 1e-05
NEGATIVE_FILL = -1e30
MESH = pl.DeviceIdType.MESH
F32 = jnp.float32
BF16 = jnp.bfloat16
VMEM_LIMIT = 60 * 1024 * 1024
SIDE = 4
GROUP = 16
UNIT = 16
QKV = 3 * HEAD
CUT = 96
LATE = 128


def dot(a, b):
    return jnp.dot(a, b, preferred_element_type=F32)


class Plane:
    def __init__(self):
        self.me = lax.axis_index("mlp")
        self.z = self.me // SIDE
        self.y = self.me % SIDE

    def at(self, dz, dy):
        return ((self.z + dz + SIDE) % SIDE) * SIDE + (self.y + dy + SIDE) % SIDE

    def off(self, half, d1, d2):
        return self.at(d1, d2) if half == 0 else self.at(d2, d1)

    def source(self, half, d1, d2):
        return self.off(half, -d1, -d2)


def barrier_all(me, count):
    sem = pltpu.get_barrier_semaphore()
    for k in range(1, count):
        pl.semaphore_signal(sem, inc=1, device_id={"mlp": (me + k) % count}, device_id_type=MESH)
    return sem


def exchange_start(me, packed, landed, sems):
    def scatter(k, carry):
        to = (me + k) % GROUP
        pltpu.make_async_remote_copy(
            packed.at[to], landed.at[me], sems.at[0], sems.at[1], device_id={"mlp": to}, device_id_type=MESH
        ).start()
        return carry

    lax.fori_loop(1, GROUP, scatter, 0)
    landed[me] = packed[me]


def exchange_middle(me, landed, full, sems):
    many = landed.at[pl.ds(0, GROUP - 1)]
    pltpu.make_async_copy(many, many, sems.at[1]).wait()
    full[me] = jnp.sum(landed[...].astype(F32), axis=0).astype(BF16)

    def gather(k, carry):
        to = (me + k) % GROUP
        pltpu.make_async_remote_copy(
            full.at[me], full.at[me], sems.at[2], sems.at[3], device_id={"mlp": to}, device_id_type=MESH
        ).start()
        return carry

    lax.fori_loop(1, GROUP, gather, 0)


def exchange_end(landed, sems):
    many = landed.at[pl.ds(0, GROUP - 1)]
    for number in (3, 0, 2):
        pltpu.make_async_copy(many, many, sems.at[number]).wait()


GATHER_GROUPS = (
    tuple((h, d1, 0) for h in (0, 1) for d1 in (0, 1, -1, 2)),
    tuple((h, d1, d2) for h in (0, 1) for d1 in (0, 1) for d2 in (1, -1)),
    tuple((h, d1, d2) for h in (0, 1) for d1 in (-1, 2) for d2 in (1, -1)),
    tuple((h, d1, 2) for h in (0, 1) for d1 in (0, 1, -1, 2)),
)


def front_kernel(
    tokens, gain, bias, in_bias, table, slots, w_qkv, w_up, w_left, w_qkv_right, w_up_right,
    out_attended, out_hidden, adapter,
    xs, weights, right_qkv, right_up, rows_in, acc, picked, packed, landed, full,
    starts, row_index, row_start, row_adapter, names, cosine, sine, ranks, row_ranks, queries,
    early, late, pass_early, pass_late, top, total, summed,
    load_sems, send_sem, recv_sems, ex_sems, near_send, near_recv,
):
    plane = Plane()
    me = plane.me
    req = lax.axis_index("req")
    chip, core = req // 2, req % 2
    ahead = ((chip + 1) % SIDE) * 2 + core
    behind = ((chip + 3) % SIDE) * 2 + core
    other = chip * 2 + 1 - core
    hid = w_up.shape[1]
    count = GROUP * 64
    loads = [
        pltpu.make_async_copy(w_qkv, weights.at[:, pl.ds(0, QKV)], load_sems.at[0]),
        pltpu.make_async_copy(w_up, weights.at[:, pl.ds(QKV, hid)], load_sems.at[1]),
        pltpu.make_async_copy(w_left, weights.at[:, pl.ds(QKV + hid, 128)], load_sems.at[2]),
        pltpu.make_async_copy(w_qkv_right, right_qkv, load_sems.at[3]),
        pltpu.make_async_copy(w_up_right, right_up, load_sems.at[4]),
    ]
    for load in loads:
        load.start()
    sem = barrier_all(me, GROUP)
    for device in (ahead, behind, other):
        pl.semaphore_signal(sem, inc=1, device_id={"req": device}, device_id_type=MESH)
    for part in range(0, 64, 16):
        values = tokens[part : part + 16, :].astype(F32)
        center = values - jnp.mean(values, axis=1, keepdims=True)
        spread = jnp.mean(center * center, axis=1, keepdims=True)
        scaled = center * lax.rsqrt(spread + EPSILON)
        xs[me, part : part + 16, :] = (scaled * gain[...] + bias[...]).astype(BF16)
    pl.semaphore_wait(sem, GROUP + 2)

    def send(slot, half, units, axis, step):
        first, many = units
        rows = pl.ds(half * 32 + first * UNIT, many * UNIT)
        to = plane.off(half, step, 0) if axis == 1 else plane.off(half, 0, step)
        pltpu.make_async_remote_copy(
            xs.at[slot, rows, :], xs.at[slot, rows, :], send_sem, recv_sems.at[slot, half * 2 + first],
            device_id={"mlp": to}, device_id_type=MESH,
        ).start()

    def landed_piece(half, d1, d2, units):
        first, many = units
        slot = plane.source(half, d1, d2)
        rows = pl.ds(half * 32 + first * UNIT, many * UNIT)
        view = xs.at[slot, rows, :]
        pltpu.make_async_copy(view, view, recv_sems.at[slot, half * 2 + first]).wait()
        return slot

    whole = (0, 2)
    for half in (0, 1):
        for step in (1, -1):
            send(me, half, whole, 1, step)
    for half in (0, 1):
        for step in (1, -1):
            send(me, half, whole, 2, step)

    long = table[0:1, :].astype(F32)
    requests = long.shape[1]
    before = lax.broadcasted_iota(jnp.int32, (requests, requests), 0) < lax.broadcasted_iota(
        jnp.int32, (requests, requests), 1
    )
    begins = dot(jnp.broadcast_to(long, (8, requests)).astype(BF16), before.astype(F32).astype(BF16))[:1, :]
    ends = begins + long
    ids = table[1:2, :].astype(F32)

    def locate(block, carry):
        rows = lax.broadcasted_iota(jnp.int32, (64, 1), 0)
        index = (req * count + block * 64 + rows).astype(F32)
        inside = jnp.logical_and(begins <= index, index < ends)
        start = jnp.sum(jnp.where(inside, begins, 0.0), axis=1, keepdims=True)
        mine = jnp.sum(jnp.where(inside, ids, 0.0), axis=1, keepdims=True)
        starts[block] = start.reshape(4, UNIT, 1)
        adapter[block] = mine.reshape(4, UNIT, 1)
        return carry

    lax.fori_loop(0, GROUP, locate, 0)

    def pieces(number):
        return [(i, plane.source(h, d1, d2), h) for i, (h, d1, d2) in enumerate(GATHER_GROUPS[number])]

    piece_row = lax.broadcasted_iota(jnp.int32, (32, 1), 0)
    piece_lane = lax.broadcasted_iota(jnp.int32, (1, 256), 1)
    for number in range(4):
        name = piece_lane
        for i, slot, half in pieces(number):
            at = slice(i * 32, (i + 1) * 32)
            first = slot * 64 + half * 32
            row_index[number, at, :] = (req * count + first + piece_row).astype(F32)
            row_start[number, at, :] = starts[slot, 2 * half : 2 * half + 2].reshape(32, 1)
            row_adapter[number, at, :] = adapter[slot, 2 * half : 2 * half + 2].reshape(32, 1)
            name = jnp.where(piece_lane // 32 == i, first + piece_lane % 32, name)
        names[:, number * 256 : (number + 1) * 256] = name.astype(F32)

    for half in (0, 1):
        for d1 in (1, -1):
            slot = landed_piece(half, d1, 0, whole)
            send(slot, half, (0, 1) if d1 == 1 else (1, 1), 1, d1)
            for step in (1, -1):
                send(slot, half, whole, 2, step)

    def relay(half, d1, d2, pieces):
        for units in pieces:
            slot = landed_piece(half, d1, d2, units)
        send(slot, half, (0, 1) if d2 == 1 else (1, 1), 2, d2)

    lane = lax.broadcasted_iota(jnp.int32, (1, 128), 1)
    even = lane % 2 == 0

    frequency = jnp.exp((lane // 2).astype(F32) * (-2.0 * math.log(10000.0) / ROT))

    def angles(number, carry):
        angle = (row_index[number] - row_start[number]) * frequency
        turned = lane < ROT
        cosine[number] = jnp.where(turned, jnp.cos(angle), 1.0)
        sine[number] = jnp.where(turned, jnp.where(even, -1.0, 1.0) * jnp.sin(angle), 0.0)
        return carry

    chosen = jnp.where(lane < 32, slots[0], jnp.where(lane < 64, slots[1], jnp.where(lane < 96, slots[2], slots[3])))
    chosen = chosen.astype(F32)

    def multiply(number):
        for i, slot, half in pieces(number):
            rows_in[i * 32 : (i + 1) * 32, :] = xs[slot, pl.ds(half * 32, 32), :]
        left = dot(rows_in[...], weights[:, QKV + hid :])
        kept = jnp.where(row_adapter[number] == chosen, left, 0.0).astype(BF16)
        for i, slot, half in pieces(number):
            picked[slot, 2 * half : 2 * half + 2] = kept[i * 32 : (i + 1) * 32, :].reshape(2, UNIT, 128)

    def multiply_wide(number, begin, end):
        def column(n, carry):
            columns = pl.ds(pl.multiple_of(n * 256, 256), 256)
            acc[number, :, columns] = dot(rows_in[...], weights[:, columns])
            return carry

        lax.fori_loop(begin, end, column, 0)

    low, high, every = pl.ds(0, CUT), pl.ds(CUT, 256 - CUT), pl.ds(0, 256)
    started = []

    def view(slot, part, rows=every):
        return early.at[slot, part, rows] if part < 4 else late.at[slot, :, rows]

    def pass_on(src, dst, number, device):
        copy = pltpu.make_async_remote_copy(
            src, dst, near_send.at[number], near_recv.at[number], device_id={"req": device}, device_id_type=MESH
        )
        copy.start()
        started.append(copy)

    def take(ref, number):
        pltpu.make_async_copy(ref, ref, near_recv.at[number]).wait()

    def by_way(part):
        return pass_early.at[part] if part < 4 else pass_late

    def near_sends(part):
        if part < 4:
            early[0, part] = acc[part, :, HEAD:QKV].astype(BF16)
        at = 10 * part
        pass_on(view(0, part, low), view(2, part, low), at, ahead)
        pass_on(view(0, part, high), by_way(part), at + 2, behind)
        pass_on(view(0, part, high), view(2, part, high), at + 1, ahead)
        pass_on(view(0, part), view(1 + 4 * core, part), at + 3, other)

    def near_low(part):
        at = 10 * part
        take(view(2, part, low), at)
        pass_on(view(2, part, low), view(4, part, low), at + 6, ahead)
        pass_on(view(2, part, low), view(3 - 2 * core, part, low), at + 4, other)

    def near_passing(part):
        at = 10 * part
        take(by_way(part), at + 2)
        pass_on(by_way(part), view(4, part, high), at + 7, behind)

    def near_high(part):
        at = 10 * part
        take(view(2, part, high), at + 1)
        pass_on(view(2, part, high), view(3 - 2 * core, part, high), at + 5, other)

    def near_relays(part):
        near_low(part)
        near_passing(part)
        near_high(part)

    def next_relays(part):
        at = 10 * part
        take(view(4, part, high), at + 7)
        pass_on(view(4, part, high), view(5 - 2 * core, part, high), at + 9, other)
        take(view(4, part, low), at + 6)
        pass_on(view(4, part, low), view(5 - 2 * core, part, low), at + 8, other)

    def take_all(slot, first, second=None):
        for part in range(5):
            if second is None:
                take(view(slot, part), 10 * part + first)
            else:
                take(view(slot, part, low), 10 * part + first)
                take(view(slot, part, high), 10 * part + second)

    tiles = (QKV + hid) // 256
    lax.fori_loop(0, 2, angles, 0)
    for half in (0, 1):
        for d2 in (1, -1):
            relay(half, 0, d2, (whole,))
    for half in (0, 1):
        for unit in ((0, 1), (1, 1)):
            slot = landed_piece(half, 2, 0, unit)
            for step in (1, -1):
                send(slot, half, unit, 2, step)
    for load in loads[:3]:
        load.wait()
    multiply(0)
    multiply_wide(0, 0, tiles)
    near_sends(0)
    for half in (0, 1):
        for d1 in (1, -1):
            for d2 in (1, -1):
                relay(half, d1, d2, (whole,))
    multiply(1)
    multiply_wide(1, 0, tiles)
    near_sends(1)
    near_low(0)
    near_passing(0)
    lax.fori_loop(2, 4, angles, 0)
    for half in (0, 1):
        for d2 in (1, -1):
            relay(half, 2, d2, ((0, 1), (1, 1)))
    near_high(0)
    multiply(2)
    multiply_wide(2, 0, tiles)
    near_sends(2)
    near_relays(1)
    for half in (0, 1):
        for d1 in (0, 1, -1, 2):
            for unit in ((0, 1), (1, 1)):
                landed_piece(half, d1, 2, unit)
    multiply(3)

    row_id = lax.broadcasted_iota(jnp.int32, (128, 128), 0)
    col_id = lax.broadcasted_iota(jnp.int32, (128, 128), 1)
    together = jnp.zeros((256, 128), F32)
    for unit in range(4):
        fold = jnp.logical_and(col_id // 32 == unit, row_id % 32 == col_id % 32).astype(F32).astype(BF16)
        together = together + dot(picked[:, unit].reshape(256, 128), fold)
    packed[...] = together.astype(BF16).reshape(GROUP, UNIT, 128)
    exchange_start(me, packed, landed, ex_sems)
    multiply_wide(3, 1, 3)
    near_sends(3)
    exchange_middle(me, landed, full, ex_sems)
    multiply_wide(3, 0, 1)
    multiply_wide(3, 3, tiles)
    near_relays(2)
    next_relays(0)
    for load in loads[3:]:
        load.wait()
    exchange_end(landed, ex_sems)
    for unit in range(4):
        spread = jnp.logical_and(row_id - unit * 32 == col_id - 64, row_id // 32 == unit).astype(F32).astype(BF16)
        ranks[:, unit] = dot(full[...].reshape(256, 128), spread).astype(BF16).reshape(GROUP, UNIT, 128)
    for number in range(4):
        for i, slot, half in pieces(number):
            row_ranks[number, i * 32 : (i + 1) * 32, :] = ranks[slot, 2 * half : 2 * half + 2].reshape(32, 128)

    owner = (lax.broadcasted_iota(jnp.int32, (1, 1024), 1) // RANK).astype(F32)
    spread_row = lax.broadcasted_iota(jnp.int32, (128, 1024), 0)
    spread_col = lax.broadcasted_iota(jnp.int32, (128, 1024), 1)
    fold_row = lax.broadcasted_iota(jnp.int32, (1024, 128), 0)
    fold_col = lax.broadcasted_iota(jnp.int32, (1024, 128), 1)

    def widened(values, mine, first):
        spread = (spread_row == 64 + first + spread_col % RANK).astype(F32).astype(BF16)
        return jnp.where(mine, dot(values, spread), 0.0).astype(BF16)

    def turn(head, number):
        swapped = jnp.where(even, pltpu.roll(head, 127, 1), pltpu.roll(head, 1, 1))
        return head * cosine[number] + swapped * sine[number]

    def heads(number, carry):
        mine = row_adapter[number] == owner
        own = row_ranks[number]
        wide = widened(own, mine, 0)
        query = acc[number, :, :HEAD] + dot(wide, right_qkv[:, :HEAD])
        scale = jnp.asarray(HEAD ** (-0.5), BF16)
        first = turn(query[:, :128], number).astype(BF16) * scale
        second = query[:, 128:].astype(BF16) * scale
        main = jnp.concatenate([jnp.where(lane < ROT, 0.0, first.astype(F32)).astype(BF16), second], axis=1)
        back = lax.dot_general(
            main, right_qkv[:, HEAD : 2 * HEAD], (((1,), (1,)), ((), ())), preferred_element_type=F32
        )
        fold = (fold_col == 64 + fold_row % RANK).astype(F32).astype(BF16)
        low_rank = dot(jnp.where(mine, back, 0.0).astype(BF16), fold)
        queries[number, :, :HEAD] = main
        queries[number, :, HEAD:] = jnp.where(lane < ROT, first.astype(F32), low_rank).astype(BF16)
        key = acc[number, :, HEAD : HEAD + 128] + dot(wide, right_qkv[:, HEAD : HEAD + 128])
        late[0, number] = jnp.where(lane < ROT, turn(key, number), own.astype(F32)).astype(BF16)
        return carry

    lax.fori_loop(0, 4, heads, 0)
    near_sends(4)

    def finish_hidden(number):
        wide = widened(row_ranks[number], row_adapter[number] == owner, RANK)
        for part in range(hid // 256):
            columns = slice(part * 256, (part + 1) * 256)
            value = acc[number, :, QKV + part * 256 : QKV + (part + 1) * 256]
            value = value + dot(wide, right_up[:, columns]) + in_bias[:, columns]
            value = jax.nn.gelu(value, approximate=True).astype(BF16)
            for i, slot, half in pieces(number):
                out_hidden[slot, 2 * half : 2 * half + 2, :, columns] = value[i * 32 : (i + 1) * 32, :].reshape(
                    2, UNIT, 256
                )

    def attend_all(slot, own=False):
        def body(b, carry):
            tail = late[slot].reshape(count, LATE)
            keys = jnp.concatenate([early[slot, :, :, :HEAD].reshape(count, HEAD), tail], axis=1)
            values = jnp.concatenate([early[slot, :, :, HEAD:].reshape(count, HEAD), tail], axis=1)
            scores = lax.dot_general(queries[b], keys, (((1,), (1,)), ((), ())), preferred_element_type=F32)
            key_id = names[...] + ((req - slot) * count).astype(F32)
            allowed = key_id >= row_start[b]
            if own:
                allowed = jnp.logical_and(allowed, key_id <= row_index[b])
            scores = jnp.where(allowed, scores, NEGATIVE_FILL)
            peak = jnp.max(scores, axis=1, keepdims=True)
            if own:
                kept = jnp.exp(scores - peak)
                total[b] = jnp.sum(kept, axis=1, keepdims=True)
                summed[b] = dot(kept.astype(BF16), values)
            else:
                old = top[b]
                peak = jnp.maximum(old, peak)
                kept = jnp.exp(scores - peak)
                decay = jnp.exp(old - peak)
                total[b] = total[b] * decay + jnp.sum(kept, axis=1, keepdims=True)
                summed[b] = summed[b] * decay + dot(kept.astype(BF16), values)
            top[b] = peak
            return carry

        lax.fori_loop(0, 4, body, 0)

    def attend_on(which, slot):
        @pl.when(core == which)
        def _():
            attend_all(slot)

    near_relays(3)
    next_relays(1)
    next_relays(2)
    attend_all(0, True)
    near_low(4)
    near_passing(4)
    next_relays(3)
    take_all(5 - 4 * core, 3)
    attend_on(1, 1)
    near_high(4)
    attend_all(2)
    next_relays(4)
    take_all(1 + 2 * core, 4, 5)
    attend_all(1 + 2 * core)
    attend_all(4)
    take_all(3 + 2 * core, 8, 9)
    attend_on(0, 3)
    for number in range(4):
        finish_hidden(number)
    for number in range(4):
        share = 1.0 / total[number]
        tail = (summed[number, :, HEAD:] * share).astype(BF16)
        wide = widened(tail, row_adapter[number] == owner, 0)
        value = (summed[number, :, :HEAD] * share + dot(wide, right_qkv[:, 2 * HEAD :])).astype(BF16)
        for i, slot, half in pieces(number):
            out_attended[slot, 2 * half : 2 * half + 2] = value[i * 32 : (i + 1) * 32, :].reshape(2, UNIT, HEAD)
    for copy in started:
        copy.wait_send()
    sent = xs.at[pl.ds(0, GROUP - 1)]
    pltpu.make_async_copy(sent, sent, send_sem).wait()


REDUCE_GROUPS = (
    tuple((h, d1, 2) for h in (0, 1) for d1 in (2, 1, -1, 0)),
    tuple((h, d1, d2) for h in (0, 1) for d1 in (2, 1) for d2 in (1, -1)),
    tuple((h, d1, d2) for h in (0, 1) for d1 in (-1, 0) for d2 in (1, -1)),
    tuple((h, d1, 0) for h in (0, 1) for d1 in (2, 1, -1, 0)),
)
FAR = {2: 0, 1: 1, -1: 2, 0: 3}


def output_kernel(
    attended, hidden, adapter, tokens, out_bias, w_left_attn, w_left_hid, w_attn, w_down, w_right,
    out,
    inputs, left, weights, part, from2, from1, rows_in, packed, landed, full,
    load_sems, send_sem, sems2, sems1, ex_sems,
):
    plane = Plane()
    me = plane.me
    hid = w_left_hid.shape[0]
    depth = HEAD + hid
    loads = [
        pltpu.make_async_copy(attended, inputs.at[:, :, :, pl.ds(0, HEAD)], load_sems.at[0]),
        pltpu.make_async_copy(hidden, inputs.at[:, :, :, pl.ds(HEAD, hid)], load_sems.at[1]),
        pltpu.make_async_copy(w_left_attn, left.at[pl.ds(0, HEAD)], load_sems.at[2]),
        pltpu.make_async_copy(w_left_hid, left.at[pl.ds(HEAD, hid)], load_sems.at[3]),
        pltpu.make_async_copy(w_attn, weights.at[pl.ds(0, HEAD)], load_sems.at[4]),
        pltpu.make_async_copy(w_down, weights.at[pl.ds(HEAD, hid)], load_sems.at[5]),
        pltpu.make_async_copy(w_right, weights.at[pl.ds(depth, 128)], load_sems.at[6]),
    ]
    for load in loads:
        load.start()
    sem = barrier_all(me, GROUP)
    for load in loads[:4]:
        load.wait()

    lane = lax.broadcasted_iota(jnp.int32, (1, 1024), 1)
    fold_row = lax.broadcasted_iota(jnp.int32, (1024, 128), 0)
    fold_col = lax.broadcasted_iota(jnp.int32, (1024, 128), 1)

    def lower(unit, together):
        mine = adapter[:, unit].reshape(256, 1) == (lane // RANK).astype(F32)
        for first, begin, end in ((0, 0, HEAD), (RANK, HEAD, depth)):
            product = dot(inputs[:, unit, :, begin:end].reshape(256, end - begin), left[begin:end, :])
            kept = jnp.where(mine, product, 0.0).astype(BF16)
            fold = (fold_col == unit * 32 + first + fold_row % RANK).astype(F32).astype(BF16)
            together = together + dot(kept, fold)
        return together

    together = lax.fori_loop(0, 4, lower, jnp.zeros((256, 128), F32))
    packed[...] = together.astype(BF16).reshape(GROUP, UNIT, 128)
    pl.semaphore_wait(sem, GROUP - 1)
    exchange_start(me, packed, landed, ex_sems)
    exchange_middle(me, landed, full, ex_sems)
    for load in loads[4:]:
        load.wait()
    exchange_end(landed, ex_sems)
    lane = lax.broadcasted_iota(jnp.int32, (1, 128), 1)
    row_id = lax.broadcasted_iota(jnp.int32, (128, 128), 0)
    col_id = lax.broadcasted_iota(jnp.int32, (128, 128), 1)
    for unit in range(4):
        mine = adapter[:, unit].reshape(256, 1) == (me * 4 + lane // 32).astype(F32)
        spread = (row_id == unit * 32 + col_id % 32).astype(F32).astype(BF16)
        wide = jnp.where(mine, dot(full[...].reshape(256, 128), spread), 0.0).astype(BF16)
        inputs[:, unit, :, depth:] = wide.reshape(GROUP, UNIT, 128)

    def multiply(number):
        for i, (half, d1, d2) in enumerate(REDUCE_GROUPS[number]):
            slot = plane.source(half, d1, d2)
            for u in (0, 1):
                at = i * 32 + u * UNIT
                rows_in[at : at + UNIT, :] = inputs[slot, half * 2 + u]

        def column(n, carry):
            columns = pl.ds(pl.multiple_of(n * 256, 256), 256)
            result = dot(rows_in[...], weights[:, columns]).astype(BF16)
            for i, (half, d1, d2) in enumerate(REDUCE_GROUPS[number]):
                slot = plane.source(half, d1, d2)
                part[slot, pl.ds(half * 32, 32), columns] = result[i * 32 : (i + 1) * 32, :]
            return carry

        lax.fori_loop(0, out.shape[1] // 256, column, 0)

    def rows_of(half, u):
        return pl.ds(half * 32 + u * UNIT, UNIT)

    def landing(half, axis, side, d1, place):
        index = half * 2 + side
        if axis == 2:
            return from2.at[index, FAR[d1], place], sems2.at[index, FAR[d1] * 3 + place]
        return from1.at[index, place], sems1.at[index, place]

    def send(half, d1, d2, u, axis):
        d = d2 if axis == 2 else d1
        back = d if d != 2 else (1 if u == 0 else -1)
        side = 0 if back == 1 else 1
        place = 2 if d == 2 else u
        slot = plane.source(half, d1, d2)
        to = plane.off(half, 0, -back) if axis == 2 else plane.off(half, -back, 0)
        target, arrived = landing(half, axis, side, d1, place)
        pltpu.make_async_remote_copy(
            part.at[slot, rows_of(half, u), :], target, send_sem, arrived, device_id={"mlp": to}, device_id_type=MESH
        ).start()

    def arrive(half, axis, side, d1, place):
        ref, arrived = landing(half, axis, side, d1, place)
        pltpu.make_async_copy(ref, ref, arrived).wait()
        return ref

    def add(half, d1, d2, u, children):
        refs = [arrive(half, axis, side, d1, place) for axis, side, place in children]
        slot = plane.source(half, d1, d2)
        here = part.at[slot, rows_of(half, u), :]
        value = here[...].astype(F32)
        for ref in refs:
            value = value + ref[...].astype(F32)
        here[...] = value.astype(BF16)

    multiply(0)
    for d1 in (2, 1, -1, 0):
        for half in (0, 1):
            for u in (0, 1):
                send(half, d1, 2, u, 2)
    for number in (1, 2):
        multiply(number)
        for half, d1, d2 in REDUCE_GROUPS[number]:
            send(half, d1, d2, 1 if d2 == 1 else 0, 2)
    for number in (1, 2):
        for half, d1, d2 in REDUCE_GROUPS[number]:
            u = 0 if d2 == 1 else 1
            add(half, d1, d2, u, ((2, 0 if d2 == 1 else 1, 2),))
            send(half, d1, d2, u, 2)
    multiply(3)
    both = lambda u: ((2, 0, u), (2, 1, u))
    for half in (0, 1):
        for u in (0, 1):
            add(half, 2, 0, u, both(u))
            send(half, 2, 0, u, 1)
    for d1 in (1, -1):
        for half in (0, 1):
            u = 1 if d1 == 1 else 0
            add(half, d1, 0, u, both(u))
            send(half, d1, 0, u, 1)
    for d1 in (1, -1):
        for half in (0, 1):
            u = 0 if d1 == 1 else 1
            add(half, d1, 0, u, both(u) + ((1, 0 if d1 == 1 else 1, 2),))
            send(half, d1, 0, u, 1)
    for half in (0, 1):
        for u in (0, 1):
            refs = [arrive(half, axis, side, 0, place) for axis, side, place in both(u) + ((1, 0, u), (1, 1, u))]
            rows = rows_of(half, u)
            value = part[me, rows, :].astype(F32)
            for ref in refs:
                value = value + ref[...].astype(F32)
            out[rows, :] = (value + tokens[rows, :].astype(F32) + out_bias[...]).astype(BF16)
    sent = part.at[pl.ds(0, GROUP - 1)]
    pltpu.make_async_copy(sent, sent, send_sem).wait()


def per_device(
    tokens, layer_norm_gain, layer_norm_bias, query_key_weight, output_weight, up_weight, input_bias, down_weight,
    output_bias, input_adapter_left, query_key_value_right, up_adapter_right, output_adapter_left, down_adapter_left,
    output_adapter_right, lengths, request_adapter, slot_adapter,
):
    rows, width = tokens.shape
    hid = up_weight.shape[1]
    vmem = pl.BlockSpec(memory_space=pltpu.VMEM)
    smem = pl.BlockSpec(memory_space=pltpu.SMEM)
    anywhere = pl.BlockSpec(memory_space=pl.ANY)
    dma = pltpu.SemaphoreType.DMA
    by_unit = (GROUP, 4, UNIT)
    attended, hidden, adapter = pl.pallas_call(
        front_kernel,
        out_shape=(
            jax.ShapeDtypeStruct(by_unit + (HEAD,), BF16),
            jax.ShapeDtypeStruct(by_unit + (hid,), BF16),
            jax.ShapeDtypeStruct(by_unit + (1,), F32),
        ),
        in_specs=[vmem] * 5 + [smem] + [anywhere] * 5,
        out_specs=(vmem, vmem, vmem),
        scratch_shapes=[
            pltpu.VMEM((GROUP, rows, width), BF16),
            pltpu.VMEM((width, QKV + hid + 128), BF16),
            pltpu.VMEM(query_key_value_right.shape[:1] + (QKV,), BF16),
            pltpu.VMEM(up_adapter_right.shape, BF16),
            pltpu.VMEM((256, width), BF16),
            pltpu.VMEM((4, 256, QKV + hid), F32),
            pltpu.VMEM(by_unit + (128,), BF16),
            pltpu.VMEM((GROUP, UNIT, 128), BF16),
            pltpu.VMEM((GROUP, UNIT, 128), BF16),
            pltpu.VMEM((GROUP, UNIT, 128), BF16),
            pltpu.VMEM(by_unit + (1,), F32),
            pltpu.VMEM((4, 256, 1), F32),
            pltpu.VMEM((4, 256, 1), F32),
            pltpu.VMEM((4, 256, 1), F32),
            pltpu.VMEM((1, 1024), F32),
            pltpu.VMEM((4, 256, 128), F32),
            pltpu.VMEM((4, 256, 128), F32),
            pltpu.VMEM(by_unit + (128,), BF16),
            pltpu.VMEM((4, 256, 128), BF16),
            pltpu.VMEM((4, 256, HEAD + LATE), BF16),
            pltpu.VMEM((6, 4, 256, 2 * HEAD), BF16),
            pltpu.VMEM((6, 4, 256, LATE), BF16),
            pltpu.VMEM((4, 256 - CUT, 2 * HEAD), BF16),
            pltpu.VMEM((4, 256 - CUT, LATE), BF16),
            pltpu.VMEM((4, 256, 1), F32),
            pltpu.VMEM((4, 256, 1), F32),
            pltpu.VMEM((4, 256, HEAD + LATE), F32),
            dma((5,)),
            dma,
            dma((GROUP, 4)),
            dma((4,)),
            dma((50,)),
            dma((50,)),
        ],
        compiler_params=pltpu.CompilerParams(
            collective_id=0, has_side_effects=True, vmem_limit_bytes=VMEM_LIMIT
        ),
        name="front_stage",
    )(
        tokens, layer_norm_gain[None, :], layer_norm_bias[None, :], input_bias[None, :],
        jnp.stack([lengths, request_adapter]), slot_adapter,
        query_key_weight.reshape(width, QKV), up_weight, input_adapter_left,
        query_key_value_right.reshape(-1, QKV), up_adapter_right,
    )

    depth = HEAD + hid + 128
    return pl.pallas_call(
        output_kernel,
        out_shape=jax.ShapeDtypeStruct((rows, width), BF16),
        in_specs=[anywhere] * 2 + [vmem] * 3 + [anywhere] * 5,
        out_specs=vmem,
        scratch_shapes=[
            pltpu.VMEM(by_unit + (depth,), BF16),
            pltpu.VMEM((HEAD + hid, 1024), BF16),
            pltpu.VMEM((depth, width), BF16),
            pltpu.VMEM((GROUP, rows, width), BF16),
            pltpu.VMEM((4, 4, 3, UNIT, width), BF16),
            pltpu.VMEM((4, 3, UNIT, width), BF16),
            pltpu.VMEM((256, depth), BF16),
            pltpu.VMEM((GROUP, UNIT, 128), BF16),
            pltpu.VMEM((GROUP, UNIT, 128), BF16),
            pltpu.VMEM((GROUP, UNIT, 128), BF16),
            dma((7,)),
            dma,
            dma((4, 12)),
            dma((4, 3)),
            dma((4,)),
        ],
        compiler_params=pltpu.CompilerParams(
            collective_id=1, has_side_effects=True, vmem_limit_bytes=VMEM_LIMIT
        ),
        name="output_stage",
    )(
        attended, hidden, adapter, tokens, output_bias[None, :],
        output_adapter_left.reshape(HEAD, -1), down_adapter_left, output_weight.reshape(HEAD, width), down_weight,
        output_adapter_right,
    )


def solution(mesh):
    in_specs = (
        P(("req", "mlp"), None), P(), P(), P(None, "mlp", None), P("mlp", None, None), P(None, "mlp"), P("mlp"),
        P("mlp", None), P(), P(None, "mlp"), P(None, "mlp", None), P(None, "mlp"), P("mlp", None, None),
        P("mlp", None), P("mlp", None), P(), P(), P("mlp"),
    )
    return jax.shard_map(
        per_device, mesh=mesh, in_specs=in_specs, out_specs=P(("req", "mlp"), None), check_vma=False
    )
```

```python
import math

import jax
import jax.numpy as jnp
from jax import lax
from jax.experimental import pallas as pl
from jax.experimental.pallas import tpu as pltpu
from jax.sharding import PartitionSpec as P

HEAD = 256
ROT = 64
RANK = 16
EPSILON = 1e-05
NEGATIVE_FILL = -1e30
MESH = pl.DeviceIdType.MESH
F32 = jnp.float32
BF16 = jnp.bfloat16
VMEM_LIMIT = 63 * 1024 * 1024
SIDE = 4
GROUP = 16
UNIT = 16
QKV = 3 * HEAD
CUT = 96
LATE = 128


def dot(a, b):
    return jnp.dot(a, b, preferred_element_type=F32)


class Plane:
    def __init__(self):
        self.me = lax.axis_index("mlp")
        self.z = self.me // SIDE
        self.y = self.me % SIDE

    def at(self, dz, dy):
        return ((self.z + dz + SIDE) % SIDE) * SIDE + (self.y + dy + SIDE) % SIDE

    def off(self, half, d1, d2):
        return self.at(d1, d2) if half == 0 else self.at(d2, d1)

    def source(self, half, d1, d2):
        return self.off(half, -d1, -d2)


def barrier_all(me, count):
    sem = pltpu.get_barrier_semaphore()
    for k in range(1, count):
        pl.semaphore_signal(sem, inc=1, device_id={"mlp": (me + k) % count}, device_id_type=MESH)
    return sem


def exchange_start(me, packed, landed, sems):
    def scatter(k, carry):
        to = (me + k) % GROUP
        pltpu.make_async_remote_copy(
            packed.at[to], landed.at[me], sems.at[0], sems.at[1], device_id={"mlp": to}, device_id_type=MESH
        ).start()
        return carry

    lax.fori_loop(1, GROUP, scatter, 0)
    landed[me] = packed[me]


def exchange_middle(me, landed, full, sems):
    many = landed.at[pl.ds(0, GROUP - 1)]
    pltpu.make_async_copy(many, many, sems.at[1]).wait()
    full[me] = jnp.sum(landed[...].astype(F32), axis=0).astype(BF16)

    def gather(k, carry):
        to = (me + k) % GROUP
        pltpu.make_async_remote_copy(
            full.at[me], full.at[me], sems.at[2], sems.at[3], device_id={"mlp": to}, device_id_type=MESH
        ).start()
        return carry

    lax.fori_loop(1, GROUP, gather, 0)


def exchange_end(landed, sems):
    many = landed.at[pl.ds(0, GROUP - 1)]
    for number in (3, 0, 2):
        pltpu.make_async_copy(many, many, sems.at[number]).wait()


GATHER_GROUPS = (
    tuple((h, d1, 0) for h in (0, 1) for d1 in (0, 1, -1, 2)),
    tuple((h, d1, d2) for h in (0, 1) for d1 in (0, 1) for d2 in (1, -1)),
    tuple((h, d1, d2) for h in (0, 1) for d1 in (-1, 2) for d2 in (1, -1)),
    tuple((h, d1, 2) for h in (0, 1) for d1 in (0, 1, -1, 2)),
)


REDUCE_GROUPS = (
    tuple((h, d1, 2) for h in (0, 1) for d1 in (2, 1, -1, 0)),
    tuple((h, d1, d2) for h in (0, 1) for d1 in (2, 1) for d2 in (1, -1)),
    tuple((h, d1, d2) for h in (0, 1) for d1 in (-1, 0) for d2 in (1, -1)),
    tuple((h, d1, 0) for h in (0, 1) for d1 in (2, 1, -1, 0)),
)
FAR = {2: 0, 1: 1, -1: 2, 0: 3}


def layer_kernel(
    tokens, gain, bias, in_bias, out_bias, table, slots, w_qkv, w_up, w_left, w_qkv_right, w_up_right,
    w_left_attn, w_left_hid, w_attn, w_down, w_right,
    out,
    xs, weights, right_qkv, right_up, rows_in, acc, picked, packed, landed, full,
    starts, adapter, row_index, row_start, row_adapter, names, cosine, sine, ranks, row_ranks, queries,
    early, late, pass_early, pass_late, top, total, summed,
    inputs, left, chosen_rows, from2, from1,
    load_sems, send_sem, recv_sems, ex_sems, near_send, near_recv, weight_sems, back_sem, sems2, sems1,
):
    plane = Plane()
    me = plane.me
    req = lax.axis_index("req")
    chip, core = req // 2, req % 2
    ahead = ((chip + 1) % SIDE) * 2 + core
    behind = ((chip + 3) % SIDE) * 2 + core
    other = chip * 2 + 1 - core
    hid = w_up.shape[1]
    count = GROUP * 64
    loads = [
        pltpu.make_async_copy(w_qkv, weights.at[:, pl.ds(0, QKV)], load_sems.at[0]),
        pltpu.make_async_copy(w_up, weights.at[:, pl.ds(QKV, hid)], load_sems.at[1]),
        pltpu.make_async_copy(w_left, weights.at[:, pl.ds(QKV + hid, 128)], load_sems.at[2]),
        pltpu.make_async_copy(w_qkv_right, right_qkv, load_sems.at[3]),
        pltpu.make_async_copy(w_up_right, right_up, load_sems.at[4]),
        pltpu.make_async_copy(w_left_attn, left.at[pl.ds(0, HEAD)], load_sems.at[5]),
        pltpu.make_async_copy(w_left_hid, left.at[pl.ds(HEAD, hid)], load_sems.at[6]),
    ]
    for load in loads:
        load.start()
    sem = barrier_all(me, GROUP)
    for device in (ahead, behind, other):
        pl.semaphore_signal(sem, inc=1, device_id={"req": device}, device_id_type=MESH)
    for part in range(0, 64, 16):
        values = tokens[part : part + 16, :].astype(F32)
        center = values - jnp.mean(values, axis=1, keepdims=True)
        spread = jnp.mean(center * center, axis=1, keepdims=True)
        scaled = center * lax.rsqrt(spread + EPSILON)
        xs[me, part : part + 16, :] = (scaled * gain[...] + bias[...]).astype(BF16)
    pl.semaphore_wait(sem, GROUP + 2)

    def send(slot, half, units, axis, step):
        first, many = units
        rows = pl.ds(half * 32 + first * UNIT, many * UNIT)
        to = plane.off(half, step, 0) if axis == 1 else plane.off(half, 0, step)
        pltpu.make_async_remote_copy(
            xs.at[slot, rows, :], xs.at[slot, rows, :], send_sem, recv_sems.at[slot, half * 2 + first],
            device_id={"mlp": to}, device_id_type=MESH,
        ).start()

    def landed_piece(half, d1, d2, units):
        first, many = units
        slot = plane.source(half, d1, d2)
        rows = pl.ds(half * 32 + first * UNIT, many * UNIT)
        view = xs.at[slot, rows, :]
        pltpu.make_async_copy(view, view, recv_sems.at[slot, half * 2 + first]).wait()
        return slot

    whole = (0, 2)
    for half in (0, 1):
        for step in (1, -1):
            send(me, half, whole, 1, step)
    for half in (0, 1):
        for step in (1, -1):
            send(me, half, whole, 2, step)

    long = table[0:1, :].astype(F32)
    requests = long.shape[1]
    before = lax.broadcasted_iota(jnp.int32, (requests, requests), 0) < lax.broadcasted_iota(
        jnp.int32, (requests, requests), 1
    )
    begins = dot(jnp.broadcast_to(long, (8, requests)).astype(BF16), before.astype(F32).astype(BF16))[:1, :]
    ends = begins + long
    ids = table[1:2, :].astype(F32)

    def locate(block, carry):
        rows = lax.broadcasted_iota(jnp.int32, (64, 1), 0)
        index = (req * count + block * 64 + rows).astype(F32)
        inside = jnp.logical_and(begins <= index, index < ends)
        start = jnp.sum(jnp.where(inside, begins, 0.0), axis=1, keepdims=True)
        mine = jnp.sum(jnp.where(inside, ids, 0.0), axis=1, keepdims=True)
        starts[block] = start.reshape(4, UNIT, 1)
        adapter[block] = mine.reshape(4, UNIT, 1)
        return carry

    lax.fori_loop(0, GROUP, locate, 0)

    def pieces(number):
        return [(i, plane.source(h, d1, d2), h) for i, (h, d1, d2) in enumerate(GATHER_GROUPS[number])]

    piece_row = lax.broadcasted_iota(jnp.int32, (32, 1), 0)
    piece_lane = lax.broadcasted_iota(jnp.int32, (1, 256), 1)
    for number in range(4):
        name = piece_lane
        for i, slot, half in pieces(number):
            at = slice(i * 32, (i + 1) * 32)
            first = slot * 64 + half * 32
            row_index[number, at, :] = (req * count + first + piece_row).astype(F32)
            row_start[number, at, :] = starts[slot, 2 * half : 2 * half + 2].reshape(32, 1)
            row_adapter[number, at, :] = adapter[slot, 2 * half : 2 * half + 2].reshape(32, 1)
            name = jnp.where(piece_lane // 32 == i, first + piece_lane % 32, name)
        names[:, number * 256 : (number + 1) * 256] = name.astype(F32)

    for half in (0, 1):
        for d1 in (1, -1):
            slot = landed_piece(half, d1, 0, whole)
            send(slot, half, (0, 1) if d1 == 1 else (1, 1), 1, d1)
            for step in (1, -1):
                send(slot, half, whole, 2, step)

    def relay(half, d1, d2, pieces):
        for units in pieces:
            slot = landed_piece(half, d1, d2, units)
        send(slot, half, (0, 1) if d2 == 1 else (1, 1), 2, d2)

    lane = lax.broadcasted_iota(jnp.int32, (1, 128), 1)
    even = lane % 2 == 0

    frequency = jnp.exp((lane // 2).astype(F32) * (-2.0 * math.log(10000.0) / ROT))

    def angles(number, carry):
        angle = (row_index[number] - row_start[number]) * frequency
        turned = lane < ROT
        cosine[number] = jnp.where(turned, jnp.cos(angle), 1.0)
        sine[number] = jnp.where(turned, jnp.where(even, -1.0, 1.0) * jnp.sin(angle), 0.0)
        return carry

    chosen = jnp.where(lane < 32, slots[0], jnp.where(lane < 64, slots[1], jnp.where(lane < 96, slots[2], slots[3])))
    chosen = chosen.astype(F32)

    def multiply(number):
        for i, slot, half in pieces(number):
            rows_in[i * 32 : (i + 1) * 32, :] = xs[slot, pl.ds(half * 32, 32), :]
        left = dot(rows_in[...], weights[:, QKV + hid :])
        kept = jnp.where(row_adapter[number] == chosen, left, 0.0).astype(BF16)
        for i, slot, half in pieces(number):
            picked[slot, 2 * half : 2 * half + 2] = kept[i * 32 : (i + 1) * 32, :].reshape(2, UNIT, 128)

    def multiply_wide(number, begin, end):
        def column(n, carry):
            columns = pl.ds(pl.multiple_of(n * 256, 256), 256)
            acc[number, :, columns] = dot(rows_in[...], weights[:, columns])
            return carry

        lax.fori_loop(begin, end, column, 0)

    low, high, every = pl.ds(0, CUT), pl.ds(CUT, 256 - CUT), pl.ds(0, 256)
    started = []

    def view(slot, part, rows=every):
        return early.at[slot, part, rows] if part < 4 else late.at[slot, :, rows]

    def pass_on(src, dst, number, device):
        copy = pltpu.make_async_remote_copy(
            src, dst, near_send.at[number], near_recv.at[number], device_id={"req": device}, device_id_type=MESH
        )
        copy.start()
        started.append(copy)

    def take(ref, number):
        pltpu.make_async_copy(ref, ref, near_recv.at[number]).wait()

    def by_way(part):
        return pass_early.at[part] if part < 4 else pass_late

    def near_sends(part):
        if part < 4:
            early[0, part] = acc[part, :, HEAD:QKV].astype(BF16)
        at = 10 * part
        pass_on(view(0, part, low), view(2, part, low), at, ahead)
        pass_on(view(0, part, high), by_way(part), at + 2, behind)
        pass_on(view(0, part, high), view(2, part, high), at + 1, ahead)
        pass_on(view(0, part), view(1 + 4 * core, part), at + 3, other)

    def near_low(part):
        at = 10 * part
        take(view(2, part, low), at)
        pass_on(view(2, part, low), view(4, part, low), at + 6, ahead)
        pass_on(view(2, part, low), view(3 - 2 * core, part, low), at + 4, other)

    def near_passing(part):
        at = 10 * part
        take(by_way(part), at + 2)
        pass_on(by_way(part), view(4, part, high), at + 7, behind)

    def near_high(part):
        at = 10 * part
        take(view(2, part, high), at + 1)
        pass_on(view(2, part, high), view(3 - 2 * core, part, high), at + 5, other)

    def near_relays(part):
        near_low(part)
        near_passing(part)
        near_high(part)

    def next_relays(part):
        at = 10 * part
        take(view(4, part, high), at + 7)
        pass_on(view(4, part, high), view(5 - 2 * core, part, high), at + 9, other)
        take(view(4, part, low), at + 6)
        pass_on(view(4, part, low), view(5 - 2 * core, part, low), at + 8, other)

    def take_all(slot, first, second=None):
        for part in range(5):
            if second is None:
                take(view(slot, part), 10 * part + first)
            else:
                take(view(slot, part, low), 10 * part + first)
                take(view(slot, part, high), 10 * part + second)

    tiles = (QKV + hid) // 256
    lax.fori_loop(0, 2, angles, 0)
    for half in (0, 1):
        for d2 in (1, -1):
            relay(half, 0, d2, (whole,))
    for half in (0, 1):
        for unit in ((0, 1), (1, 1)):
            slot = landed_piece(half, 2, 0, unit)
            for step in (1, -1):
                send(slot, half, unit, 2, step)
    for load in loads[:3]:
        load.wait()
    multiply(0)
    multiply_wide(0, 0, tiles)
    near_sends(0)
    for half in (0, 1):
        for d1 in (1, -1):
            for d2 in (1, -1):
                relay(half, d1, d2, (whole,))
    multiply(1)
    multiply_wide(1, 0, tiles)
    near_sends(1)
    near_low(0)
    near_passing(0)
    lax.fori_loop(2, 4, angles, 0)
    for half in (0, 1):
        for d2 in (1, -1):
            relay(half, 2, d2, ((0, 1), (1, 1)))
    near_high(0)
    multiply(2)
    multiply_wide(2, 0, tiles)
    near_sends(2)
    near_relays(1)
    for half in (0, 1):
        for d1 in (0, 1, -1, 2):
            for unit in ((0, 1), (1, 1)):
                landed_piece(half, d1, 2, unit)
    multiply(3)

    row_id = lax.broadcasted_iota(jnp.int32, (128, 128), 0)
    col_id = lax.broadcasted_iota(jnp.int32, (128, 128), 1)
    together = jnp.zeros((256, 128), F32)
    for unit in range(4):
        fold = jnp.logical_and(col_id // 32 == unit, row_id % 32 == col_id % 32).astype(F32).astype(BF16)
        together = together + dot(picked[:, unit].reshape(256, 128), fold)
    packed[0] = together.astype(BF16).reshape(GROUP, UNIT, 128)
    exchange_start(me, packed.at[0], landed.at[0], ex_sems.at[0])
    multiply_wide(3, 1, 3)
    near_sends(3)
    exchange_middle(me, landed.at[0], full.at[0], ex_sems.at[0])
    multiply_wide(3, 0, 1)
    multiply_wide(3, 3, tiles)
    depth = HEAD + hid
    width = out.shape[1]
    deep = depth + 128
    stored = []
    for n in range(width // 256):
        columns = pl.ds(n // 4 * 256, 256)
        for j, (ref, first, size) in enumerate(((w_attn, 0, HEAD), (w_down, HEAD, hid), (w_right, depth, 128))):
            copy = pltpu.make_async_copy(
                ref.at[:, pl.ds(n * 256, 256)], weights.at[pl.ds(n % 4 * deep + first, size), columns],
                weight_sems.at[n * 3 + j],
            )
            copy.start()
            stored.append(copy)
    near_relays(2)
    next_relays(0)
    for load in loads[3:]:
        load.wait()
    exchange_end(landed.at[0], ex_sems.at[0])
    for unit in range(4):
        spread = jnp.logical_and(row_id - unit * 32 == col_id - 64, row_id // 32 == unit).astype(F32).astype(BF16)
        ranks[:, unit] = dot(full[0].reshape(256, 128), spread).astype(BF16).reshape(GROUP, UNIT, 128)
    for number in range(4):
        for i, slot, half in pieces(number):
            row_ranks[number, i * 32 : (i + 1) * 32, :] = ranks[slot, 2 * half : 2 * half + 2].reshape(32, 128)

    owner = (lax.broadcasted_iota(jnp.int32, (1, 1024), 1) // RANK).astype(F32)
    spread_row = lax.broadcasted_iota(jnp.int32, (128, 1024), 0)
    spread_col = lax.broadcasted_iota(jnp.int32, (128, 1024), 1)
    fold_row = lax.broadcasted_iota(jnp.int32, (1024, 128), 0)
    fold_col = lax.broadcasted_iota(jnp.int32, (1024, 128), 1)

    def widened(values, mine, first):
        spread = (spread_row == 64 + first + spread_col % RANK).astype(F32).astype(BF16)
        return jnp.where(mine, dot(values, spread), 0.0).astype(BF16)

    def turn(head, number):
        swapped = jnp.where(even, pltpu.roll(head, 127, 1), pltpu.roll(head, 1, 1))
        return head * cosine[number] + swapped * sine[number]

    def heads(number, carry):
        mine = row_adapter[number] == owner
        own = row_ranks[number]
        wide = widened(own, mine, 0)
        query = acc[number, :, :HEAD] + dot(wide, right_qkv[:, :HEAD])
        scale = jnp.asarray(HEAD ** (-0.5), BF16)
        first = turn(query[:, :128], number).astype(BF16) * scale
        second = query[:, 128:].astype(BF16) * scale
        main = jnp.concatenate([jnp.where(lane < ROT, 0.0, first.astype(F32)).astype(BF16), second], axis=1)
        back = lax.dot_general(
            main, right_qkv[:, HEAD : 2 * HEAD], (((1,), (1,)), ((), ())), preferred_element_type=F32
        )
        fold = (fold_col == 64 + fold_row % RANK).astype(F32).astype(BF16)
        low_rank = dot(jnp.where(mine, back, 0.0).astype(BF16), fold)
        queries[number, :, :HEAD] = main
        queries[number, :, HEAD:] = jnp.where(lane < ROT, first.astype(F32), low_rank).astype(BF16)
        key = acc[number, :, HEAD : HEAD + 128] + dot(wide, right_qkv[:, HEAD : HEAD + 128])
        late[0, number] = jnp.where(lane < ROT, turn(key, number), own.astype(F32)).astype(BF16)
        return carry

    lax.fori_loop(0, 4, heads, 0)
    near_sends(4)

    def finish_hidden(number):
        wide = widened(row_ranks[number], row_adapter[number] == owner, RANK)
        for part in range(hid // 256):
            columns = slice(part * 256, (part + 1) * 256)
            value = acc[number, :, QKV + part * 256 : QKV + (part + 1) * 256]
            value = value + dot(wide, right_up[:, columns]) + in_bias[:, columns]
            value = jax.nn.gelu(value, approximate=True).astype(BF16)
            for i, slot, half in pieces(number):
                inputs[slot, 2 * half : 2 * half + 2, :, HEAD + part * 256 : HEAD + (part + 1) * 256] = value[
                    i * 32 : (i + 1) * 32, :
                ].reshape(2, UNIT, 256)

    def attend_all(slot, own=False):
        def body(b, carry):
            tail = late[slot].reshape(count, LATE)
            keys = jnp.concatenate([early[slot, :, :, :HEAD].reshape(count, HEAD), tail], axis=1)
            values = jnp.concatenate([early[slot, :, :, HEAD:].reshape(count, HEAD), tail], axis=1)
            scores = lax.dot_general(queries[b], keys, (((1,), (1,)), ((), ())), preferred_element_type=F32)
            key_id = names[...] + ((req - slot) * count).astype(F32)
            allowed = key_id >= row_start[b]
            if own:
                allowed = jnp.logical_and(allowed, key_id <= row_index[b])
            scores = jnp.where(allowed, scores, NEGATIVE_FILL)
            peak = jnp.max(scores, axis=1, keepdims=True)
            if own:
                kept = jnp.exp(scores - peak)
                total[b] = jnp.sum(kept, axis=1, keepdims=True)
                summed[b] = dot(kept.astype(BF16), values)
            else:
                old = top[b]
                peak = jnp.maximum(old, peak)
                kept = jnp.exp(scores - peak)
                decay = jnp.exp(old - peak)
                total[b] = total[b] * decay + jnp.sum(kept, axis=1, keepdims=True)
                summed[b] = summed[b] * decay + dot(kept.astype(BF16), values)
            top[b] = peak
            return carry

        lax.fori_loop(0, 4, body, 0)

    def attend_on(which, slot):
        @pl.when(core == which)
        def _():
            attend_all(slot)

    def lower(unit, first, begin, end):
        mine = adapter[:, unit].reshape(256, 1) == owner
        product = dot(inputs[:, unit, :, begin:end].reshape(256, end - begin), left[begin:end, :])
        fold = (fold_col == unit * 32 + first + fold_row % RANK).astype(F32).astype(BF16)
        return dot(jnp.where(mine, product, 0.0).astype(BF16), fold)

    near_relays(3)
    next_relays(1)
    next_relays(2)
    finish_hidden(0)
    attend_all(0, True)
    near_low(4)
    finish_hidden(1)
    finish_hidden(2)
    near_passing(4)
    next_relays(3)
    take_all(5 - 4 * core, 3)
    finish_hidden(3)
    attend_on(1, 1)
    near_high(4)
    attend_all(2)
    next_relays(4)
    take_all(1 + 2 * core, 4, 5)
    attend_all(1 + 2 * core)
    attend_all(4)
    together = lax.fori_loop(0, 4, lambda unit, sum_: sum_ + lower(unit, RANK, HEAD, depth), jnp.zeros((256, 128), F32))
    take_all(3 + 2 * core, 8, 9)
    attend_on(0, 3)
    for number in range(4):
        share = 1.0 / total[number]
        tail = (summed[number, :, HEAD:] * share).astype(BF16)
        wide = widened(tail, row_adapter[number] == owner, 0)
        value = (summed[number, :, :HEAD] * share + dot(wide, right_qkv[:, 2 * HEAD :])).astype(BF16)
        for i, slot, half in pieces(number):
            inputs[slot, 2 * half : 2 * half + 2, :, :HEAD] = value[i * 32 : (i + 1) * 32, :].reshape(2, UNIT, HEAD)
    for unit in range(4):
        together = together + lower(unit, 0, 0, HEAD)
    packed[1] = together.astype(BF16).reshape(GROUP, UNIT, 128)
    exchange_start(me, packed.at[1], landed.at[1], ex_sems.at[1])
    for copy in started:
        copy.wait_send()
    sent = xs.at[pl.ds(0, GROUP - 1)]
    pltpu.make_async_copy(sent, sent, send_sem).wait()
    for copy in stored:
        copy.wait()

    def back_weights(n, first, size):
        return weights[pl.ds(pl.multiple_of(n % 4 * deep + first, 128), size), pl.ds(pl.multiple_of(n // 4 * 256, 256), 256)]

    def base(n, carry):
        acc[n % 4, :, pl.ds(pl.multiple_of(n // 4 * 256, 256), 256)] = dot(
            chosen_rows[:, :depth], back_weights(n, 0, depth)
        )
        return carry

    for i, (half, d1, d2) in enumerate(REDUCE_GROUPS[0]):
        slot = plane.source(half, d1, d2)
        chosen_rows[i * 32 : (i + 1) * 32, :depth] = inputs[slot, 2 * half : 2 * half + 2, :, :depth].reshape(32, depth)
    tiles = width // 256
    lax.fori_loop(0, tiles // 2, base, 0)
    exchange_middle(me, landed.at[1], full.at[1], ex_sems.at[1])
    lax.fori_loop(tiles // 2, tiles, base, 0)
    exchange_end(landed.at[1], ex_sems.at[1])
    held = (me * 4 + lane // 32).astype(F32)
    for unit in range(4):
        mine = adapter[:, unit].reshape(256, 1) == held
        spread = (row_id == unit * 32 + col_id % 32).astype(F32).astype(BF16)
        wide = jnp.where(mine, dot(full[1].reshape(256, 128), spread), 0.0).astype(BF16)
        inputs[:, unit, :, depth:] = wide.reshape(GROUP, UNIT, 128)

    def first_group():
        for i, (half, d1, d2) in enumerate(REDUCE_GROUPS[0]):
            slot = plane.source(half, d1, d2)
            chosen_rows[i * 32 : (i + 1) * 32, depth:] = inputs[slot, 2 * half : 2 * half + 2, :, depth:].reshape(32, 128)

        def column(n, carry):
            columns = pl.ds(pl.multiple_of(n * 256, 256), 256)
            result = dot(chosen_rows[:, depth:], back_weights(n, depth, 128))
            result = (result + acc[n % 4, :, pl.ds(pl.multiple_of(n // 4 * 256, 256), 256)]).astype(BF16)
            for i, (half, d1, d2) in enumerate(REDUCE_GROUPS[0]):
                xs[plane.source(half, d1, d2), pl.ds(half * 32, 32), columns] = result[i * 32 : (i + 1) * 32, :]
            return carry

        lax.fori_loop(0, width // 256, column, 0)

    def multiply_back(number):
        for i, (half, d1, d2) in enumerate(REDUCE_GROUPS[number]):
            slot = plane.source(half, d1, d2)
            chosen_rows[i * 32 : (i + 1) * 32, :] = inputs[slot, 2 * half : 2 * half + 2].reshape(32, deep)

        def column(n, carry):
            columns = pl.ds(pl.multiple_of(n * 256, 256), 256)
            result = dot(chosen_rows[...], back_weights(n, 0, deep)).astype(BF16)
            for i, (half, d1, d2) in enumerate(REDUCE_GROUPS[number]):
                xs[plane.source(half, d1, d2), pl.ds(half * 32, 32), columns] = result[i * 32 : (i + 1) * 32, :]
            return carry

        lax.fori_loop(0, width // 256, column, 0)

    def unit_rows(half, u):
        return pl.ds(half * 32 + u * UNIT, UNIT)

    def landing(half, axis, side, d1, place):
        index = half * 2 + side
        if axis == 2:
            return from2.at[index, FAR[d1], place], sems2.at[index, FAR[d1] * 3 + place]
        return from1.at[index, place], sems1.at[index, place]

    def send_back(half, d1, d2, u, axis):
        d = d2 if axis == 2 else d1
        back = d if d != 2 else (1 if u == 0 else -1)
        side = 0 if back == 1 else 1
        place = 2 if d == 2 else u
        slot = plane.source(half, d1, d2)
        to = plane.off(half, 0, -back) if axis == 2 else plane.off(half, -back, 0)
        target, arrived = landing(half, axis, side, d1, place)
        pltpu.make_async_remote_copy(
            xs.at[slot, unit_rows(half, u), :], target, back_sem, arrived, device_id={"mlp": to}, device_id_type=MESH
        ).start()

    def arrive_back(half, axis, side, d1, place):
        ref, arrived = landing(half, axis, side, d1, place)
        pltpu.make_async_copy(ref, ref, arrived).wait()
        return ref

    def add(half, d1, d2, u, children):
        refs = [arrive_back(half, axis, side, d1, place) for axis, side, place in children]
        slot = plane.source(half, d1, d2)
        here = xs.at[slot, unit_rows(half, u), :]
        value = here[...].astype(F32)
        for ref in refs:
            value = value + ref[...].astype(F32)
        here[...] = value.astype(BF16)

    first_group()
    for d1 in (2, 1, -1, 0):
        for half in (0, 1):
            for u in (0, 1):
                send_back(half, d1, 2, u, 2)
    for number in (1, 2):
        multiply_back(number)
        for half, d1, d2 in REDUCE_GROUPS[number]:
            send_back(half, d1, d2, 1 if d2 == 1 else 0, 2)
    for number in (1, 2):
        for half, d1, d2 in REDUCE_GROUPS[number]:
            u = 0 if d2 == 1 else 1
            add(half, d1, d2, u, ((2, 0 if d2 == 1 else 1, 2),))
            send_back(half, d1, d2, u, 2)
    multiply_back(3)
    both = lambda u: ((2, 0, u), (2, 1, u))
    for half in (0, 1):
        for u in (0, 1):
            add(half, 2, 0, u, both(u))
            send_back(half, 2, 0, u, 1)
    for d1 in (1, -1):
        for half in (0, 1):
            u = 1 if d1 == 1 else 0
            add(half, d1, 0, u, both(u))
            send_back(half, d1, 0, u, 1)
    for d1 in (1, -1):
        for half in (0, 1):
            u = 0 if d1 == 1 else 1
            add(half, d1, 0, u, both(u) + ((1, 0 if d1 == 1 else 1, 2),))
            send_back(half, d1, 0, u, 1)
    for half in (0, 1):
        for u in (0, 1):
            refs = [arrive_back(half, axis, side, 0, place) for axis, side, place in both(u) + ((1, 0, u), (1, 1, u))]
            rows = unit_rows(half, u)
            value = xs[me, rows, :].astype(F32)
            for ref in refs:
                value = value + ref[...].astype(F32)
            out[rows, :] = (value + tokens[rows, :].astype(F32) + out_bias[...]).astype(BF16)
    sent = xs.at[pl.ds(0, GROUP - 1)]
    pltpu.make_async_copy(sent, sent, back_sem).wait()


def per_device(
    tokens, layer_norm_gain, layer_norm_bias, query_key_weight, output_weight, up_weight, input_bias, down_weight,
    output_bias, input_adapter_left, query_key_value_right, up_adapter_right, output_adapter_left, down_adapter_left,
    output_adapter_right, lengths, request_adapter, slot_adapter,
):
    rows, width = tokens.shape
    hid = up_weight.shape[1]
    vmem = pl.BlockSpec(memory_space=pltpu.VMEM)
    smem = pl.BlockSpec(memory_space=pltpu.SMEM)
    anywhere = pl.BlockSpec(memory_space=pl.ANY)
    dma = pltpu.SemaphoreType.DMA
    by_unit = (GROUP, 4, UNIT)
    depth = HEAD + hid
    return pl.pallas_call(
        layer_kernel,
        out_shape=jax.ShapeDtypeStruct((rows, width), BF16),
        in_specs=[vmem] * 6 + [smem] + [anywhere] * 10,
        out_specs=vmem,
        scratch_shapes=[
            pltpu.VMEM((GROUP, rows, width), BF16),
            pltpu.VMEM((width, QKV + hid + 128), BF16),
            pltpu.VMEM(query_key_value_right.shape[:1] + (QKV,), BF16),
            pltpu.VMEM(up_adapter_right.shape, BF16),
            pltpu.VMEM((256, width), BF16),
            pltpu.VMEM((4, 256, QKV + hid), F32),
            pltpu.VMEM(by_unit + (128,), BF16),
            pltpu.VMEM((2, GROUP, UNIT, 128), BF16),
            pltpu.VMEM((2, GROUP, UNIT, 128), BF16),
            pltpu.VMEM((2, GROUP, UNIT, 128), BF16),
            pltpu.VMEM(by_unit + (1,), F32),
            pltpu.VMEM(by_unit + (1,), F32),
            pltpu.VMEM((4, 256, 1), F32),
            pltpu.VMEM((4, 256, 1), F32),
            pltpu.VMEM((4, 256, 1), F32),
            pltpu.VMEM((1, 1024), F32),
            pltpu.VMEM((4, 256, 128), F32),
            pltpu.VMEM((4, 256, 128), F32),
            pltpu.VMEM(by_unit + (128,), BF16),
            pltpu.VMEM((4, 256, 128), BF16),
            pltpu.VMEM((4, 256, HEAD + LATE), BF16),
            pltpu.VMEM((6, 4, 256, 2 * HEAD), BF16),
            pltpu.VMEM((6, 4, 256, LATE), BF16),
            pltpu.VMEM((4, 256 - CUT, 2 * HEAD), BF16),
            pltpu.VMEM((4, 256 - CUT, LATE), BF16),
            pltpu.VMEM((4, 256, 1), F32),
            pltpu.VMEM((4, 256, 1), F32),
            pltpu.VMEM((4, 256, HEAD + LATE), F32),
            pltpu.VMEM(by_unit + (depth + 128,), BF16),
            pltpu.VMEM((depth, 1024), BF16),
            pltpu.VMEM((256, depth + 128), BF16),
            pltpu.VMEM((4, 4, 3, UNIT, width), BF16),
            pltpu.VMEM((4, 3, UNIT, width), BF16),
            dma((7,)),
            dma,
            dma((GROUP, 4)),
            dma((2, 4)),
            dma((50,)),
            dma((50,)),
            dma((width // 256 * 3,)),
            dma,
            dma((4, 12)),
            dma((4, 3)),
        ],
        compiler_params=pltpu.CompilerParams(
            collective_id=0, has_side_effects=True, vmem_limit_bytes=VMEM_LIMIT
        ),
        name="layer_stage",
    )(
        tokens, layer_norm_gain[None, :], layer_norm_bias[None, :], input_bias[None, :],
        output_bias[None, :], jnp.stack([lengths, request_adapter]), slot_adapter,
        query_key_weight.reshape(width, QKV), up_weight, input_adapter_left,
        query_key_value_right.reshape(-1, QKV), up_adapter_right,
        output_adapter_left.reshape(HEAD, -1), down_adapter_left, output_weight.reshape(HEAD, width), down_weight,
        output_adapter_right,
    )


def solution(mesh):
    in_specs = (
        P(("req", "mlp"), None), P(), P(), P(None, "mlp", None), P("mlp", None, None), P(None, "mlp"), P("mlp"),
        P("mlp", None), P(), P(None, "mlp"), P(None, "mlp", None), P(None, "mlp"), P("mlp", None, None),
        P("mlp", None), P("mlp", None), P(), P(), P("mlp"),
    )
    return jax.shard_map(
        per_device, mesh=mesh, in_specs=in_specs, out_specs=P(("req", "mlp"), None), check_vma=False
    )
```

```python
import math

import jax
import jax.numpy as jnp
from jax import lax
from jax.experimental import pallas as pl
from jax.experimental.pallas import tpu as pltpu
from jax.sharding import PartitionSpec as P

HEAD = 256
ROT = 64
RANK = 16
EPSILON = 1e-05
NEGATIVE_FILL = -1e30
MESH = pl.DeviceIdType.MESH
F32 = jnp.float32
BF16 = jnp.bfloat16
VMEM_LIMIT = 63 * 1024 * 1024
SIDE = 4
GROUP = 16
UNIT = 16
QKV = 3 * HEAD
CUT = 96
LATE = 128


def dot(a, b):
    return jnp.dot(a, b, preferred_element_type=F32)


class Plane:
    def __init__(self):
        self.me = lax.axis_index("mlp")
        self.z = self.me // SIDE
        self.y = self.me % SIDE

    def at(self, dz, dy):
        return ((self.z + dz + SIDE) % SIDE) * SIDE + (self.y + dy + SIDE) % SIDE

    def off(self, half, d1, d2):
        return self.at(d1, d2) if half == 0 else self.at(d2, d1)

    def source(self, half, d1, d2):
        return self.off(half, -d1, -d2)


def barrier_all(me, count):
    sem = pltpu.get_barrier_semaphore()
    for k in range(1, count):
        pl.semaphore_signal(sem, inc=1, device_id={"mlp": (me + k) % count}, device_id_type=MESH)
    return sem


FARTHEST = sorted(
    ((dz, dy) for dz in (0, 1, -1, 2) for dy in (0, 1, -1, 2) if (dz, dy) != (0, 0)), key=lambda d: -abs(d[0]) - abs(d[1])
)


def exchange_start(plane, packed, landed, sems):
    me = plane.me
    for dz, dy in FARTHEST:
        to = plane.at(dz, dy)
        pltpu.make_async_remote_copy(
            packed.at[to], landed.at[me], sems.at[0], sems.at[1], device_id={"mlp": to}, device_id_type=MESH
        ).start()
    landed[me] = packed[me]


def exchange_middle(plane, landed, full, sems):
    me = plane.me
    many = landed.at[pl.ds(0, GROUP - 1)]
    pltpu.make_async_copy(many, many, sems.at[1]).wait()
    full[me] = jnp.sum(landed[...].astype(F32), axis=0).astype(BF16)
    for dz, dy in FARTHEST:
        pltpu.make_async_remote_copy(
            full.at[me], full.at[me], sems.at[2], sems.at[3], device_id={"mlp": plane.at(dz, dy)}, device_id_type=MESH
        ).start()


def exchange_end(landed, sems):
    many = landed.at[pl.ds(0, GROUP - 1)]
    for number in (3, 0, 2):
        pltpu.make_async_copy(many, many, sems.at[number]).wait()


GATHER_GROUPS = (
    tuple((h, d1, 0) for h in (0, 1) for d1 in (0, 1, -1, 2)),
    tuple((h, d1, d2) for h in (0, 1) for d1 in (0, 1) for d2 in (1, -1)),
    tuple((h, d1, d2) for h in (0, 1) for d1 in (-1, 2) for d2 in (1, -1)),
    tuple((h, d1, 2) for h in (0, 1) for d1 in (0, 1, -1, 2)),
)


REDUCE_GROUPS = (
    tuple((h, d1, 2) for h in (0, 1) for d1 in (2, 1, -1, 0)),
    tuple((h, d1, d2) for h in (0, 1) for d1 in (2, 1) for d2 in (1, -1)),
    tuple((h, d1, d2) for h in (0, 1) for d1 in (-1, 0) for d2 in (1, -1)),
    tuple((h, d1, 0) for h in (0, 1) for d1 in (2, 1, -1, 0)),
)
FAR = {2: 0, 1: 1, -1: 2, 0: 3}


def layer_kernel(
    tokens, gain, bias, in_bias, out_bias, lengths, request_adapter, slots, w_qkv, w_up, w_left, w_qkv_right, w_up_right,
    w_left_attn, w_left_hid, w_attn, w_down, w_right,
    out,
    xs, weights, right_qkv, right_up, rows_in, acc, picked, packed, landed, full,
    starts, adapter, row_index, row_start, row_adapter, names, cosine, sine, ranks, row_ranks, queries,
    early, late, pass_early, pass_late, top, total, summed,
    inputs, left, chosen_rows, from2, from1,
    load_sems, send_sem, recv_sems, ex_sems, near_send, near_recv, weight_sems, back_sem, sems2, sems1,
):
    plane = Plane()
    me = plane.me
    req = lax.axis_index("req")
    chip, core = req // 2, req % 2
    ahead = ((chip + 1) % SIDE) * 2 + core
    behind = ((chip + 3) % SIDE) * 2 + core
    other = chip * 2 + 1 - core
    hid = w_up.shape[1]
    count = GROUP * 64
    loads = [
        pltpu.make_async_copy(w_qkv, weights.at[:, pl.ds(0, QKV)], load_sems.at[0]),
        pltpu.make_async_copy(w_up, weights.at[:, pl.ds(QKV, hid)], load_sems.at[1]),
        pltpu.make_async_copy(w_left, weights.at[:, pl.ds(QKV + hid, 128)], load_sems.at[2]),
        pltpu.make_async_copy(w_qkv_right, right_qkv, load_sems.at[3]),
        pltpu.make_async_copy(w_up_right, right_up, load_sems.at[4]),
        pltpu.make_async_copy(w_left_attn, left.at[pl.ds(0, HEAD)], load_sems.at[5]),
        pltpu.make_async_copy(w_left_hid, left.at[pl.ds(HEAD, hid)], load_sems.at[6]),
    ]
    for load in loads:
        load.start()
    sem = barrier_all(me, GROUP)
    for device in (ahead, behind, other):
        pl.semaphore_signal(sem, inc=1, device_id={"req": device}, device_id_type=MESH)
    for part in range(0, 64, 16):
        values = tokens[part : part + 16, :].astype(F32)
        center = values - jnp.mean(values, axis=1, keepdims=True)
        spread = jnp.mean(center * center, axis=1, keepdims=True)
        scaled = center * lax.rsqrt(spread + EPSILON)
        xs[me, part : part + 16, :] = (scaled * gain[...] + bias[...]).astype(BF16)
    pl.semaphore_wait(sem, GROUP + 2)

    def send(slot, half, units, axis, step):
        first, many = units
        rows = pl.ds(half * 32 + first * UNIT, many * UNIT)
        to = plane.off(half, step, 0) if axis == 1 else plane.off(half, 0, step)
        pltpu.make_async_remote_copy(
            xs.at[slot, rows, :], xs.at[slot, rows, :], send_sem, recv_sems.at[slot, half * 2 + first],
            device_id={"mlp": to}, device_id_type=MESH,
        ).start()

    def landed_piece(half, d1, d2, units):
        first, many = units
        slot = plane.source(half, d1, d2)
        rows = pl.ds(half * 32 + first * UNIT, many * UNIT)
        view = xs.at[slot, rows, :]
        pltpu.make_async_copy(view, view, recv_sems.at[slot, half * 2 + first]).wait()
        return slot

    whole = (0, 2)
    for half in (0, 1):
        for step in (1, -1):
            send(me, half, whole, 1, step)
    for half in (0, 1):
        for step in (1, -1):
            send(me, half, whole, 2, step)

    long = lengths[...].reshape(1, -1).astype(F32)
    requests = long.shape[1]
    before = lax.broadcasted_iota(jnp.int32, (requests, requests), 0) < lax.broadcasted_iota(
        jnp.int32, (requests, requests), 1
    )
    begins = dot(jnp.broadcast_to(long, (8, requests)).astype(BF16), before.astype(F32).astype(BF16))[:1, :]
    ends = begins + long
    ids = request_adapter[...].reshape(1, -1).astype(F32)

    def locate(block, carry):
        rows = lax.broadcasted_iota(jnp.int32, (64, 1), 0)
        index = (req * count + block * 64 + rows).astype(F32)
        inside = jnp.logical_and(begins <= index, index < ends)
        start = jnp.sum(jnp.where(inside, begins, 0.0), axis=1, keepdims=True)
        mine = jnp.sum(jnp.where(inside, ids, 0.0), axis=1, keepdims=True)
        starts[block] = start.reshape(4, UNIT, 1)
        adapter[block] = mine.reshape(4, UNIT, 1)
        return carry

    lax.fori_loop(0, GROUP, locate, 0)

    def pieces(number):
        return [(i, plane.source(h, d1, d2), h) for i, (h, d1, d2) in enumerate(GATHER_GROUPS[number])]

    piece_row = lax.broadcasted_iota(jnp.int32, (32, 1), 0)
    piece_lane = lax.broadcasted_iota(jnp.int32, (1, 256), 1)
    for number in range(4):
        name = piece_lane
        for i, slot, half in pieces(number):
            at = slice(i * 32, (i + 1) * 32)
            first = slot * 64 + half * 32
            row_index[number, at, :] = (req * count + first + piece_row).astype(F32)
            row_start[number, at, :] = starts[slot, 2 * half : 2 * half + 2].reshape(32, 1)
            row_adapter[number, at, :] = adapter[slot, 2 * half : 2 * half + 2].reshape(32, 1)
            name = jnp.where(piece_lane // 32 == i, first + piece_lane % 32, name)
        names[:, number * 256 : (number + 1) * 256] = name.astype(F32)

    for half in (0, 1):
        for d1 in (1, -1):
            slot = landed_piece(half, d1, 0, whole)
            send(slot, half, (0, 1) if d1 == 1 else (1, 1), 1, d1)
            for step in (1, -1):
                send(slot, half, whole, 2, step)

    def relay(half, d1, d2, pieces):
        for units in pieces:
            slot = landed_piece(half, d1, d2, units)
        send(slot, half, (0, 1) if d2 == 1 else (1, 1), 2, d2)

    lane = lax.broadcasted_iota(jnp.int32, (1, 128), 1)
    even = lane % 2 == 0

    frequency = jnp.exp((lane // 2).astype(F32) * (-2.0 * math.log(10000.0) / ROT))

    def angles(number, carry):
        angle = (row_index[number] - row_start[number]) * frequency
        turned = lane < ROT
        cosine[number] = jnp.where(turned, jnp.cos(angle), 1.0)
        sine[number] = jnp.where(turned, jnp.where(even, -1.0, 1.0) * jnp.sin(angle), 0.0)
        return carry

    chosen = jnp.where(lane < 32, slots[0], jnp.where(lane < 64, slots[1], jnp.where(lane < 96, slots[2], slots[3])))
    chosen = chosen.astype(F32)

    def multiply(number):
        for i, slot, half in pieces(number):
            rows_in[i * 32 : (i + 1) * 32, :] = xs[slot, pl.ds(half * 32, 32), :]
        left = dot(rows_in[...], weights[:, QKV + hid :])
        kept = jnp.where(row_adapter[number] == chosen, left, 0.0).astype(BF16)
        for i, slot, half in pieces(number):
            picked[slot, 2 * half : 2 * half + 2] = kept[i * 32 : (i + 1) * 32, :].reshape(2, UNIT, 128)

    def multiply_wide(number, begin, end):
        def column(n, carry):
            columns = pl.ds(pl.multiple_of(n * 256, 256), 256)
            acc[number, :, columns] = dot(rows_in[...], weights[:, columns])
            return carry

        lax.fori_loop(begin, end, column, 0)

    low, high, every = pl.ds(0, CUT), pl.ds(CUT, 256 - CUT), pl.ds(0, 256)
    started = []

    def view(slot, part, rows=every):
        return early.at[slot, part, rows] if part < 4 else late.at[slot, :, rows]

    def pass_on(src, dst, number, device):
        copy = pltpu.make_async_remote_copy(
            src, dst, near_send.at[number], near_recv.at[number], device_id={"req": device}, device_id_type=MESH
        )
        copy.start()
        started.append(copy)

    def take(ref, number):
        pltpu.make_async_copy(ref, ref, near_recv.at[number]).wait()

    def by_way(part):
        return pass_early.at[part] if part < 4 else pass_late

    def near_sends(part):
        if part < 4:
            early[0, part] = acc[part, :, HEAD:QKV].astype(BF16)
        at = 10 * part
        pass_on(view(0, part, low), view(2, part, low), at, ahead)
        pass_on(view(0, part, high), by_way(part), at + 2, behind)
        pass_on(view(0, part, high), view(2, part, high), at + 1, ahead)
        pass_on(view(0, part), view(1 + 4 * core, part), at + 3, other)

    def near_low(part):
        at = 10 * part
        take(view(2, part, low), at)
        pass_on(view(2, part, low), view(4, part, low), at + 6, ahead)
        pass_on(view(2, part, low), view(3 - 2 * core, part, low), at + 4, other)

    def near_passing(part):
        at = 10 * part
        take(by_way(part), at + 2)
        pass_on(by_way(part), view(4, part, high), at + 7, behind)

    def near_high(part):
        at = 10 * part
        take(view(2, part, high), at + 1)
        pass_on(view(2, part, high), view(3 - 2 * core, part, high), at + 5, other)

    def near_relays(part):
        near_low(part)
        near_passing(part)
        near_high(part)

    def next_relays(part):
        at = 10 * part
        take(view(4, part, high), at + 7)
        pass_on(view(4, part, high), view(5 - 2 * core, part, high), at + 9, other)
        take(view(4, part, low), at + 6)
        pass_on(view(4, part, low), view(5 - 2 * core, part, low), at + 8, other)

    def take_all(slot, first, second=None):
        for part in range(5):
            if second is None:
                take(view(slot, part), 10 * part + first)
            else:
                take(view(slot, part, low), 10 * part + first)
                take(view(slot, part, high), 10 * part + second)

    tiles = (QKV + hid) // 256
    lax.fori_loop(0, 2, angles, 0)
    for half in (0, 1):
        for d2 in (1, -1):
            relay(half, 0, d2, (whole,))
    for half in (0, 1):
        for unit in ((0, 1), (1, 1)):
            slot = landed_piece(half, 2, 0, unit)
            for step in (1, -1):
                send(slot, half, unit, 2, step)
    for load in loads[:3]:
        load.wait()
    multiply(0)
    multiply_wide(0, 0, tiles)
    near_sends(0)
    for half in (0, 1):
        for d1 in (1, -1):
            for d2 in (1, -1):
                relay(half, d1, d2, (whole,))
    multiply(1)
    multiply_wide(1, 0, tiles)
    near_sends(1)
    near_low(0)
    near_passing(0)
    lax.fori_loop(2, 4, angles, 0)
    for half in (0, 1):
        for d2 in (1, -1):
            relay(half, 2, d2, ((0, 1), (1, 1)))
    near_high(0)
    multiply(2)
    multiply_wide(2, 0, tiles)
    near_sends(2)
    near_relays(1)
    for half in (0, 1):
        for d1 in (0, 1, -1, 2):
            for unit in ((0, 1), (1, 1)):
                landed_piece(half, d1, 2, unit)
    multiply(3)

    row_id = lax.broadcasted_iota(jnp.int32, (128, 128), 0)
    col_id = lax.broadcasted_iota(jnp.int32, (128, 128), 1)
    together = jnp.zeros((256, 128), F32)
    for unit in range(4):
        fold = jnp.logical_and(col_id // 32 == unit, row_id % 32 == col_id % 32).astype(F32).astype(BF16)
        together = together + dot(picked[:, unit].reshape(256, 128), fold)
    packed[0] = together.astype(BF16).reshape(GROUP, UNIT, 128)
    exchange_start(plane, packed.at[0], landed.at[0], ex_sems.at[0])
    multiply_wide(3, 1, 3)
    near_sends(3)
    exchange_middle(plane, landed.at[0], full.at[0], ex_sems.at[0])
    multiply_wide(3, 0, 1)
    multiply_wide(3, 3, tiles)
    near_relays(2)
    next_relays(0)
    for load in loads[3:]:
        load.wait()
    exchange_end(landed.at[0], ex_sems.at[0])
    for unit in range(4):
        spread = jnp.logical_and(row_id - unit * 32 == col_id - 64, row_id // 32 == unit).astype(F32).astype(BF16)
        ranks[:, unit] = dot(full[0].reshape(256, 128), spread).astype(BF16).reshape(GROUP, UNIT, 128)
    for number in range(4):
        for i, slot, half in pieces(number):
            row_ranks[number, i * 32 : (i + 1) * 32, :] = ranks[slot, 2 * half : 2 * half + 2].reshape(32, 128)

    owner = (lax.broadcasted_iota(jnp.int32, (1, 1024), 1) // RANK).astype(F32)
    spread_row = lax.broadcasted_iota(jnp.int32, (128, 1024), 0)
    spread_col = lax.broadcasted_iota(jnp.int32, (128, 1024), 1)
    fold_row = lax.broadcasted_iota(jnp.int32, (1024, 128), 0)
    fold_col = lax.broadcasted_iota(jnp.int32, (1024, 128), 1)

    def widened(values, mine, first):
        spread = (spread_row == 64 + first + spread_col % RANK).astype(F32).astype(BF16)
        return jnp.where(mine, dot(values, spread), 0.0).astype(BF16)

    def turn(head, number):
        swapped = jnp.where(even, pltpu.roll(head, 127, 1), pltpu.roll(head, 1, 1))
        return head * cosine[number] + swapped * sine[number]

    def wide_of(number):
        return rows_in.at[:, pl.ds(pl.multiple_of(number * 1024, 1024), 1024)]

    def late_keys(number, carry):
        own = row_ranks[number]
        wide = widened(own, row_adapter[number] == owner, 0)
        wide_of(number)[...] = wide
        key = acc[number, :, HEAD : HEAD + 128] + dot(wide, right_qkv[:, HEAD : HEAD + 128])
        late[0, number] = jnp.where(lane < ROT, turn(key, number), own.astype(F32)).astype(BF16)
        return carry

    def query_rows(number, carry):
        query = acc[number, :, :HEAD] + dot(wide_of(number)[...], right_qkv[:, :HEAD])
        scale = jnp.asarray(HEAD ** (-0.5), BF16)
        first = turn(query[:, :128], number).astype(BF16) * scale
        second = query[:, 128:].astype(BF16) * scale
        main = jnp.concatenate([jnp.where(lane < ROT, 0.0, first.astype(F32)).astype(BF16), second], axis=1)
        back = lax.dot_general(
            main, right_qkv[:, HEAD : 2 * HEAD], (((1,), (1,)), ((), ())), preferred_element_type=F32
        )
        fold = (fold_col == 64 + fold_row % RANK).astype(F32).astype(BF16)
        low_rank = dot(jnp.where(row_adapter[number] == owner, back, 0.0).astype(BF16), fold)
        queries[number, :, :HEAD] = main
        queries[number, :, HEAD:] = jnp.where(lane < ROT, first.astype(F32), low_rank).astype(BF16)
        return carry

    lax.fori_loop(0, 4, late_keys, 0)
    near_sends(4)
    lax.fori_loop(0, 4, query_rows, 0)

    def finish_hidden(number):
        wide = widened(row_ranks[number], row_adapter[number] == owner, RANK)
        for part in range(hid // 256):
            columns = slice(part * 256, (part + 1) * 256)
            value = acc[number, :, QKV + part * 256 : QKV + (part + 1) * 256]
            value = value + dot(wide, right_up[:, columns]) + in_bias[:, columns]
            value = jax.nn.gelu(value, approximate=True).astype(BF16)
            for i, slot, half in pieces(number):
                inputs[slot, 2 * half : 2 * half + 2, :, HEAD + part * 256 : HEAD + (part + 1) * 256] = value[
                    i * 32 : (i + 1) * 32, :
                ].reshape(2, UNIT, 256)

    def attend_all(slot, own=False):
        def body(b, carry):
            tail = late[slot].reshape(count, LATE)
            keys = jnp.concatenate([early[slot, :, :, :HEAD].reshape(count, HEAD), tail], axis=1)
            values = jnp.concatenate([early[slot, :, :, HEAD:].reshape(count, HEAD), tail], axis=1)
            scores = lax.dot_general(queries[b], keys, (((1,), (1,)), ((), ())), preferred_element_type=F32)
            key_id = names[...] + ((req - slot) * count).astype(F32)
            allowed = key_id >= row_start[b]
            if own:
                allowed = jnp.logical_and(allowed, key_id <= row_index[b])
            scores = jnp.where(allowed, scores, NEGATIVE_FILL)
            peak = jnp.max(scores, axis=1, keepdims=True)
            if own:
                kept = jnp.exp(scores - peak)
                total[b] = jnp.sum(kept, axis=1, keepdims=True)
                summed[b] = dot(kept.astype(BF16), values)
            else:
                old = top[b]
                peak = jnp.maximum(old, peak)
                kept = jnp.exp(scores - peak)
                decay = jnp.exp(old - peak)
                total[b] = total[b] * decay + jnp.sum(kept, axis=1, keepdims=True)
                summed[b] = summed[b] * decay + dot(kept.astype(BF16), values)
            top[b] = peak
            return carry

        lax.fori_loop(0, 4, body, 0)

    def attend_on(which, slot):
        @pl.when(core == which)
        def _():
            attend_all(slot)

    depth = HEAD + hid
    width = out.shape[1]
    deep = depth + 128
    stored = []

    def store_weights():
        for n in range(width // 1024):
            for j, (ref, first, size) in enumerate(((w_attn, 0, HEAD), (w_down, HEAD, hid), (w_right, depth, 128))):
                copy = pltpu.make_async_copy(
                    ref.at[:, pl.ds(n * 1024, 1024)], weights.at[pl.ds(n * deep + first, size), pl.ds(0, 1024)],
                    weight_sems.at[n * 3 + j],
                )
                copy.start()
                stored.append(copy)

    def lower(unit, first, begin, end):
        mine = adapter[:, unit].reshape(256, 1) == owner
        product = dot(inputs[:, unit, :, begin:end].reshape(256, end - begin), left[begin:end, :])
        fold = (fold_col == unit * 32 + first + fold_row % RANK).astype(F32).astype(BF16)
        return dot(jnp.where(mine, product, 0.0).astype(BF16), fold)

    near_relays(3)
    next_relays(1)
    near_low(4)
    finish_hidden(0)
    finish_hidden(1)
    near_passing(4)
    next_relays(2)
    attend_all(0, True)
    next_relays(3)
    take_all(5 - 4 * core, 3)
    attend_on(1, 1)
    store_weights()
    near_high(4)
    attend_all(2)
    next_relays(4)
    take_all(1 + 2 * core, 4, 5)
    attend_all(1 + 2 * core)
    attend_all(4)
    finish_hidden(2)
    finish_hidden(3)
    together = lax.fori_loop(0, 4, lambda unit, sum_: sum_ + lower(unit, RANK, HEAD, depth), jnp.zeros((256, 128), F32))
    take_all(3 + 2 * core, 8, 9)
    attend_on(0, 3)
    for number in range(4):
        share = 1.0 / total[number]
        tail = (summed[number, :, HEAD:] * share).astype(BF16)
        wide = widened(tail, row_adapter[number] == owner, 0)
        value = (summed[number, :, :HEAD] * share + dot(wide, right_qkv[:, 2 * HEAD :])).astype(BF16)
        for i, slot, half in pieces(number):
            inputs[slot, 2 * half : 2 * half + 2, :, :HEAD] = value[i * 32 : (i + 1) * 32, :].reshape(2, UNIT, HEAD)
    for unit in range(4):
        together = together + lower(unit, 0, 0, HEAD)
    packed[1] = together.astype(BF16).reshape(GROUP, UNIT, 128)
    exchange_start(plane, packed.at[1], landed.at[1], ex_sems.at[1])
    for copy in started:
        copy.wait_send()
    sent = xs.at[pl.ds(0, GROUP - 1)]
    pltpu.make_async_copy(sent, sent, send_sem).wait()
    for copy in stored:
        copy.wait()

    def back_weights(n, first, size):
        return weights[pl.ds(pl.multiple_of(n // 4 * deep + first, 128), size), pl.ds(pl.multiple_of(n % 4 * 256, 256), 256)]

    def base(n, carry):
        acc[n % 4, :, pl.ds(pl.multiple_of(n // 4 * 256, 256), 256)] = dot(
            chosen_rows[:, :depth], back_weights(n, 0, depth)
        )
        return carry

    for i, (half, d1, d2) in enumerate(REDUCE_GROUPS[0]):
        slot = plane.source(half, d1, d2)
        chosen_rows[i * 32 : (i + 1) * 32, :depth] = inputs[slot, 2 * half : 2 * half + 2, :, :depth].reshape(32, depth)
    tiles = width // 256
    lax.fori_loop(0, tiles // 2, base, 0)
    exchange_middle(plane, landed.at[1], full.at[1], ex_sems.at[1])
    lax.fori_loop(tiles // 2, tiles, base, 0)
    exchange_end(landed.at[1], ex_sems.at[1])
    held = (me * 4 + lane // 32).astype(F32)
    for unit in range(4):
        mine = adapter[:, unit].reshape(256, 1) == held
        spread = (row_id == unit * 32 + col_id % 32).astype(F32).astype(BF16)
        wide = jnp.where(mine, dot(full[1].reshape(256, 128), spread), 0.0).astype(BF16)
        inputs[:, unit, :, depth:] = wide.reshape(GROUP, UNIT, 128)

    def first_group():
        for i, (half, d1, d2) in enumerate(REDUCE_GROUPS[0]):
            slot = plane.source(half, d1, d2)
            chosen_rows[i * 32 : (i + 1) * 32, depth:] = inputs[slot, 2 * half : 2 * half + 2, :, depth:].reshape(32, 128)

        def column(n, carry):
            columns = pl.ds(pl.multiple_of(n * 256, 256), 256)
            result = dot(chosen_rows[:, depth:], back_weights(n, depth, 128))
            result = (result + acc[n % 4, :, pl.ds(pl.multiple_of(n // 4 * 256, 256), 256)]).astype(BF16)
            for i, (half, d1, d2) in enumerate(REDUCE_GROUPS[0]):
                xs[plane.source(half, d1, d2), pl.ds(half * 32, 32), columns] = result[i * 32 : (i + 1) * 32, :]
            return carry

        lax.fori_loop(0, width // 256, column, 0)

    def multiply_back(number):
        for i, (half, d1, d2) in enumerate(REDUCE_GROUPS[number]):
            slot = plane.source(half, d1, d2)
            chosen_rows[i * 32 : (i + 1) * 32, :] = inputs[slot, 2 * half : 2 * half + 2].reshape(32, deep)

        def column(n, carry):
            columns = pl.ds(pl.multiple_of(n * 256, 256), 256)
            result = dot(chosen_rows[...], back_weights(n, 0, deep)).astype(BF16)
            for i, (half, d1, d2) in enumerate(REDUCE_GROUPS[number]):
                xs[plane.source(half, d1, d2), pl.ds(half * 32, 32), columns] = result[i * 32 : (i + 1) * 32, :]
            return carry

        lax.fori_loop(0, width // 256, column, 0)

    def unit_rows(half, u):
        return pl.ds(half * 32 + u * UNIT, UNIT)

    def landing(half, axis, side, d1, place):
        index = half * 2 + side
        if axis == 2:
            return from2.at[index, FAR[d1], place], sems2.at[index, FAR[d1] * 3 + place]
        return from1.at[index, place], sems1.at[index, place]

    def send_back(half, d1, d2, u, axis):
        d = d2 if axis == 2 else d1
        back = d if d != 2 else (1 if u == 0 else -1)
        side = 0 if back == 1 else 1
        place = 2 if d == 2 else u
        slot = plane.source(half, d1, d2)
        to = plane.off(half, 0, -back) if axis == 2 else plane.off(half, -back, 0)
        target, arrived = landing(half, axis, side, d1, place)
        pltpu.make_async_remote_copy(
            xs.at[slot, unit_rows(half, u), :], target, back_sem, arrived, device_id={"mlp": to}, device_id_type=MESH
        ).start()

    def arrive_back(half, axis, side, d1, place):
        ref, arrived = landing(half, axis, side, d1, place)
        pltpu.make_async_copy(ref, ref, arrived).wait()
        return ref

    def add(half, d1, d2, u, children):
        refs = [arrive_back(half, axis, side, d1, place) for axis, side, place in children]
        slot = plane.source(half, d1, d2)
        here = xs.at[slot, unit_rows(half, u), :]
        value = here[...].astype(F32)
        for ref in refs:
            value = value + ref[...].astype(F32)
        here[...] = value.astype(BF16)

    first_group()
    for d1 in (2, 1, -1, 0):
        for half in (0, 1):
            for u in (0, 1):
                send_back(half, d1, 2, u, 2)
    for number in (1, 2):
        multiply_back(number)
        for half, d1, d2 in REDUCE_GROUPS[number]:
            send_back(half, d1, d2, 1 if d2 == 1 else 0, 2)
    for number in (1, 2):
        for half, d1, d2 in REDUCE_GROUPS[number]:
            u = 0 if d2 == 1 else 1
            add(half, d1, d2, u, ((2, 0 if d2 == 1 else 1, 2),))
            send_back(half, d1, d2, u, 2)
    multiply_back(3)
    both = lambda u: ((2, 0, u), (2, 1, u))
    for half in (0, 1):
        for u in (0, 1):
            add(half, 2, 0, u, both(u))
            send_back(half, 2, 0, u, 1)
    for d1 in (1, -1):
        for half in (0, 1):
            u = 1 if d1 == 1 else 0
            add(half, d1, 0, u, both(u))
            send_back(half, d1, 0, u, 1)
    for d1 in (1, -1):
        for half in (0, 1):
            u = 0 if d1 == 1 else 1
            add(half, d1, 0, u, both(u) + ((1, 0 if d1 == 1 else 1, 2),))
            send_back(half, d1, 0, u, 1)
    for half in (0, 1):
        for u in (0, 1):
            refs = [arrive_back(half, axis, side, 0, place) for axis, side, place in both(u) + ((1, 0, u), (1, 1, u))]
            rows = unit_rows(half, u)
            value = xs[me, rows, :].astype(F32)
            for ref in refs:
                value = value + ref[...].astype(F32)
            out[rows, :] = (value + tokens[rows, :].astype(F32) + out_bias[...]).astype(BF16)
    sent = xs.at[pl.ds(0, GROUP - 1)]
    pltpu.make_async_copy(sent, sent, back_sem).wait()


def per_device(
    tokens, layer_norm_gain, layer_norm_bias, query_key_weight, output_weight, up_weight, input_bias, down_weight,
    output_bias, input_adapter_left, query_key_value_right, up_adapter_right, output_adapter_left, down_adapter_left,
    output_adapter_right, lengths, request_adapter, slot_adapter,
):
    rows, width = tokens.shape
    hid = up_weight.shape[1]
    vmem = pl.BlockSpec(memory_space=pltpu.VMEM)
    smem = pl.BlockSpec(memory_space=pltpu.SMEM)
    anywhere = pl.BlockSpec(memory_space=pl.ANY)
    dma = pltpu.SemaphoreType.DMA
    by_unit = (GROUP, 4, UNIT)
    depth = HEAD + hid
    return pl.pallas_call(
        layer_kernel,
        out_shape=jax.ShapeDtypeStruct((rows, width), BF16),
        in_specs=[vmem] * 7 + [smem] + [anywhere] * 10,
        out_specs=vmem,
        scratch_shapes=[
            pltpu.VMEM((GROUP, rows, width), BF16),
            pltpu.VMEM((width, QKV + hid + 128), BF16),
            pltpu.VMEM(query_key_value_right.shape[:1] + (QKV,), BF16),
            pltpu.VMEM(up_adapter_right.shape, BF16),
            pltpu.VMEM((256, width), BF16),
            pltpu.VMEM((4, 256, QKV + hid), F32),
            pltpu.VMEM(by_unit + (128,), BF16),
            pltpu.VMEM((2, GROUP, UNIT, 128), BF16),
            pltpu.VMEM((2, GROUP, UNIT, 128), BF16),
            pltpu.VMEM((2, GROUP, UNIT, 128), BF16),
            pltpu.VMEM(by_unit + (1,), F32),
            pltpu.VMEM(by_unit + (1,), F32),
            pltpu.VMEM((4, 256, 1), F32),
            pltpu.VMEM((4, 256, 1), F32),
            pltpu.VMEM((4, 256, 1), F32),
            pltpu.VMEM((1, 1024), F32),
            pltpu.VMEM((4, 256, 128), F32),
            pltpu.VMEM((4, 256, 128), F32),
            pltpu.VMEM(by_unit + (128,), BF16),
            pltpu.VMEM((4, 256, 128), BF16),
            pltpu.VMEM((4, 256, HEAD + LATE), BF16),
            pltpu.VMEM((6, 4, 256, 2 * HEAD), BF16),
            pltpu.VMEM((6, 4, 256, LATE), BF16),
            pltpu.VMEM((4, 256 - CUT, 2 * HEAD), BF16),
            pltpu.VMEM((4, 256 - CUT, LATE), BF16),
            pltpu.VMEM((4, 256, 1), F32),
            pltpu.VMEM((4, 256, 1), F32),
            pltpu.VMEM((4, 256, HEAD + LATE), F32),
            pltpu.VMEM(by_unit + (depth + 128,), BF16),
            pltpu.VMEM((depth, 1024), BF16),
            pltpu.VMEM((256, depth + 128), BF16),
            pltpu.VMEM((4, 4, 3, UNIT, width), BF16),
            pltpu.VMEM((4, 3, UNIT, width), BF16),
            dma((7,)),
            dma,
            dma((GROUP, 4)),
            dma((2, 4)),
            dma((50,)),
            dma((50,)),
            dma((width // 1024 * 3,)),
            dma,
            dma((4, 12)),
            dma((4, 3)),
        ],
        compiler_params=pltpu.CompilerParams(
            collective_id=0, has_side_effects=True, vmem_limit_bytes=VMEM_LIMIT
        ),
        name="layer_stage",
    )(
        tokens, layer_norm_gain[None, :], layer_norm_bias[None, :], input_bias[None, :],
        output_bias[None, :], lengths, request_adapter, slot_adapter,
        query_key_weight.reshape(width, QKV), up_weight, input_adapter_left,
        query_key_value_right.reshape(-1, QKV), up_adapter_right,
        output_adapter_left.reshape(HEAD, -1), down_adapter_left, output_weight.reshape(HEAD, width), down_weight,
        output_adapter_right,
    )


def solution(mesh):
    in_specs = (
        P(("req", "mlp"), None), P(), P(), P(None, "mlp", None), P("mlp", None, None), P(None, "mlp"), P("mlp"),
        P("mlp", None), P(), P(None, "mlp"), P(None, "mlp", None), P(None, "mlp"), P("mlp", None, None),
        P("mlp", None), P("mlp", None), P(), P(), P("mlp"),
    )
    return jax.shard_map(
        per_device, mesh=mesh, in_specs=in_specs, out_specs=P(("req", "mlp"), None), check_vma=False
    )
```

```python
import math

import jax
import jax.numpy as jnp
from jax import lax
from jax.experimental import pallas as pl
from jax.experimental.pallas import tpu as pltpu
from jax.sharding import PartitionSpec as P

HEAD = 256
ROT = 64
RANK = 16
EPSILON = 1e-05
NEGATIVE_FILL = -1e30
MESH = pl.DeviceIdType.MESH
F32 = jnp.float32
BF16 = jnp.bfloat16
VMEM_LIMIT = 63 * 1024 * 1024
SIDE = 4
GROUP = 16
UNIT = 16
QKV = 3 * HEAD
CUT = 96
LATE = 128


def dot(a, b):
    return jnp.dot(a, b, preferred_element_type=F32)


class Plane:
    def __init__(self):
        self.me = lax.axis_index("mlp")
        self.z = self.me // SIDE
        self.y = self.me % SIDE

    def at(self, dz, dy):
        return ((self.z + dz + SIDE) % SIDE) * SIDE + (self.y + dy + SIDE) % SIDE

    def off(self, half, d1, d2):
        return self.at(d1, d2) if half == 0 else self.at(d2, d1)

    def source(self, half, d1, d2):
        return self.off(half, -d1, -d2)


def barrier_all(me, count):
    sem = pltpu.get_barrier_semaphore()
    for k in range(1, count):
        pl.semaphore_signal(sem, inc=1, device_id={"mlp": (me + k) % count}, device_id_type=MESH)
    return sem


FARTHEST = sorted(
    ((dz, dy) for dz in (0, 1, -1, 2) for dy in (0, 1, -1, 2) if (dz, dy) != (0, 0)), key=lambda d: -abs(d[0]) - abs(d[1])
)


def exchange_start(plane, packed, landed, sems):
    me = plane.me
    for dz, dy in FARTHEST:
        to = plane.at(dz, dy)
        pltpu.make_async_remote_copy(
            packed.at[to], landed.at[me], sems.at[0], sems.at[1], device_id={"mlp": to}, device_id_type=MESH
        ).start()
    landed[me] = packed[me]


def exchange_middle(plane, landed, full, sems):
    me = plane.me
    many = landed.at[pl.ds(0, GROUP - 1)]
    pltpu.make_async_copy(many, many, sems.at[1]).wait()
    full[me] = jnp.sum(landed[...].astype(F32), axis=0).astype(BF16)
    for dz, dy in FARTHEST:
        pltpu.make_async_remote_copy(
            full.at[me], full.at[me], sems.at[2], sems.at[3], device_id={"mlp": plane.at(dz, dy)}, device_id_type=MESH
        ).start()


def exchange_end(landed, sems):
    many = landed.at[pl.ds(0, GROUP - 1)]
    for number in (3, 0, 2):
        pltpu.make_async_copy(many, many, sems.at[number]).wait()


GATHER_GROUPS = (
    tuple((h, d1, 0) for h in (0, 1) for d1 in (0, 1, -1, 2)),
    tuple((h, d1, d2) for h in (0, 1) for d1 in (0, 1) for d2 in (1, -1)),
    tuple((h, d1, d2) for h in (0, 1) for d1 in (-1, 2) for d2 in (1, -1)),
    tuple((h, d1, 2) for h in (0, 1) for d1 in (0, 1, -1, 2)),
)


REDUCE_GROUPS = (
    tuple((h, d1, 2) for h in (0, 1) for d1 in (2, 1, -1, 0)),
    tuple((h, d1, d2) for h in (0, 1) for d1 in (2, 1) for d2 in (1, -1)),
    tuple((h, d1, d2) for h in (0, 1) for d1 in (-1, 0) for d2 in (1, -1)),
    tuple((h, d1, 0) for h in (0, 1) for d1 in (2, 1, -1, 0)),
)
FAR = {2: 0, 1: 1, -1: 2, 0: 3}


def layer_kernel(
    tokens, gain, bias, in_bias, out_bias, lengths, request_adapter, slots, w_qkv, w_up, w_left, w_qkv_right, w_up_right,
    w_left_attn, w_left_hid, w_attn, w_down, w_right,
    out,
    xs, weights, right_qkv, right_up, rows_in, acc, picked, packed, landed, full,
    starts, adapter, row_index, row_start, row_adapter, names, cosine, sine, ranks, row_ranks, queries,
    early, late, pass_early, pass_late, top, total, summed,
    inputs, left, chosen_rows, from2, from1,
    load_sems, send_sem, recv_sems, ex_sems, near_send, near_recv, weight_sems, back_sem, sems2, sems1,
):
    plane = Plane()
    me = plane.me
    req = lax.axis_index("req")
    chip, core = req // 2, req % 2
    ahead = ((chip + 1) % SIDE) * 2 + core
    behind = ((chip + 3) % SIDE) * 2 + core
    other = chip * 2 + 1 - core
    hid = w_up.shape[1]
    count = GROUP * 64
    loads = [
        pltpu.make_async_copy(w_qkv, weights.at[:, pl.ds(0, QKV)], load_sems.at[0]),
        pltpu.make_async_copy(w_up, weights.at[:, pl.ds(QKV, hid)], load_sems.at[1]),
        pltpu.make_async_copy(w_left, weights.at[:, pl.ds(QKV + hid, 128)], load_sems.at[2]),
        pltpu.make_async_copy(w_qkv_right, right_qkv, load_sems.at[3]),
        pltpu.make_async_copy(w_up_right, right_up, load_sems.at[4]),
        pltpu.make_async_copy(w_left_attn, left.at[pl.ds(0, HEAD)], load_sems.at[5]),
        pltpu.make_async_copy(w_left_hid, left.at[pl.ds(HEAD, hid)], load_sems.at[6]),
    ]
    for load in loads:
        load.start()
    sem = barrier_all(me, GROUP)
    for device in (ahead, behind, other):
        pl.semaphore_signal(sem, inc=1, device_id={"req": device}, device_id_type=MESH)
    for part in range(0, 64, 16):
        values = tokens[part : part + 16, :].astype(F32)
        center = values - jnp.mean(values, axis=1, keepdims=True)
        spread = jnp.mean(center * center, axis=1, keepdims=True)
        scaled = center * lax.rsqrt(spread + EPSILON)
        xs[me, part : part + 16, :] = (scaled * gain[...] + bias[...]).astype(BF16)
    pl.semaphore_wait(sem, GROUP + 2)

    def send(slot, half, units, axis, step):
        first, many = units
        rows = pl.ds(half * 32 + first * UNIT, many * UNIT)
        to = plane.off(half, step, 0) if axis == 1 else plane.off(half, 0, step)
        pltpu.make_async_remote_copy(
            xs.at[slot, rows, :], xs.at[slot, rows, :], send_sem, recv_sems.at[slot, half * 2 + first],
            device_id={"mlp": to}, device_id_type=MESH,
        ).start()

    def landed_piece(half, d1, d2, units):
        first, many = units
        slot = plane.source(half, d1, d2)
        rows = pl.ds(half * 32 + first * UNIT, many * UNIT)
        view = xs.at[slot, rows, :]
        pltpu.make_async_copy(view, view, recv_sems.at[slot, half * 2 + first]).wait()
        return slot

    whole = (0, 2)
    for half in (0, 1):
        for step in (1, -1):
            send(me, half, whole, 1, step)
    for half in (0, 1):
        for step in (1, -1):
            send(me, half, whole, 2, step)

    long = lengths[...].reshape(1, -1).astype(F32)
    requests = long.shape[1]
    before = lax.broadcasted_iota(jnp.int32, (requests, requests), 0) < lax.broadcasted_iota(
        jnp.int32, (requests, requests), 1
    )
    begins = dot(jnp.broadcast_to(long, (8, requests)).astype(BF16), before.astype(F32).astype(BF16))[:1, :]
    ends = begins + long
    ids = request_adapter[...].reshape(1, -1).astype(F32)

    def locate(block, carry):
        rows = lax.broadcasted_iota(jnp.int32, (64, 1), 0)
        index = (req * count + block * 64 + rows).astype(F32)
        inside = jnp.logical_and(begins <= index, index < ends)
        start = jnp.sum(jnp.where(inside, begins, 0.0), axis=1, keepdims=True)
        mine = jnp.sum(jnp.where(inside, ids, 0.0), axis=1, keepdims=True)
        starts[block] = start.reshape(4, UNIT, 1)
        adapter[block] = mine.reshape(4, UNIT, 1)
        return carry

    lax.fori_loop(0, GROUP, locate, 0)

    def pieces(number):
        return [(i, plane.source(h, d1, d2), h) for i, (h, d1, d2) in enumerate(GATHER_GROUPS[number])]

    piece_row = lax.broadcasted_iota(jnp.int32, (32, 1), 0)
    piece_lane = lax.broadcasted_iota(jnp.int32, (1, 256), 1)
    for number in range(4):
        name = piece_lane
        for i, slot, half in pieces(number):
            at = slice(i * 32, (i + 1) * 32)
            first = slot * 64 + half * 32
            row_index[number, at, :] = (req * count + first + piece_row).astype(F32)
            row_start[number, at, :] = starts[slot, 2 * half : 2 * half + 2].reshape(32, 1)
            row_adapter[number, at, :] = adapter[slot, 2 * half : 2 * half + 2].reshape(32, 1)
            name = jnp.where(piece_lane // 32 == i, first + piece_lane % 32, name)
        names[:, number * 256 : (number + 1) * 256] = name.astype(F32)

    for half in (0, 1):
        for d1 in (1, -1):
            slot = landed_piece(half, d1, 0, whole)
            send(slot, half, (0, 1) if d1 == 1 else (1, 1), 1, d1)
            for step in (1, -1):
                send(slot, half, whole, 2, step)

    def relay(half, d1, d2, pieces):
        for units in pieces:
            slot = landed_piece(half, d1, d2, units)
        send(slot, half, (0, 1) if d2 == 1 else (1, 1), 2, d2)

    lane = lax.broadcasted_iota(jnp.int32, (1, 128), 1)
    even = lane % 2 == 0

    frequency = jnp.exp((lane // 2).astype(F32) * (-2.0 * math.log(10000.0) / ROT))

    def angles(number, carry):
        angle = (row_index[number] - row_start[number]) * frequency
        turned = lane < ROT
        cosine[number] = jnp.where(turned, jnp.cos(angle), 1.0)
        sine[number] = jnp.where(turned, jnp.where(even, -1.0, 1.0) * jnp.sin(angle), 0.0)
        return carry

    chosen = jnp.where(lane < 32, slots[0], jnp.where(lane < 64, slots[1], jnp.where(lane < 96, slots[2], slots[3])))
    chosen = chosen.astype(F32)

    def multiply(number):
        for i, slot, half in pieces(number):
            rows_in[i * 32 : (i + 1) * 32, :] = xs[slot, pl.ds(half * 32, 32), :]
        left = dot(rows_in[...], weights[:, QKV + hid :])
        kept = jnp.where(row_adapter[number] == chosen, left, 0.0).astype(BF16)
        for i, slot, half in pieces(number):
            picked[slot, 2 * half : 2 * half + 2] = kept[i * 32 : (i + 1) * 32, :].reshape(2, UNIT, 128)

    def multiply_wide(number, begin, end):
        def column(n, carry):
            columns = pl.ds(pl.multiple_of(n * 256, 256), 256)
            acc[number, :, columns] = dot(rows_in[...], weights[:, columns])
            return carry

        lax.fori_loop(begin, end, column, 0)

    low, high, every = pl.ds(0, CUT), pl.ds(CUT, 256 - CUT), pl.ds(0, 256)
    started = []

    def view(slot, part, rows=every):
        return early.at[slot, part, rows] if part < 4 else late.at[slot, :, rows]

    def pass_on(src, dst, number, device):
        copy = pltpu.make_async_remote_copy(
            src, dst, near_send.at[number], near_recv.at[number], device_id={"req": device}, device_id_type=MESH
        )
        copy.start()
        started.append(copy)

    def take(ref, number):
        pltpu.make_async_copy(ref, ref, near_recv.at[number]).wait()

    def by_way(part):
        return pass_early.at[part] if part < 4 else pass_late

    def near_sends(part):
        if part < 4:
            early[0, part] = acc[part, :, HEAD:QKV].astype(BF16)
        at = 10 * part
        pass_on(view(0, part, low), view(2, part, low), at, ahead)
        pass_on(view(0, part, high), by_way(part), at + 2, behind)
        pass_on(view(0, part, high), view(2, part, high), at + 1, ahead)
        pass_on(view(0, part), view(1 + 4 * core, part), at + 3, other)

    def near_low(part):
        at = 10 * part
        take(view(2, part, low), at)
        pass_on(view(2, part, low), view(4, part, low), at + 6, ahead)
        pass_on(view(2, part, low), view(3 - 2 * core, part, low), at + 4, other)

    def near_passing(part):
        at = 10 * part
        take(by_way(part), at + 2)
        pass_on(by_way(part), view(4, part, high), at + 7, behind)

    def near_high(part):
        at = 10 * part
        take(view(2, part, high), at + 1)
        pass_on(view(2, part, high), view(3 - 2 * core, part, high), at + 5, other)

    def near_relays(part):
        near_low(part)
        near_passing(part)
        near_high(part)

    def next_relays(part):
        at = 10 * part
        take(view(4, part, high), at + 7)
        pass_on(view(4, part, high), view(5 - 2 * core, part, high), at + 9, other)
        take(view(4, part, low), at + 6)
        pass_on(view(4, part, low), view(5 - 2 * core, part, low), at + 8, other)

    def take_all(slot, first, second=None):
        for part in range(5):
            if second is None:
                take(view(slot, part), 10 * part + first)
            else:
                take(view(slot, part, low), 10 * part + first)
                take(view(slot, part, high), 10 * part + second)

    tiles = (QKV + hid) // 256
    lax.fori_loop(0, 2, angles, 0)
    for half in (0, 1):
        for d2 in (1, -1):
            relay(half, 0, d2, (whole,))
    for half in (0, 1):
        for unit in ((0, 1), (1, 1)):
            slot = landed_piece(half, 2, 0, unit)
            for step in (1, -1):
                send(slot, half, unit, 2, step)
    for load in loads[:3]:
        load.wait()
    multiply(0)
    multiply_wide(0, 0, tiles)
    near_sends(0)
    for half in (0, 1):
        for d1 in (1, -1):
            for d2 in (1, -1):
                relay(half, d1, d2, (whole,))
    multiply(1)
    multiply_wide(1, 0, tiles)
    near_sends(1)
    near_low(0)
    near_passing(0)
    lax.fori_loop(2, 4, angles, 0)
    for half in (0, 1):
        for d2 in (1, -1):
            relay(half, 2, d2, ((0, 1), (1, 1)))
    near_high(0)
    multiply(2)
    multiply_wide(2, 0, tiles)
    near_sends(2)
    near_relays(1)
    for half in (0, 1):
        for d1 in (0, 1, -1, 2):
            for unit in ((0, 1), (1, 1)):
                landed_piece(half, d1, 2, unit)
    multiply(3)

    row_id = lax.broadcasted_iota(jnp.int32, (128, 128), 0)
    col_id = lax.broadcasted_iota(jnp.int32, (128, 128), 1)
    together = jnp.zeros((256, 128), F32)
    for unit in range(4):
        fold = jnp.logical_and(col_id // 32 == unit, row_id % 32 == col_id % 32).astype(F32).astype(BF16)
        together = together + dot(picked[:, unit].reshape(256, 128), fold)
    packed[0] = together.astype(BF16).reshape(GROUP, UNIT, 128)
    exchange_start(plane, packed.at[0], landed.at[0], ex_sems.at[0])
    multiply_wide(3, 1, 3)
    near_sends(3)
    exchange_middle(plane, landed.at[0], full.at[0], ex_sems.at[0])
    multiply_wide(3, 0, 1)
    multiply_wide(3, 3, tiles)
    near_relays(2)
    next_relays(0)
    for load in loads[3:]:
        load.wait()
    exchange_end(landed.at[0], ex_sems.at[0])
    for unit in range(4):
        spread = jnp.logical_and(row_id - unit * 32 == col_id - 64, row_id // 32 == unit).astype(F32).astype(BF16)
        ranks[:, unit] = dot(full[0].reshape(256, 128), spread).astype(BF16).reshape(GROUP, UNIT, 128)
    for number in range(4):
        for i, slot, half in pieces(number):
            row_ranks[number, i * 32 : (i + 1) * 32, :] = ranks[slot, 2 * half : 2 * half + 2].reshape(32, 128)

    owner = (lax.broadcasted_iota(jnp.int32, (1, 1024), 1) // RANK).astype(F32)
    spread_row = lax.broadcasted_iota(jnp.int32, (128, 1024), 0)
    spread_col = lax.broadcasted_iota(jnp.int32, (128, 1024), 1)
    fold_row = lax.broadcasted_iota(jnp.int32, (1024, 128), 0)
    fold_col = lax.broadcasted_iota(jnp.int32, (1024, 128), 1)

    def widened(values, mine, first):
        spread = (spread_row == 64 + first + spread_col % RANK).astype(F32).astype(BF16)
        return jnp.where(mine, dot(values, spread), 0.0).astype(BF16)

    def turn(head, number):
        swapped = jnp.where(even, pltpu.roll(head, 127, 1), pltpu.roll(head, 1, 1))
        return head * cosine[number] + swapped * sine[number]

    def wide_of(number):
        return rows_in.at[:, pl.ds(pl.multiple_of(number * 1024, 1024), 1024)]

    def late_keys(number, carry):
        own = row_ranks[number]
        wide = widened(own, row_adapter[number] == owner, 0)
        wide_of(number)[...] = wide
        key = acc[number, :, HEAD : HEAD + 128] + dot(wide, right_qkv[:, HEAD : HEAD + 128])
        late[0, number] = jnp.where(lane < ROT, turn(key, number), own.astype(F32)).astype(BF16)
        return carry

    def query_rows(number, carry):
        query = acc[number, :, :HEAD] + dot(wide_of(number)[...], right_qkv[:, :HEAD])
        scale = jnp.asarray(HEAD ** (-0.5), BF16)
        first = turn(query[:, :128], number).astype(BF16) * scale
        second = query[:, 128:].astype(BF16) * scale
        main = jnp.concatenate([jnp.where(lane < ROT, 0.0, first.astype(F32)).astype(BF16), second], axis=1)
        back = lax.dot_general(
            main, right_qkv[:, HEAD : 2 * HEAD], (((1,), (1,)), ((), ())), preferred_element_type=F32
        )
        fold = (fold_col == 64 + fold_row % RANK).astype(F32).astype(BF16)
        low_rank = dot(jnp.where(row_adapter[number] == owner, back, 0.0).astype(BF16), fold)
        queries[number, :, :HEAD] = main
        queries[number, :, HEAD:] = jnp.where(lane < ROT, first.astype(F32), low_rank).astype(BF16)
        return carry

    lax.fori_loop(0, 4, late_keys, 0)
    near_sends(4)
    lax.fori_loop(0, 4, query_rows, 0)

    def finish_hidden(number):
        wide = widened(row_ranks[number], row_adapter[number] == owner, RANK)
        for part in range(hid // 256):
            columns = slice(part * 256, (part + 1) * 256)
            value = acc[number, :, QKV + part * 256 : QKV + (part + 1) * 256]
            value = value + dot(wide, right_up[:, columns]) + in_bias[:, columns]
            value = jax.nn.gelu(value, approximate=True).astype(BF16)
            for i, slot, half in pieces(number):
                inputs[slot, 2 * half : 2 * half + 2, :, HEAD + part * 256 : HEAD + (part + 1) * 256] = value[
                    i * 32 : (i + 1) * 32, :
                ].reshape(2, UNIT, 256)

    def attend_all(slot, own=False):
        def body(pair, carry):
            tail = late[slot].reshape(count, LATE)
            keys = jnp.concatenate([early[slot, :, :, :HEAD].reshape(count, HEAD), tail], axis=1)
            values = jnp.concatenate([early[slot, :, :, HEAD:].reshape(count, HEAD), tail], axis=1)
            key_id = names[...] + ((req - slot) * count).astype(F32)
            blocks = (pair * 2, pair * 2 + 1)
            scores = [
                lax.dot_general(queries[b], keys, (((1,), (1,)), ((), ())), preferred_element_type=F32) for b in blocks
            ]
            results = []
            for b, score in zip(blocks, scores):
                allowed = key_id >= row_start[b]
                if own:
                    allowed = jnp.logical_and(allowed, key_id <= row_index[b])
                score = jnp.where(allowed, score, NEGATIVE_FILL)
                peak = jnp.max(score, axis=1, keepdims=True)
                if not own:
                    peak = jnp.maximum(top[b], peak)
                kept = jnp.exp(score - peak)
                results.append((peak, jnp.sum(kept, axis=1, keepdims=True), dot(kept.astype(BF16), values)))
            for b, (peak, part, product) in zip(blocks, results):
                if not own:
                    decay = jnp.exp(top[b] - peak)
                    part = part + total[b] * decay
                    product = product + summed[b] * decay
                top[b] = peak
                total[b] = part
                summed[b] = product
            return carry

        lax.fori_loop(0, 2, body, 0)

    def attend_on(which, slot):
        @pl.when(core == which)
        def _():
            attend_all(slot)

    depth = HEAD + hid
    width = out.shape[1]
    deep = depth + 128
    stored = []

    def store_weights():
        for n in range(width // 1024):
            for j, (ref, first, size) in enumerate(((w_attn, 0, HEAD), (w_down, HEAD, hid), (w_right, depth, 128))):
                copy = pltpu.make_async_copy(
                    ref.at[:, pl.ds(n * 1024, 1024)], weights.at[pl.ds(n * deep + first, size), pl.ds(0, 1024)],
                    weight_sems.at[n * 3 + j],
                )
                copy.start()
                stored.append(copy)

    def lower(unit, first, begin, end):
        mine = adapter[:, unit].reshape(256, 1) == owner
        product = dot(inputs[:, unit, :, begin:end].reshape(256, end - begin), left[begin:end, :])
        fold = (fold_col == unit * 32 + first + fold_row % RANK).astype(F32).astype(BF16)
        return dot(jnp.where(mine, product, 0.0).astype(BF16), fold)

    near_relays(3)
    next_relays(1)
    near_low(4)
    finish_hidden(0)
    finish_hidden(1)
    near_passing(4)
    next_relays(2)
    attend_all(0, True)
    next_relays(3)
    take_all(5 - 4 * core, 3)
    attend_on(1, 1)
    store_weights()
    near_high(4)
    attend_all(2)
    next_relays(4)
    take_all(1 + 2 * core, 4, 5)
    attend_all(1 + 2 * core)
    attend_all(4)
    finish_hidden(2)
    finish_hidden(3)
    together = lax.fori_loop(0, 4, lambda unit, sum_: sum_ + lower(unit, RANK, HEAD, depth), jnp.zeros((256, 128), F32))
    take_all(3 + 2 * core, 8, 9)
    attend_on(0, 3)
    for number in range(4):
        share = 1.0 / total[number]
        tail = (summed[number, :, HEAD:] * share).astype(BF16)
        wide = widened(tail, row_adapter[number] == owner, 0)
        value = (summed[number, :, :HEAD] * share + dot(wide, right_qkv[:, 2 * HEAD :])).astype(BF16)
        for i, slot, half in pieces(number):
            inputs[slot, 2 * half : 2 * half + 2, :, :HEAD] = value[i * 32 : (i + 1) * 32, :].reshape(2, UNIT, HEAD)
    for unit in range(4):
        together = together + lower(unit, 0, 0, HEAD)
    packed[1] = together.astype(BF16).reshape(GROUP, UNIT, 128)
    exchange_start(plane, packed.at[1], landed.at[1], ex_sems.at[1])
    for copy in started:
        copy.wait_send()
    sent = xs.at[pl.ds(0, GROUP - 1)]
    pltpu.make_async_copy(sent, sent, send_sem).wait()
    for copy in stored:
        copy.wait()

    def back_weights(n, first, size):
        return weights[pl.ds(pl.multiple_of(n // 4 * deep + first, 128), size), pl.ds(pl.multiple_of(n % 4 * 256, 256), 256)]

    def base(n, carry):
        acc[n % 4, :, pl.ds(pl.multiple_of(n // 4 * 256, 256), 256)] = dot(
            chosen_rows[:, :depth], back_weights(n, 0, depth)
        )
        return carry

    for i, (half, d1, d2) in enumerate(REDUCE_GROUPS[0]):
        slot = plane.source(half, d1, d2)
        chosen_rows[i * 32 : (i + 1) * 32, :depth] = inputs[slot, 2 * half : 2 * half + 2, :, :depth].reshape(32, depth)
    tiles = width // 256
    lax.fori_loop(0, tiles // 2, base, 0)
    exchange_middle(plane, landed.at[1], full.at[1], ex_sems.at[1])
    lax.fori_loop(tiles // 2, tiles, base, 0)
    exchange_end(landed.at[1], ex_sems.at[1])
    held = (me * 4 + lane // 32).astype(F32)
    for unit in range(4):
        mine = adapter[:, unit].reshape(256, 1) == held
        spread = (row_id == unit * 32 + col_id % 32).astype(F32).astype(BF16)
        wide = jnp.where(mine, dot(full[1].reshape(256, 128), spread), 0.0).astype(BF16)
        inputs[:, unit, :, depth:] = wide.reshape(GROUP, UNIT, 128)

    def first_group():
        for i, (half, d1, d2) in enumerate(REDUCE_GROUPS[0]):
            slot = plane.source(half, d1, d2)
            chosen_rows[i * 32 : (i + 1) * 32, depth:] = inputs[slot, 2 * half : 2 * half + 2, :, depth:].reshape(32, 128)

        def column(n, carry):
            columns = pl.ds(pl.multiple_of(n * 256, 256), 256)
            result = dot(chosen_rows[:, depth:], back_weights(n, depth, 128))
            result = (result + acc[n % 4, :, pl.ds(pl.multiple_of(n // 4 * 256, 256), 256)]).astype(BF16)
            for i, (half, d1, d2) in enumerate(REDUCE_GROUPS[0]):
                xs[plane.source(half, d1, d2), pl.ds(half * 32, 32), columns] = result[i * 32 : (i + 1) * 32, :]
            return carry

        lax.fori_loop(0, width // 256, column, 0)

    def multiply_back(number):
        for i, (half, d1, d2) in enumerate(REDUCE_GROUPS[number]):
            slot = plane.source(half, d1, d2)
            chosen_rows[i * 32 : (i + 1) * 32, :] = inputs[slot, 2 * half : 2 * half + 2].reshape(32, deep)

        def column(n, carry):
            columns = pl.ds(pl.multiple_of(n * 256, 256), 256)
            result = dot(chosen_rows[...], back_weights(n, 0, deep)).astype(BF16)
            for i, (half, d1, d2) in enumerate(REDUCE_GROUPS[number]):
                xs[plane.source(half, d1, d2), pl.ds(half * 32, 32), columns] = result[i * 32 : (i + 1) * 32, :]
            return carry

        lax.fori_loop(0, width // 256, column, 0)

    def unit_rows(half, u):
        return pl.ds(half * 32 + u * UNIT, UNIT)

    def landing(half, axis, side, d1, place):
        index = half * 2 + side
        if axis == 2:
            return from2.at[index, FAR[d1], place], sems2.at[index, FAR[d1] * 3 + place]
        return from1.at[index, place], sems1.at[index, place]

    def send_back(half, d1, d2, u, axis):
        d = d2 if axis == 2 else d1
        back = d if d != 2 else (1 if u == 0 else -1)
        side = 0 if back == 1 else 1
        place = 2 if d == 2 else u
        slot = plane.source(half, d1, d2)
        to = plane.off(half, 0, -back) if axis == 2 else plane.off(half, -back, 0)
        target, arrived = landing(half, axis, side, d1, place)
        pltpu.make_async_remote_copy(
            xs.at[slot, unit_rows(half, u), :], target, back_sem, arrived, device_id={"mlp": to}, device_id_type=MESH
        ).start()

    def arrive_back(half, axis, side, d1, place):
        ref, arrived = landing(half, axis, side, d1, place)
        pltpu.make_async_copy(ref, ref, arrived).wait()
        return ref

    def add(half, d1, d2, u, children):
        refs = [arrive_back(half, axis, side, d1, place) for axis, side, place in children]
        slot = plane.source(half, d1, d2)
        here = xs.at[slot, unit_rows(half, u), :]
        value = here[...].astype(F32)
        for ref in refs:
            value = value + ref[...].astype(F32)
        here[...] = value.astype(BF16)

    first_group()
    for d1 in (2, 1, -1, 0):
        for half in (0, 1):
            for u in (0, 1):
                send_back(half, d1, 2, u, 2)
    for number in (1, 2):
        multiply_back(number)
        for half, d1, d2 in REDUCE_GROUPS[number]:
            send_back(half, d1, d2, 1 if d2 == 1 else 0, 2)
    for number in (1, 2):
        for half, d1, d2 in REDUCE_GROUPS[number]:
            u = 0 if d2 == 1 else 1
            add(half, d1, d2, u, ((2, 0 if d2 == 1 else 1, 2),))
            send_back(half, d1, d2, u, 2)
    multiply_back(3)
    both = lambda u: ((2, 0, u), (2, 1, u))
    for half in (0, 1):
        for u in (0, 1):
            add(half, 2, 0, u, both(u))
            send_back(half, 2, 0, u, 1)
    for d1 in (1, -1):
        for half in (0, 1):
            u = 1 if d1 == 1 else 0
            add(half, d1, 0, u, both(u))
            send_back(half, d1, 0, u, 1)
    for d1 in (1, -1):
        for half in (0, 1):
            u = 0 if d1 == 1 else 1
            add(half, d1, 0, u, both(u) + ((1, 0 if d1 == 1 else 1, 2),))
            send_back(half, d1, 0, u, 1)
    for half in (0, 1):
        for u in (0, 1):
            refs = [arrive_back(half, axis, side, 0, place) for axis, side, place in both(u) + ((1, 0, u), (1, 1, u))]
            rows = unit_rows(half, u)
            value = xs[me, rows, :].astype(F32)
            for ref in refs:
                value = value + ref[...].astype(F32)
            out[rows, :] = (value + tokens[rows, :].astype(F32) + out_bias[...]).astype(BF16)
    sent = xs.at[pl.ds(0, GROUP - 1)]
    pltpu.make_async_copy(sent, sent, back_sem).wait()


def per_device(
    tokens, layer_norm_gain, layer_norm_bias, query_key_weight, output_weight, up_weight, input_bias, down_weight,
    output_bias, input_adapter_left, query_key_value_right, up_adapter_right, output_adapter_left, down_adapter_left,
    output_adapter_right, lengths, request_adapter, slot_adapter,
):
    rows, width = tokens.shape
    hid = up_weight.shape[1]
    vmem = pl.BlockSpec(memory_space=pltpu.VMEM)
    smem = pl.BlockSpec(memory_space=pltpu.SMEM)
    anywhere = pl.BlockSpec(memory_space=pl.ANY)
    dma = pltpu.SemaphoreType.DMA
    by_unit = (GROUP, 4, UNIT)
    depth = HEAD + hid
    return pl.pallas_call(
        layer_kernel,
        out_shape=jax.ShapeDtypeStruct((rows, width), BF16),
        in_specs=[vmem] * 7 + [smem] + [anywhere] * 10,
        out_specs=vmem,
        scratch_shapes=[
            pltpu.VMEM((GROUP, rows, width), BF16),
            pltpu.VMEM((width, QKV + hid + 128), BF16),
            pltpu.VMEM(query_key_value_right.shape[:1] + (QKV,), BF16),
            pltpu.VMEM(up_adapter_right.shape, BF16),
            pltpu.VMEM((256, width), BF16),
            pltpu.VMEM((4, 256, QKV + hid), F32),
            pltpu.VMEM(by_unit + (128,), BF16),
            pltpu.VMEM((2, GROUP, UNIT, 128), BF16),
            pltpu.VMEM((2, GROUP, UNIT, 128), BF16),
            pltpu.VMEM((2, GROUP, UNIT, 128), BF16),
            pltpu.VMEM(by_unit + (1,), F32),
            pltpu.VMEM(by_unit + (1,), F32),
            pltpu.VMEM((4, 256, 1), F32),
            pltpu.VMEM((4, 256, 1), F32),
            pltpu.VMEM((4, 256, 1), F32),
            pltpu.VMEM((1, 1024), F32),
            pltpu.VMEM((4, 256, 128), F32),
            pltpu.VMEM((4, 256, 128), F32),
            pltpu.VMEM(by_unit + (128,), BF16),
            pltpu.VMEM((4, 256, 128), BF16),
            pltpu.VMEM((4, 256, HEAD + LATE), BF16),
            pltpu.VMEM((6, 4, 256, 2 * HEAD), BF16),
            pltpu.VMEM((6, 4, 256, LATE), BF16),
            pltpu.VMEM((4, 256 - CUT, 2 * HEAD), BF16),
            pltpu.VMEM((4, 256 - CUT, LATE), BF16),
            pltpu.VMEM((4, 256, 1), F32),
            pltpu.VMEM((4, 256, 1), F32),
            pltpu.VMEM((4, 256, HEAD + LATE), F32),
            pltpu.VMEM(by_unit + (depth + 128,), BF16),
            pltpu.VMEM((depth, 1024), BF16),
            pltpu.VMEM((256, depth + 128), BF16),
            pltpu.VMEM((4, 4, 3, UNIT, width), BF16),
            pltpu.VMEM((4, 3, UNIT, width), BF16),
            dma((7,)),
            dma,
            dma((GROUP, 4)),
            dma((2, 4)),
            dma((50,)),
            dma((50,)),
            dma((width // 1024 * 3,)),
            dma,
            dma((4, 12)),
            dma((4, 3)),
        ],
        compiler_params=pltpu.CompilerParams(
            collective_id=0, has_side_effects=True, vmem_limit_bytes=VMEM_LIMIT
        ),
        name="layer_stage",
    )(
        tokens, layer_norm_gain[None, :], layer_norm_bias[None, :], input_bias[None, :],
        output_bias[None, :], lengths, request_adapter, slot_adapter,
        query_key_weight.reshape(width, QKV), up_weight, input_adapter_left,
        query_key_value_right.reshape(-1, QKV), up_adapter_right,
        output_adapter_left.reshape(HEAD, -1), down_adapter_left, output_weight.reshape(HEAD, width), down_weight,
        output_adapter_right,
    )


def solution(mesh):
    in_specs = (
        P(("req", "mlp"), None), P(), P(), P(None, "mlp", None), P("mlp", None, None), P(None, "mlp"), P("mlp"),
        P("mlp", None), P(), P(None, "mlp"), P(None, "mlp", None), P(None, "mlp"), P("mlp", None, None),
        P("mlp", None), P("mlp", None), P(), P(), P("mlp"),
    )
    return jax.shard_map(
        per_device, mesh=mesh, in_specs=in_specs, out_specs=P(("req", "mlp"), None), check_vma=False
    )
```

```python
import math

import jax
import jax.numpy as jnp
from jax import lax
from jax.experimental import pallas as pl
from jax.experimental.pallas import tpu as pltpu
from jax.sharding import PartitionSpec as P

HEAD = 256
ROT = 64
RANK = 16
EPSILON = 1e-05
NEGATIVE_FILL = -1e30
MESH = pl.DeviceIdType.MESH
F32 = jnp.float32
BF16 = jnp.bfloat16
VMEM_LIMIT = 63 * 1024 * 1024
SIDE = 4
GROUP = 16
UNIT = 16
QKV = 3 * HEAD
CUT = 96
LATE = 128


def dot(a, b):
    return jnp.dot(a, b, preferred_element_type=F32)


class Plane:
    def __init__(self):
        self.me = lax.axis_index("mlp")
        self.z = self.me // SIDE
        self.y = self.me % SIDE

    def at(self, dz, dy):
        return ((self.z + dz + SIDE) % SIDE) * SIDE + (self.y + dy + SIDE) % SIDE

    def off(self, half, d1, d2):
        return self.at(d1, d2) if half == 0 else self.at(d2, d1)

    def source(self, half, d1, d2):
        return self.off(half, -d1, -d2)


FARTHEST = sorted(
    ((dz, dy) for dz in (0, 1, -1, 2) for dy in (0, 1, -1, 2) if (dz, dy) != (0, 0)), key=lambda d: -abs(d[0]) - abs(d[1])
)


def exchange_start(plane, packed, landed, sems):
    me = plane.me
    for dz, dy in FARTHEST:
        to = plane.at(dz, dy)
        pltpu.make_async_remote_copy(
            packed.at[to], landed.at[me], sems.at[0], sems.at[1], device_id={"mlp": to}, device_id_type=MESH
        ).start()
    landed[me] = packed[me]


def exchange_middle(plane, landed, full, sems):
    me = plane.me
    many = landed.at[pl.ds(0, GROUP - 1)]
    pltpu.make_async_copy(many, many, sems.at[1]).wait()
    full[me] = jnp.sum(landed[...].astype(F32), axis=0).astype(BF16)
    for dz, dy in FARTHEST:
        pltpu.make_async_remote_copy(
            full.at[me], full.at[me], sems.at[2], sems.at[3], device_id={"mlp": plane.at(dz, dy)}, device_id_type=MESH
        ).start()


def exchange_end(landed, sems):
    many = landed.at[pl.ds(0, GROUP - 1)]
    for number in (3, 0, 2):
        pltpu.make_async_copy(many, many, sems.at[number]).wait()


GATHER_GROUPS = (
    tuple((h, d1, 0) for h in (0, 1) for d1 in (0, 1, -1, 2)),
    tuple((h, d1, d2) for h in (0, 1) for d1 in (0, 1) for d2 in (1, -1)),
    tuple((h, d1, d2) for h in (0, 1) for d1 in (-1, 2) for d2 in (1, -1)),
    tuple((h, d1, 2) for h in (0, 1) for d1 in (0, 1, -1, 2)),
)


REDUCE_GROUPS = (
    tuple((h, d1, 2) for h in (0, 1) for d1 in (2, 1, -1, 0)),
    tuple((h, d1, d2) for h in (0, 1) for d1 in (2, 1) for d2 in (1, -1)),
    tuple((h, d1, d2) for h in (0, 1) for d1 in (-1, 0) for d2 in (1, -1)),
    tuple((h, d1, 0) for h in (0, 1) for d1 in (2, 1, -1, 0)),
)
FAR = {2: 0, 1: 1, -1: 2, 0: 3}


def layer_kernel(
    tokens, gain, bias, in_bias, out_bias, lengths, request_adapter, slots, w_qkv, w_up, w_left, w_qkv_right, w_up_right,
    w_left_attn, w_left_hid, w_attn, w_down, w_right,
    out,
    xs, weights, right_qkv, right_up, rows_in, acc, picked, packed, landed, full,
    starts, adapter, row_index, row_start, row_adapter, names, cosine, sine, ranks, row_ranks, queries,
    early, late, pass_early, pass_late, top, total, summed,
    inputs, left, chosen_rows, from2, from1,
    load_sems, send_sem, recv_sems, ex_sems, near_send, near_recv, weight_sems, back_sem, sems2, sems1,
):
    plane = Plane()
    me = plane.me
    req = lax.axis_index("req")
    chip, core = req // 2, req % 2
    ahead = ((chip + 1) % SIDE) * 2 + core
    behind = ((chip + 3) % SIDE) * 2 + core
    other = chip * 2 + 1 - core
    hid = w_up.shape[1]
    count = GROUP * 64
    loads = [
        pltpu.make_async_copy(w_qkv, weights.at[:, pl.ds(0, QKV)], load_sems.at[0]),
        pltpu.make_async_copy(w_up, weights.at[:, pl.ds(QKV, hid)], load_sems.at[1]),
        pltpu.make_async_copy(w_left, weights.at[:, pl.ds(QKV + hid, 128)], load_sems.at[2]),
        pltpu.make_async_copy(w_qkv_right, right_qkv, load_sems.at[3]),
        pltpu.make_async_copy(w_up_right, right_up, load_sems.at[4]),
        pltpu.make_async_copy(w_left_attn, left.at[pl.ds(0, HEAD)], load_sems.at[5]),
        pltpu.make_async_copy(w_left_hid, left.at[pl.ds(HEAD, hid)], load_sems.at[6]),
    ]
    for load in loads:
        load.start()
    sem = pltpu.get_barrier_semaphore()
    for dz, dy in ((1, 0), (-1, 0), (0, 1), (0, -1)):
        pl.semaphore_signal(sem, inc=1, device_id={"mlp": plane.at(dz, dy)}, device_id_type=MESH)
    for device in (ahead, behind, other):
        pl.semaphore_signal(sem, inc=1, device_id={"req": device}, device_id_type=MESH)
    for part in range(0, 64, 16):
        values = tokens[part : part + 16, :].astype(F32)
        center = values - jnp.mean(values, axis=1, keepdims=True)
        spread = jnp.mean(center * center, axis=1, keepdims=True)
        scaled = center * lax.rsqrt(spread + EPSILON)
        xs[me, part : part + 16, :] = (scaled * gain[...] + bias[...]).astype(BF16)
    pl.semaphore_wait(sem, 7)

    def send(slot, half, units, axis, step):
        first, many = units
        rows = pl.ds(half * 32 + first * UNIT, many * UNIT)
        to = plane.off(half, step, 0) if axis == 1 else plane.off(half, 0, step)
        pltpu.make_async_remote_copy(
            xs.at[slot, rows, :], xs.at[slot, rows, :], send_sem, recv_sems.at[slot, half * 2 + first],
            device_id={"mlp": to}, device_id_type=MESH,
        ).start()

    def landed_piece(half, d1, d2, units):
        first, many = units
        slot = plane.source(half, d1, d2)
        rows = pl.ds(half * 32 + first * UNIT, many * UNIT)
        view = xs.at[slot, rows, :]
        pltpu.make_async_copy(view, view, recv_sems.at[slot, half * 2 + first]).wait()
        return slot

    whole = (0, 2)
    for half in (0, 1):
        for step in (1, -1):
            send(me, half, whole, 1, step)
    for half in (0, 1):
        for step in (1, -1):
            send(me, half, whole, 2, step)

    long = lengths[...].reshape(1, -1).astype(F32)
    requests = long.shape[1]
    before = lax.broadcasted_iota(jnp.int32, (requests, requests), 0) < lax.broadcasted_iota(
        jnp.int32, (requests, requests), 1
    )
    begins = dot(jnp.broadcast_to(long, (8, requests)).astype(BF16), before.astype(F32).astype(BF16))[:1, :]
    ends = begins + long
    ids = request_adapter[...].reshape(1, -1).astype(F32)

    def locate(block, carry):
        rows = lax.broadcasted_iota(jnp.int32, (64, 1), 0)
        index = (req * count + block * 64 + rows).astype(F32)
        inside = jnp.logical_and(begins <= index, index < ends)
        start = jnp.sum(jnp.where(inside, begins, 0.0), axis=1, keepdims=True)
        mine = jnp.sum(jnp.where(inside, ids, 0.0), axis=1, keepdims=True)
        starts[block] = start.reshape(4, UNIT, 1)
        adapter[block] = mine.reshape(4, UNIT, 1)
        return carry

    lax.fori_loop(0, GROUP, locate, 0)

    def pieces(number):
        return [(i, plane.source(h, d1, d2), h) for i, (h, d1, d2) in enumerate(GATHER_GROUPS[number])]

    piece_row = lax.broadcasted_iota(jnp.int32, (32, 1), 0)
    piece_lane = lax.broadcasted_iota(jnp.int32, (1, 256), 1)
    for number in range(4):
        name = piece_lane
        for i, slot, half in pieces(number):
            at = slice(i * 32, (i + 1) * 32)
            first = slot * 64 + half * 32
            row_index[number, at, :] = (req * count + first + piece_row).astype(F32)
            row_start[number, at, :] = starts[slot, 2 * half : 2 * half + 2].reshape(32, 1)
            row_adapter[number, at, :] = adapter[slot, 2 * half : 2 * half + 2].reshape(32, 1)
            name = jnp.where(piece_lane // 32 == i, first + piece_lane % 32, name)
        names[:, number * 256 : (number + 1) * 256] = name.astype(F32)

    for half in (0, 1):
        for d1 in (1, -1):
            slot = landed_piece(half, d1, 0, whole)
            send(slot, half, (0, 1) if d1 == 1 else (1, 1), 1, d1)
            for step in (1, -1):
                send(slot, half, whole, 2, step)

    def relay(half, d1, d2, pieces):
        for units in pieces:
            slot = landed_piece(half, d1, d2, units)
        send(slot, half, (0, 1) if d2 == 1 else (1, 1), 2, d2)

    lane = lax.broadcasted_iota(jnp.int32, (1, 128), 1)
    even = lane % 2 == 0

    frequency = jnp.exp((lane // 2).astype(F32) * (-2.0 * math.log(10000.0) / ROT))

    def angles(number, carry):
        angle = (row_index[number] - row_start[number]) * frequency
        turned = lane < ROT
        cosine[number] = jnp.where(turned, jnp.cos(angle), 1.0)
        sine[number] = jnp.where(turned, jnp.where(even, -1.0, 1.0) * jnp.sin(angle), 0.0)
        return carry

    chosen = jnp.where(lane < 32, slots[0], jnp.where(lane < 64, slots[1], jnp.where(lane < 96, slots[2], slots[3])))
    chosen = chosen.astype(F32)

    def multiply(number):
        for i, slot, half in pieces(number):
            rows_in[i * 32 : (i + 1) * 32, :] = xs[slot, pl.ds(half * 32, 32), :]
        left = dot(rows_in[...], weights[:, QKV + hid :])
        kept = jnp.where(row_adapter[number] == chosen, left, 0.0).astype(BF16)
        for i, slot, half in pieces(number):
            picked[slot, 2 * half : 2 * half + 2] = kept[i * 32 : (i + 1) * 32, :].reshape(2, UNIT, 128)

    def multiply_wide(number, begin, end):
        def column(n, carry):
            columns = pl.ds(pl.multiple_of(n * 256, 256), 256)
            acc[number, :, columns] = dot(rows_in[...], weights[:, columns])
            return carry

        lax.fori_loop(begin, end, column, 0)

    low, high, every = pl.ds(0, CUT), pl.ds(CUT, 256 - CUT), pl.ds(0, 256)
    started = []

    def view(slot, part, rows=every):
        return early.at[slot, part, rows] if part < 4 else late.at[slot, :, rows]

    def pass_on(src, dst, number, device):
        copy = pltpu.make_async_remote_copy(
            src, dst, near_send.at[number], near_recv.at[number], device_id={"req": device}, device_id_type=MESH
        )
        copy.start()
        started.append(copy)

    def take(ref, number):
        pltpu.make_async_copy(ref, ref, near_recv.at[number]).wait()

    def by_way(part):
        return pass_early.at[part] if part < 4 else pass_late

    def near_sends(part):
        if part < 4:
            early[0, part] = acc[part, :, HEAD:QKV].astype(BF16)
        at = 10 * part
        pass_on(view(0, part, low), view(2, part, low), at, ahead)
        pass_on(view(0, part, high), by_way(part), at + 2, behind)
        pass_on(view(0, part, high), view(2, part, high), at + 1, ahead)
        pass_on(view(0, part), view(1 + 4 * core, part), at + 3, other)

    def near_low(part):
        at = 10 * part
        take(view(2, part, low), at)
        pass_on(view(2, part, low), view(4, part, low), at + 6, ahead)
        pass_on(view(2, part, low), view(3 - 2 * core, part, low), at + 4, other)

    def near_passing(part):
        at = 10 * part
        take(by_way(part), at + 2)
        pass_on(by_way(part), view(4, part, high), at + 7, behind)

    def near_high(part):
        at = 10 * part
        take(view(2, part, high), at + 1)
        pass_on(view(2, part, high), view(3 - 2 * core, part, high), at + 5, other)

    def near_relays(part):
        near_low(part)
        near_passing(part)
        near_high(part)

    def next_relays(part):
        at = 10 * part
        take(view(4, part, high), at + 7)
        pass_on(view(4, part, high), view(5 - 2 * core, part, high), at + 9, other)
        take(view(4, part, low), at + 6)
        pass_on(view(4, part, low), view(5 - 2 * core, part, low), at + 8, other)

    def take_all(slot, first, second=None):
        for part in range(5):
            if second is None:
                take(view(slot, part), 10 * part + first)
            else:
                take(view(slot, part, low), 10 * part + first)
                take(view(slot, part, high), 10 * part + second)

    tiles = (QKV + hid) // 256
    lax.fori_loop(0, 2, angles, 0)
    for half in (0, 1):
        for d2 in (1, -1):
            relay(half, 0, d2, (whole,))
    for half in (0, 1):
        for unit in ((0, 1), (1, 1)):
            slot = landed_piece(half, 2, 0, unit)
            for step in (1, -1):
                send(slot, half, unit, 2, step)
    for load in loads[:3]:
        load.wait()
    multiply(0)
    multiply_wide(0, 0, tiles)
    near_sends(0)
    for half in (0, 1):
        for d1 in (1, -1):
            for d2 in (1, -1):
                relay(half, d1, d2, (whole,))
    multiply(1)
    multiply_wide(1, 0, tiles)
    near_sends(1)
    near_low(0)
    near_passing(0)
    lax.fori_loop(2, 4, angles, 0)
    for half in (0, 1):
        for d2 in (1, -1):
            relay(half, 2, d2, ((0, 1), (1, 1)))
    near_high(0)
    multiply(2)
    multiply_wide(2, 0, tiles)
    near_sends(2)
    near_relays(1)
    for half in (0, 1):
        for d1 in (0, 1, -1, 2):
            for unit in ((0, 1), (1, 1)):
                landed_piece(half, d1, 2, unit)
    multiply(3)

    row_id = lax.broadcasted_iota(jnp.int32, (128, 128), 0)
    col_id = lax.broadcasted_iota(jnp.int32, (128, 128), 1)
    together = jnp.zeros((256, 128), F32)
    for unit in range(4):
        fold = jnp.logical_and(col_id // 32 == unit, row_id % 32 == col_id % 32).astype(F32).astype(BF16)
        together = together + dot(picked[:, unit].reshape(256, 128), fold)
    packed[0] = together.astype(BF16).reshape(GROUP, UNIT, 128)
    exchange_start(plane, packed.at[0], landed.at[0], ex_sems.at[0])
    multiply_wide(3, 1, 3)
    near_sends(3)
    exchange_middle(plane, landed.at[0], full.at[0], ex_sems.at[0])
    multiply_wide(3, 0, 1)
    multiply_wide(3, 3, tiles)
    near_relays(2)
    next_relays(0)
    for load in loads[3:]:
        load.wait()
    exchange_end(landed.at[0], ex_sems.at[0])
    for unit in range(4):
        spread = jnp.logical_and(row_id - unit * 32 == col_id - 64, row_id // 32 == unit).astype(F32).astype(BF16)
        ranks[:, unit] = dot(full[0].reshape(256, 128), spread).astype(BF16).reshape(GROUP, UNIT, 128)
    for number in range(4):
        for i, slot, half in pieces(number):
            row_ranks[number, i * 32 : (i + 1) * 32, :] = ranks[slot, 2 * half : 2 * half + 2].reshape(32, 128)

    owner = (lax.broadcasted_iota(jnp.int32, (1, 1024), 1) // RANK).astype(F32)
    spread_row = lax.broadcasted_iota(jnp.int32, (128, 1024), 0)
    spread_col = lax.broadcasted_iota(jnp.int32, (128, 1024), 1)
    fold_row = lax.broadcasted_iota(jnp.int32, (1024, 128), 0)
    fold_col = lax.broadcasted_iota(jnp.int32, (1024, 128), 1)

    def widened(values, mine, first):
        spread = (spread_row == 64 + first + spread_col % RANK).astype(F32).astype(BF16)
        return jnp.where(mine, dot(values, spread), 0.0).astype(BF16)

    def turn(head, number):
        swapped = jnp.where(even, pltpu.roll(head, 127, 1), pltpu.roll(head, 1, 1))
        return head * cosine[number] + swapped * sine[number]

    def wide_of(number):
        return rows_in.at[:, pl.ds(pl.multiple_of(number * 1024, 1024), 1024)]

    def late_keys(number, carry):
        own = row_ranks[number]
        wide = widened(own, row_adapter[number] == owner, 0)
        wide_of(number)[...] = wide
        key = acc[number, :, HEAD : HEAD + 128] + dot(wide, right_qkv[:, HEAD : HEAD + 128])
        late[0, number] = jnp.where(lane < ROT, turn(key, number), own.astype(F32)).astype(BF16)
        return carry

    def query_rows(number, carry):
        query = acc[number, :, :HEAD] + dot(wide_of(number)[...], right_qkv[:, :HEAD])
        scale = jnp.asarray(HEAD ** (-0.5), BF16)
        first = turn(query[:, :128], number).astype(BF16) * scale
        second = query[:, 128:].astype(BF16) * scale
        main = jnp.concatenate([jnp.where(lane < ROT, 0.0, first.astype(F32)).astype(BF16), second], axis=1)
        back = lax.dot_general(
            main, right_qkv[:, HEAD : 2 * HEAD], (((1,), (1,)), ((), ())), preferred_element_type=F32
        )
        fold = (fold_col == 64 + fold_row % RANK).astype(F32).astype(BF16)
        low_rank = dot(jnp.where(row_adapter[number] == owner, back, 0.0).astype(BF16), fold)
        queries[number, :, :HEAD] = main
        queries[number, :, HEAD:] = jnp.where(lane < ROT, first.astype(F32), low_rank).astype(BF16)
        return carry

    lax.fori_loop(0, 4, late_keys, 0, unroll=True)
    near_sends(4)
    lax.fori_loop(0, 4, query_rows, 0, unroll=2)

    def finish_hidden(number):
        wide = widened(row_ranks[number], row_adapter[number] == owner, RANK)
        for part in range(hid // 256):
            columns = slice(part * 256, (part + 1) * 256)
            value = acc[number, :, QKV + part * 256 : QKV + (part + 1) * 256]
            value = value + dot(wide, right_up[:, columns]) + in_bias[:, columns]
            value = jax.nn.gelu(value, approximate=True).astype(BF16)
            for i, slot, half in pieces(number):
                inputs[slot, 2 * half : 2 * half + 2, :, HEAD + part * 256 : HEAD + (part + 1) * 256] = value[
                    i * 32 : (i + 1) * 32, :
                ].reshape(2, UNIT, 256)

    def attend_all(slot, own=False):
        def body(pair, carry):
            tail = late[slot].reshape(count, LATE)
            keys = jnp.concatenate([early[slot, :, :, :HEAD].reshape(count, HEAD), tail], axis=1)
            values = jnp.concatenate([early[slot, :, :, HEAD:].reshape(count, HEAD), tail], axis=1)
            key_id = names[...] + ((req - slot) * count).astype(F32)
            blocks = (pair * 2, pair * 2 + 1)
            scores = [
                lax.dot_general(queries[b], keys, (((1,), (1,)), ((), ())), preferred_element_type=F32) for b in blocks
            ]
            results = []
            for b, score in zip(blocks, scores):
                allowed = key_id >= row_start[b]
                if own:
                    allowed = jnp.logical_and(allowed, key_id <= row_index[b])
                score = jnp.where(allowed, score, NEGATIVE_FILL)
                peak = jnp.max(score, axis=1, keepdims=True)
                if not own:
                    peak = jnp.maximum(top[b], peak)
                kept = jnp.exp(score - peak)
                results.append((peak, jnp.sum(kept, axis=1, keepdims=True), dot(kept.astype(BF16), values)))
            for b, (peak, part, product) in zip(blocks, results):
                if not own:
                    decay = jnp.exp(top[b] - peak)
                    part = part + total[b] * decay
                    product = product + summed[b] * decay
                top[b] = peak
                total[b] = part
                summed[b] = product
            return carry

        lax.fori_loop(0, 2, body, 0)

    def attend_on(which, slot):
        @pl.when(core == which)
        def _():
            attend_all(slot)

    depth = HEAD + hid
    width = out.shape[1]
    deep = depth + 128
    stored = []

    def store_weights():
        for n in range(width // 1024):
            for j, (ref, first, size) in enumerate(((w_attn, 0, HEAD), (w_down, HEAD, hid), (w_right, depth, 128))):
                copy = pltpu.make_async_copy(
                    ref.at[:, pl.ds(n * 1024, 1024)], weights.at[pl.ds(n * deep + first, size), pl.ds(0, 1024)],
                    weight_sems.at[n * 3 + j],
                )
                copy.start()
                stored.append(copy)

    def lower(unit, first, begin, end):
        mine = adapter[:, unit].reshape(256, 1) == owner
        product = dot(inputs[:, unit, :, begin:end].reshape(256, end - begin), left[begin:end, :])
        fold = (fold_col == unit * 32 + first + fold_row % RANK).astype(F32).astype(BF16)
        return dot(jnp.where(mine, product, 0.0).astype(BF16), fold)

    near_relays(3)
    next_relays(1)
    near_low(4)
    finish_hidden(0)
    finish_hidden(1)
    near_passing(4)
    next_relays(2)
    attend_all(0, True)
    next_relays(3)
    take_all(5 - 4 * core, 3)
    attend_on(1, 1)
    store_weights()
    near_high(4)
    attend_all(2)
    next_relays(4)
    take_all(1 + 2 * core, 4, 5)
    attend_all(1 + 2 * core)
    attend_all(4)
    finish_hidden(2)
    finish_hidden(3)
    together = lax.fori_loop(0, 4, lambda unit, sum_: sum_ + lower(unit, RANK, HEAD, depth), jnp.zeros((256, 128), F32), unroll=2)
    take_all(3 + 2 * core, 8, 9)
    attend_on(0, 3)
    for number in range(4):
        share = 1.0 / total[number]
        tail = (summed[number, :, HEAD:] * share).astype(BF16)
        wide = widened(tail, row_adapter[number] == owner, 0)
        value = (summed[number, :, :HEAD] * share + dot(wide, right_qkv[:, 2 * HEAD :])).astype(BF16)
        for i, slot, half in pieces(number):
            inputs[slot, 2 * half : 2 * half + 2, :, :HEAD] = value[i * 32 : (i + 1) * 32, :].reshape(2, UNIT, HEAD)
    for unit in range(4):
        together = together + lower(unit, 0, 0, HEAD)
    packed[1] = together.astype(BF16).reshape(GROUP, UNIT, 128)
    exchange_start(plane, packed.at[1], landed.at[1], ex_sems.at[1])
    for copy in started:
        copy.wait_send()
    sent = xs.at[pl.ds(0, GROUP - 1)]
    pltpu.make_async_copy(sent, sent, send_sem).wait()
    for copy in stored:
        copy.wait()

    def back_weights(n, first, size):
        return weights[pl.ds(pl.multiple_of(n // 4 * deep + first, 128), size), pl.ds(pl.multiple_of(n % 4 * 256, 256), 256)]

    def base(n, carry):
        acc[n % 4, :, pl.ds(pl.multiple_of(n // 4 * 256, 256), 256)] = dot(
            chosen_rows[:, :depth], back_weights(n, 0, depth)
        )
        return carry

    for i, (half, d1, d2) in enumerate(REDUCE_GROUPS[0]):
        slot = plane.source(half, d1, d2)
        chosen_rows[i * 32 : (i + 1) * 32, :depth] = inputs[slot, 2 * half : 2 * half + 2, :, :depth].reshape(32, depth)
    tiles = width // 256
    lax.fori_loop(0, tiles // 2, base, 0)
    exchange_middle(plane, landed.at[1], full.at[1], ex_sems.at[1])
    lax.fori_loop(tiles // 2, tiles, base, 0)
    exchange_end(landed.at[1], ex_sems.at[1])
    held = (me * 4 + lane // 32).astype(F32)
    for unit in range(4):
        mine = adapter[:, unit].reshape(256, 1) == held
        spread = (row_id == unit * 32 + col_id % 32).astype(F32).astype(BF16)
        wide = jnp.where(mine, dot(full[1].reshape(256, 128), spread), 0.0).astype(BF16)
        inputs[:, unit, :, depth:] = wide.reshape(GROUP, UNIT, 128)

    def first_group():
        for i, (half, d1, d2) in enumerate(REDUCE_GROUPS[0]):
            slot = plane.source(half, d1, d2)
            chosen_rows[i * 32 : (i + 1) * 32, depth:] = inputs[slot, 2 * half : 2 * half + 2, :, depth:].reshape(32, 128)

        def column(n, carry):
            columns = pl.ds(pl.multiple_of(n * 256, 256), 256)
            result = dot(chosen_rows[:, depth:], back_weights(n, depth, 128))
            result = (result + acc[n % 4, :, pl.ds(pl.multiple_of(n // 4 * 256, 256), 256)]).astype(BF16)
            for i, (half, d1, d2) in enumerate(REDUCE_GROUPS[0]):
                xs[plane.source(half, d1, d2), pl.ds(half * 32, 32), columns] = result[i * 32 : (i + 1) * 32, :]
            return carry

        lax.fori_loop(0, width // 256, column, 0)

    def multiply_back(number):
        for i, (half, d1, d2) in enumerate(REDUCE_GROUPS[number]):
            slot = plane.source(half, d1, d2)
            chosen_rows[i * 32 : (i + 1) * 32, :] = inputs[slot, 2 * half : 2 * half + 2].reshape(32, deep)

        def column(n, carry):
            columns = pl.ds(pl.multiple_of(n * 256, 256), 256)
            result = dot(chosen_rows[...], back_weights(n, 0, deep)).astype(BF16)
            for i, (half, d1, d2) in enumerate(REDUCE_GROUPS[number]):
                xs[plane.source(half, d1, d2), pl.ds(half * 32, 32), columns] = result[i * 32 : (i + 1) * 32, :]
            return carry

        lax.fori_loop(0, width // 256, column, 0)

    def unit_rows(half, u):
        return pl.ds(half * 32 + u * UNIT, UNIT)

    def landing(half, axis, side, d1, place):
        index = half * 2 + side
        if axis == 2:
            return from2.at[index, FAR[d1], place], sems2.at[index, FAR[d1] * 3 + place]
        return from1.at[index, place], sems1.at[index, place]

    def send_back(half, d1, d2, u, axis):
        d = d2 if axis == 2 else d1
        back = d if d != 2 else (1 if u == 0 else -1)
        side = 0 if back == 1 else 1
        place = 2 if d == 2 else u
        slot = plane.source(half, d1, d2)
        to = plane.off(half, 0, -back) if axis == 2 else plane.off(half, -back, 0)
        target, arrived = landing(half, axis, side, d1, place)
        pltpu.make_async_remote_copy(
            xs.at[slot, unit_rows(half, u), :], target, back_sem, arrived, device_id={"mlp": to}, device_id_type=MESH
        ).start()

    def arrive_back(half, axis, side, d1, place):
        ref, arrived = landing(half, axis, side, d1, place)
        pltpu.make_async_copy(ref, ref, arrived).wait()
        return ref

    def add(half, d1, d2, u, children):
        refs = [arrive_back(half, axis, side, d1, place) for axis, side, place in children]
        slot = plane.source(half, d1, d2)
        here = xs.at[slot, unit_rows(half, u), :]
        value = here[...].astype(F32)
        for ref in refs:
            value = value + ref[...].astype(F32)
        here[...] = value.astype(BF16)

    first_group()
    for d1 in (2, 1, -1, 0):
        for half in (0, 1):
            for u in (0, 1):
                send_back(half, d1, 2, u, 2)
    for number in (1, 2):
        multiply_back(number)
        for half, d1, d2 in REDUCE_GROUPS[number]:
            send_back(half, d1, d2, 1 if d2 == 1 else 0, 2)
    for number in (1, 2):
        for half, d1, d2 in REDUCE_GROUPS[number]:
            u = 0 if d2 == 1 else 1
            add(half, d1, d2, u, ((2, 0 if d2 == 1 else 1, 2),))
            send_back(half, d1, d2, u, 2)
    multiply_back(3)
    both = lambda u: ((2, 0, u), (2, 1, u))
    for half in (0, 1):
        for u in (0, 1):
            add(half, 2, 0, u, both(u))
            send_back(half, 2, 0, u, 1)
    for d1 in (1, -1):
        for half in (0, 1):
            u = 1 if d1 == 1 else 0
            add(half, d1, 0, u, both(u))
            send_back(half, d1, 0, u, 1)
    for d1 in (1, -1):
        for half in (0, 1):
            u = 0 if d1 == 1 else 1
            add(half, d1, 0, u, both(u) + ((1, 0 if d1 == 1 else 1, 2),))
            send_back(half, d1, 0, u, 1)
    for half in (0, 1):
        for u in (0, 1):
            refs = [arrive_back(half, axis, side, 0, place) for axis, side, place in both(u) + ((1, 0, u), (1, 1, u))]
            rows = unit_rows(half, u)
            value = xs[me, rows, :].astype(F32)
            for ref in refs:
                value = value + ref[...].astype(F32)
            out[rows, :] = (value + tokens[rows, :].astype(F32) + out_bias[...]).astype(BF16)
    sent = xs.at[pl.ds(0, GROUP - 1)]
    pltpu.make_async_copy(sent, sent, back_sem).wait()


def per_device(
    tokens, layer_norm_gain, layer_norm_bias, query_key_weight, output_weight, up_weight, input_bias, down_weight,
    output_bias, input_adapter_left, query_key_value_right, up_adapter_right, output_adapter_left, down_adapter_left,
    output_adapter_right, lengths, request_adapter, slot_adapter,
):
    rows, width = tokens.shape
    hid = up_weight.shape[1]
    vmem = pl.BlockSpec(memory_space=pltpu.VMEM)
    smem = pl.BlockSpec(memory_space=pltpu.SMEM)
    anywhere = pl.BlockSpec(memory_space=pl.ANY)
    dma = pltpu.SemaphoreType.DMA
    by_unit = (GROUP, 4, UNIT)
    depth = HEAD + hid
    return pl.pallas_call(
        layer_kernel,
        out_shape=jax.ShapeDtypeStruct((rows, width), BF16),
        in_specs=[vmem] * 7 + [smem] + [anywhere] * 10,
        out_specs=vmem,
        scratch_shapes=[
            pltpu.VMEM((GROUP, rows, width), BF16),
            pltpu.VMEM((width, QKV + hid + 128), BF16),
            pltpu.VMEM(query_key_value_right.shape[:1] + (QKV,), BF16),
            pltpu.VMEM(up_adapter_right.shape, BF16),
            pltpu.VMEM((256, width), BF16),
            pltpu.VMEM((4, 256, QKV + hid), F32),
            pltpu.VMEM(by_unit + (128,), BF16),
            pltpu.VMEM((2, GROUP, UNIT, 128), BF16),
            pltpu.VMEM((2, GROUP, UNIT, 128), BF16),
            pltpu.VMEM((2, GROUP, UNIT, 128), BF16),
            pltpu.VMEM(by_unit + (1,), F32),
            pltpu.VMEM(by_unit + (1,), F32),
            pltpu.VMEM((4, 256, 1), F32),
            pltpu.VMEM((4, 256, 1), F32),
            pltpu.VMEM((4, 256, 1), F32),
            pltpu.VMEM((1, 1024), F32),
            pltpu.VMEM((4, 256, 128), F32),
            pltpu.VMEM((4, 256, 128), F32),
            pltpu.VMEM(by_unit + (128,), BF16),
            pltpu.VMEM((4, 256, 128), BF16),
            pltpu.VMEM((4, 256, HEAD + LATE), BF16),
            pltpu.VMEM((6, 4, 256, 2 * HEAD), BF16),
            pltpu.VMEM((6, 4, 256, LATE), BF16),
            pltpu.VMEM((4, 256 - CUT, 2 * HEAD), BF16),
            pltpu.VMEM((4, 256 - CUT, LATE), BF16),
            pltpu.VMEM((4, 256, 1), F32),
            pltpu.VMEM((4, 256, 1), F32),
            pltpu.VMEM((4, 256, HEAD + LATE), F32),
            pltpu.VMEM(by_unit + (depth + 128,), BF16),
            pltpu.VMEM((depth, 1024), BF16),
            pltpu.VMEM((256, depth + 128), BF16),
            pltpu.VMEM((4, 4, 3, UNIT, width), BF16),
            pltpu.VMEM((4, 3, UNIT, width), BF16),
            dma((7,)),
            dma,
            dma((GROUP, 4)),
            dma((2, 4)),
            dma((50,)),
            dma((50,)),
            dma((width // 1024 * 3,)),
            dma,
            dma((4, 12)),
            dma((4, 3)),
        ],
        compiler_params=pltpu.CompilerParams(
            collective_id=0, has_side_effects=True, vmem_limit_bytes=VMEM_LIMIT
        ),
        name="layer_stage",
    )(
        tokens, layer_norm_gain[None, :], layer_norm_bias[None, :], input_bias[None, :],
        output_bias[None, :], lengths, request_adapter, slot_adapter,
        query_key_weight.reshape(width, QKV), up_weight, input_adapter_left,
        query_key_value_right.reshape(-1, QKV), up_adapter_right,
        output_adapter_left.reshape(HEAD, -1), down_adapter_left, output_weight.reshape(HEAD, width), down_weight,
        output_adapter_right,
    )


def solution(mesh):
    in_specs = (
        P(("req", "mlp"), None), P(), P(), P(None, "mlp", None), P("mlp", None, None), P(None, "mlp"), P("mlp"),
        P("mlp", None), P(), P(None, "mlp"), P(None, "mlp", None), P(None, "mlp"), P("mlp", None, None),
        P("mlp", None), P("mlp", None), P(), P(), P("mlp"),
    )
    return jax.shard_map(
        per_device, mesh=mesh, in_specs=in_specs, out_specs=P(("req", "mlp"), None), check_vma=False
    )
```
